32 devices in a mesh: region: 4 (over y, x), block: 8 (over z, core).
Axes of the slice: x: 2, y: 2, z: 4, core: 2. Of those that a mesh axis runs over, the one named last changes fastest.
Arguments:
- obs: bfloat16 [512, 32, 128], P(('region', 'block')), may hold values from -6 to 6
- predict: bfloat16 [512, 2, 128, 128], P(('region', 'block')), may hold values from -0.375 to 0.375
- factor: bfloat16 [512, 128, 128], P(('region', 'block')), as said below
- tau: float32 [32], replicated, may hold values from 0.5 to 2
- nbr_dev: int32 [512, 1], P(('region', 'block')), may hold values from 0 to 7; in each aligned block of 16 rows (0 to 15, 16 to 31, ...) at most 4 rows name the same one
- nbr_slot: int32 [512, 2], P(('region', 'block')), may hold values from 0 to 15
- counts: int32 [32], P(('region', 'block')), may hold values from 8 to 16
Outputs:
- grad_obs: float32 [512, 32, 128], P(('region', 'block'))
- grad_tau: float32 [32], replicated
The draws below stay inside these ranges and needn't reach their ends.
Inputs may be any that keep to these rules, and one draw needn't show every extreme that they name: `nbr_dev`: among the blocks of one device at most 4 name the same device. `nbr_slot`: column 0 is a slot on the in-region neighbour's device, column 1 a slot on the device of the previous region with the same index along block. `factor`: each block's matrix is the identity plus small entries.
All inputs are finite; a program needn't handle non-finite values.
Results may differ from the reference program's by a relative error of at most 0.0035.
Values may be sent and summed in bfloat16 or wider, within the bound.
A program may use at most 64 MiB of HBM per device.

```python
import math
import jax
import jax.numpy as jnp
import numpy as np
from jax import lax

C = 32
BS = 128
NBD = 16
CAP = 4
NB = 512
N_REGION = 4
N_BLOCK = 8


def draw_factor(key, part):
    first_key = jax.random.fold_in(key, 0)
    off = jax.random.normal(first_key, (NB, BS, BS), jnp.float32)
    scaled = off * (0.5 / BS ** 0.5)
    return (scaled + jnp.eye(BS, dtype=jnp.float32)[None]).astype(jnp.bfloat16)


def touch_ends(values, stream_key, low, largest):
    longest = values.shape.index(max(values.shape))
    spots = []
    for shift in (0, 1):
        where = [jax.random.randint(jax.random.fold_in(stream_key, axis), (), 0, length) for axis, length in enumerate(values.shape)]
        where[longest] = (where[longest] + shift) % values.shape[longest]
        spots.append(tuple(where))
    return values.at[spots[0]].set(low).at[spots[1]].set(largest)


def levels(rng, dims, shards, smallest, top_value):
    def one(dim, blocks):
        steps = jax.random.uniform(jax.random.fold_in(jax.random.fold_in(rng, 6), dim), (blocks,), jnp.float32, smallest / len(shards), top_value / len(shards))
        return jnp.repeat(jnp.exp(steps), dims[dim] // blocks).reshape((-1,) + (1,) * (len(dims) - dim - 1))

    level = one(*shards[0])
    for cut in shards[1:]:
        level = level * one(*cut)
    return level


def shared_out(key, own, number, rows, amount, top, most, lean):
    sequence = jax.random.permutation(key, amount)
    packed, common = portions_of(amount, rows * top, most, lean, True), portions_of(amount, rows * top, most, lean, False)
    places = jnp.arange(amount)

    def named(sizes, turn):
        used = int((sizes > 0).sum())
        fixed = max(1, used // 4)
        moved = fixed + (places - fixed + turn * (used - fixed)) % max(1, amount - fixed)
        return jnp.zeros((amount,), jnp.int32).at[sequence[jnp.where(places < fixed, places, moved)]].set(jnp.asarray(sizes, jnp.int32))

    sizes = jnp.where(number % 4 == 0, named(packed, number // 4), named(common, number - number // 4 - 1))
    mixed = jax.random.permutation(jax.random.fold_in(own, 3), amount)
    donor, sink = mixed[0:amount // 2 * 2:2], mixed[1:amount // 2 * 2:2]
    margin = jnp.minimum(sizes[donor] - 1, most - sizes[sink]) // 2
    margin = jnp.where((donor == sequence[0]) | (sink == sequence[0]) | (sizes[sink] == 0), 0, jnp.maximum(margin, 0))
    moved = jax.random.randint(jax.random.fold_in(own, 4), (amount // 2,), 0, 1 << 20) % (margin + 1)
    sizes = sizes.at[donor].add(-moved).at[sink].add(moved)
    items = jnp.searchsorted(jnp.cumsum(sizes), jnp.arange(rows * top), side="right").astype(jnp.int32)
    listing = items.reshape(top, rows).T
    listing = listing[jax.random.permutation(jax.random.fold_in(own, 1), rows)]
    turn = jax.random.randint(jax.random.fold_in(own, 2), (rows, 1), 0, top)
    return jnp.take_along_axis(listing, (jnp.arange(top)[None, :] + turn) % top, axis=1)


def portions_of(count, total, reach, slope, full):
    loads = [(1 << 20) // math.isqrt(grade ** slope) + 1 for grade in range(1, count + 1)]
    largest = reach if full else min(reach, max(-(-total // count), total * loads[0] // sum(loads)))
    least = 1 if total - largest >= count - 1 else 0
    holding, spare = [largest] + [least] * (count - 1), total - largest - least * (count - 1)
    while spare > 0:
        free = [i for i in range(1, count) if holding[i] < largest] or [i for i in range(1, count) if holding[i] < reach]
        whole, left = sum([loads[i] for i in free]), spare
        for i in free:
            addition = min(reach - holding[i], max(1, left * loads[i] // whole), spare)
            holding[i] = holding[i] + addition
            spare = spare - addition
    return np.array(holding)


def noise(rng, extent, width, reach, shards=(), kind=jnp.bfloat16):
    drawn = jax.random.normal(rng, extent, jnp.float32) * width
    if len(shards) > 0:
        drawn = levels(rng, extent, shards, -0.22, 0.18) * drawn
    return jnp.clip(drawn, min=-reach, max=reach).astype(kind)


def setup_inputs(seed: int = 0) -> dict:
    seeds = jax.random.split(jax.random.key(seed), 8)
    obs = noise(seeds[0], (NB, C, BS), 1.0, 6.0, ((0, 32),))
    predict = noise(seeds[1], (NB, 2, BS, BS), (2 * BS) ** -0.5, 0.375, ((0, 32),))
    factor = draw_factor(jax.random.fold_in(seeds[7], 71), 0)
    tau = jnp.clip(jnp.exp(jax.random.uniform(seeds[3], (C,), jnp.float32, math.log(0.5), math.log(2.0))), 0.5, 2.0)
    nbr_dev_keys = jax.random.split(jax.random.fold_in(seeds[4], 1), NB // NBD)
    nbr_dev_turns = jax.random.permutation(jax.random.fold_in(seeds[4], 3), NB // NBD)
    nbr_dev = jax.vmap(lambda own, number: shared_out(jax.random.fold_in(seeds[4], 2), own, number, NBD, N_BLOCK, 1, CAP, 1))(nbr_dev_keys, nbr_dev_turns).reshape((NB, 1))
    nbr_slot = touch_ends(jax.random.randint(seeds[5], (NB, 2), 0, NBD), jax.random.fold_in(seeds[5], 1), 0, NBD - 1).astype(jnp.int32)
    counts = touch_ends(jax.random.randint(seeds[6], (N_REGION * N_BLOCK,), NBD // 2, NBD + 1), jax.random.fold_in(seeds[6], 1), NBD // 2, NBD).astype(jnp.int32)
    return {"obs": obs, "predict": predict, "factor": factor, "tau": tau, "nbr_dev": nbr_dev, "nbr_slot": nbr_slot, "counts": counts}


def reference(obs, predict, factor, tau, nbr_dev, nbr_slot, counts):
    nb = obs.shape[0]
    groups = nb // NBD
    index = jnp.arange(nb, dtype=jnp.int32)
    dev_of = index // NBD
    region = dev_of // N_BLOCK
    inner = dev_of % N_BLOCK
    slot = index % NBD
    first = (region * N_BLOCK + nbr_dev[:, 0]) * NBD + nbr_slot[:, 0]
    seam = region > 0
    second = jnp.where(seam, ((region - 1) * N_BLOCK + inner) * NBD + nbr_slot[:, 1], 0).astype(jnp.int32)
    live = (slot < counts[dev_of]).astype(jnp.float32)
    seam_f = seam.astype(jnp.float32)
    near = jnp.take(obs, first, axis=0)
    far = jnp.take(obs, second, axis=0)

    def shape_g(a):
        return a.reshape((groups, NBD) + a.shape[1:])

    def per_device(items):
        own, pred, fac, y_one, y_two, seam_g, live_g = items
        p_zero = pred[:, 0].astype(jnp.float32)
        p_one = pred[:, 1].astype(jnp.float32)
        err = own.astype(jnp.float32) - jnp.einsum('bcj,bjk->bck', y_one.astype(jnp.float32), p_zero)
        err = err - seam_g[:, None, None] * jnp.einsum('bcj,bjk->bck', y_two.astype(jnp.float32), p_one)
        err = err.astype(jnp.bfloat16)
        facf = fac.astype(jnp.float32)
        white = jnp.einsum('bcj,bjk->bck', err.astype(jnp.float32), facf)
        weighted = (live_g[:, None, None] * tau[None, :, None] * white).astype(jnp.bfloat16)
        adj = jnp.einsum('bck,bjk->bcj', weighted.astype(jnp.float32), facf)
        adj16 = adj.astype(jnp.bfloat16).astype(jnp.float32)
        back_one = -jnp.einsum('bck,bjk->bcj', adj16, p_zero)
        back_two = -seam_g[:, None, None] * jnp.einsum('bck,bjk->bcj', adj16, p_one)
        squares = jnp.sum(live_g[:, None, None] * white * white, axis=(0, 2))
        return adj, back_one, back_two, squares

    adj, back_one, back_two, squares = lax.map(per_device, (shape_g(obs), shape_g(predict), shape_g(factor), shape_g(near), shape_g(far), shape_g(seam_f), shape_g(live)))
    grad = adj.reshape(obs.shape)
    grad = grad.at[first].add(back_one.reshape(obs.shape))
    grad = grad.at[second].add(back_two.reshape(obs.shape))
    total_sq = jnp.sum(squares, axis=0)
    total_live = jnp.sum(live)
    grad_tau = (0.5 * total_sq - 0.5 * BS * total_live / tau) / (nb * BS)
    return grad, grad_tau
```

```python
import functools

import jax
import jax.numpy as jnp
from jax import lax
from jax.experimental import pallas as pl
from jax.experimental.pallas import tpu as pltpu
from jax.sharding import PartitionSpec as P

MESH = pl.DeviceIdType.MESH
LANES = 128


def kernel(
    nblock,
    nregion,
    cap,
    dev_hbm,
    slot_hbm,
    counts_hbm,
    tau_hbm,
    obs_hbm,
    predict_hbm,
    factor_hbm,
    out_ref,
    gtau_ref,
    dev_ref,
    slot_ref,
    counts_ref,
    tau_ref,
    obs,
    predict,
    factor,
    req_send,
    req_recv,
    near_send,
    near_recv,
    ret_send,
    ret_recv,
    seam_obs,
    seam_tgt,
    seam_tgt_in,
    seam_ret,
    seam_ret_in,
    held,
    held_ref,
    spread,
    partial,
    back,
    adjoint,
    sq_send,
    sq_recv,
    rg_send,
    rg_recv,
    local_sem,
    req_ss,
    req_rs,
    near_ss,
    near_rs,
    ret_ss,
    ret_rs,
    sq_ss,
    sq_rs,
    rg_ss,
    rg_rs,
    seam_ss,
    seam_rs,
):
    nbd, chans, width = obs.shape
    rows = nbd * chans
    part = cap * chans
    lanes = req_send.shape[2]
    group = 2 if nblock % 2 == 0 and part % LANES == 0 else 1
    me = lax.axis_index("block")
    region = lax.axis_index("region")
    bf16, f32, i32 = jnp.bfloat16, jnp.float32, jnp.int32

    half = me // (nblock // 2)

    def farthest(turn):
        below = nblock - 1 - turn - (me + turn + 1) // nblock
        above = turn + (turn - me + nblock) // nblock
        return below + half * (above - below)

    def each_peer(body, nearest=False):
        def visit(turn):
            body(farthest(nblock - 2 - turn if nearest else turn))

        if nblock <= 8:
            for turn in range(nblock - 1):
                visit(turn)
        else:

            def run(turn, carry):
                visit(turn)
                return carry

            lax.fori_loop(0, nblock - 1, run, 0)

    def each_region(body):
        for step in range(1, nregion):
            body(lax.rem(region + step, nregion))

    def to_block(src, dst, ss, rs, peer):
        return pltpu.make_async_remote_copy(
            src_ref=src,
            dst_ref=dst,
            send_sem=ss,
            recv_sem=rs,
            device_id={"block": peer},
            device_id_type=MESH,
        )

    def to_region(src, dst, ss, rs, peer):
        return pltpu.make_async_remote_copy(
            src_ref=src,
            dst_ref=dst,
            send_sem=ss,
            recv_sem=rs,
            device_id={"region": peer},
            device_id_type=MESH,
        )

    small = [
        pltpu.make_async_copy(src, dst, local_sem.at[3 + i])
        for i, (src, dst) in enumerate(
            [(dev_hbm, dev_ref), (slot_hbm, slot_ref), (counts_hbm, counts_ref), (tau_hbm, tau_ref)]
        )
    ]
    for copy in small:
        copy.start()

    barrier = pltpu.get_barrier_semaphore()
    each_peer(
        lambda peer: pl.semaphore_signal(
            barrier, inc=1, device_id={"block": peer}, device_id_type=MESH
        )
    )
    each_region(
        lambda peer: pl.semaphore_signal(
            barrier, inc=1, device_id={"region": peer}, device_id_type=MESH
        )
    )
    load_obs = pltpu.make_async_copy(obs_hbm, obs, local_sem.at[0])
    load_predict = pltpu.make_async_copy(predict_hbm, predict, local_sem.at[1])
    load_factor = pltpu.make_async_copy(factor_hbm, factor, local_sem.at[2])
    load_obs.start()
    load_predict.start()
    load_factor.start()

    for copy in small:
        copy.wait()

    dest = [dev_ref[0, h] for h in range(nbd)]
    flat = []
    for h in range(nbd):
        rank = jnp.int32(0)
        for g in range(h):
            rank = rank + (dest[g] == dest[h]).astype(i32)
        flat.append(dest[h] * cap + rank)

    lane = lax.broadcasted_iota(i32, (nblock, lanes), 1)
    spot = lax.broadcasted_iota(i32, (nblock, lanes), 0) * cap + lane // chans
    spot = jnp.where(lane < part, spot, -1)
    wanted = jnp.full((nblock, lanes), -1, i32)
    for h in range(nbd):
        wanted = jnp.where(spot == flat[h], slot_ref[0, h] * chans + lane % chans, wanted)
    for d in range(nblock):
        req_send[d] = wanted[d : d + 1]

    block_lane = lax.broadcasted_iota(i32, (1, rows), 1)
    owner_of = block_lane // chans
    seam_row = jnp.zeros((1, rows), i32)
    for h in range(nbd):
        seam_row = jnp.where(owner_of == h, slot_ref[1, h], seam_row)
    seam_tgt[...] = seam_row * chans + block_lane % chans

    place_lane = lax.broadcasted_iota(i32, (1, LANES), 1)
    holder = jnp.full((1, LANES), nbd, i32)
    for h in range(nbd):
        holder = jnp.where(place_lane == flat[h], h, holder)
    held[...] = holder
    load_held = pltpu.make_async_copy(held, held_ref, local_sem.at[7])
    load_held.start()
    back[nbd] = jnp.zeros((chans, width), bf16)

    pl.semaphore_wait(barrier, nblock - 1 + nregion - 1)

    def request(peer, mine):
        return to_block(req_send.at[peer], req_recv.at[mine], req_ss.at[peer], req_rs.at[mine], peer)

    each_peer(lambda peer: request(peer, me).start())
    req_recv[me] = req_send[me]

    down = lax.rem(region + 1, nregion)
    up = lax.rem(region + nregion - 1, nregion)
    seam_fwd = to_region(obs_hbm, seam_obs, seam_ss.at[0], seam_rs.at[0], down)
    seam_where = to_region(seam_tgt, seam_tgt_in, seam_ss.at[1], seam_rs.at[1], up)
    seam_bwd = to_region(seam_ret, seam_ret_in, seam_ss.at[2], seam_rs.at[2], up)
    has_prev = region > 0
    has_next = region < nregion - 1

    @pl.when(has_next)
    def _():
        seam_fwd.start()

    @pl.when(has_prev)
    def _():
        seam_where.start()

    load_obs.wait()
    pick_lane = lax.broadcasted_iota(i32, (part, rows), 1)

    def picked(peer):
        row = jnp.broadcast_to(req_recv[peer], (LANES, lanes))
        column = jnp.transpose(row)[:part]
        column = jnp.concatenate([column] * (rows // LANES), axis=1)
        mask = jnp.where(column == pick_lane, 1.0, 0.0).astype(bf16)
        got = jnp.dot(mask, obs[...].reshape(rows, width), preferred_element_type=f32)
        return got.astype(bf16).reshape(cap, chans, width)

    def span(d):
        return pl.ds(d * cap, cap)

    def serve(peer, mine):
        return to_block(
            near_send.at[span(peer)],
            near_recv.at[span(mine)],
            near_ss.at[peer],
            near_rs.at[mine],
            peer,
        )

    def put(peer):
        near_send[span(peer)] = picked(peer)
        serve(peer, me).start()

    def answer(peer):
        request(me, peer).wait_recv()
        put(peer)

    each_peer(answer, nearest=True)
    near_recv[span(me)] = picked(me)

    def build(pair):
        wanted_row = jnp.concatenate(
            [req_recv[pair * group + i][:, :part] for i in range(group)], axis=1
        )
        spread[pair] = jnp.where(
            wanted_row == lax.broadcasted_iota(i32, (rows, group * part), 0), 1.0, 0.0
        ).astype(bf16)

    for pair in range(nblock // group):
        build(pair)
    load_held.wait()

    @pl.when(has_prev)
    def _():
        seam_fwd.wait_recv()

    @pl.when(jnp.logical_not(has_prev))
    def _():
        seam_obs[...] = jnp.zeros_like(seam_obs)

    load_predict.wait()
    for g in range(nbd):
        partial[g] = obs[g].astype(f32) - jnp.dot(
            seam_obs[slot_ref[1, g]], predict[g, 1], preferred_element_type=f32
        )
    load_factor.wait()

    eye = lax.broadcasted_iota(i32, (chans, LANES), 0) == lax.broadcasted_iota(
        i32, (chans, LANES), 1
    )
    tau_row = jnp.concatenate([tau_ref[...], jnp.zeros((1, LANES - chans), f32)], axis=1)
    tau_col = jnp.sum(jnp.where(eye, tau_row, 0.0), axis=1, keepdims=True)
    count = counts_ref[0]

    each_peer(lambda peer: serve(me, peer).wait_recv(), nearest=True)

    nt = (((1,), (1,)), ((), ()))
    every = range(nbd)
    err = [
        (
            partial[g]
            - jnp.dot(near_recv[flat[g]], predict[g, 0], preferred_element_type=f32)
        ).astype(bf16)
        for g in every
    ]
    white = [jnp.dot(err[g], factor[g], preferred_element_type=f32) for g in every]
    live = [(g < count).astype(f32) for g in every]
    weighted = [(live[g] * tau_col * white[g]).astype(bf16) for g in every]
    squares = live[0] * white[0] * white[0]
    for g in range(1, nbd):
        squares = squares + live[g] * white[g] * white[g]
    live_lane = lax.broadcasted_iota(i32, (1, LANES), 1) == chans
    sums = jnp.sum(
        jnp.where(eye, jnp.sum(squares, axis=1, keepdims=True), 0.0), axis=0, keepdims=True
    )
    sums = sums + jnp.where(live_lane, jnp.minimum(count, nbd).astype(f32), 0.0)
    sq_send[...] = sums

    def share(peer, mine):
        return to_block(sq_send, sq_recv.at[mine], sq_ss.at[peer], sq_rs.at[mine], peer)

    each_peer(lambda peer: share(peer, me).start())
    sq_recv[me] = sums

    adj = [lax.dot_general(weighted[g], factor[g], nt, preferred_element_type=f32) for g in every]
    for g in every:
        out_ref[g] = adj[g]
        adjoint[g] = adj[g].astype(bf16)

    for g in every:
        back[g] = lax.dot_general(
            adjoint[g], predict[g, 0], nt, preferred_element_type=f32
        ).astype(bf16)

    def pack(dst, peer):
        for k in range(cap):
            dst[k * chans : (k + 1) * chans] = back[held_ref[0, peer * cap + k]]

    def give(peer, mine):
        return to_block(ret_send.at[peer], ret_recv.at[mine], ret_ss.at[peer], ret_rs.at[mine], peer)

    def give_back(peer):
        pack(ret_send.at[peer], peer)
        give(peer, me).start()

    each_peer(give_back)
    pack(ret_recv.at[me], me)

    @pl.when(has_prev)
    def _():
        for g in range(nbd):
            seam_ret[g] = lax.dot_general(
                adjoint[g], predict[g, 1], nt, preferred_element_type=f32
            ).astype(bf16)
        seam_bwd.start()

    each_peer(lambda peer: share(me, peer).wait_recv(), nearest=True)
    line = sq_recv[0]
    for d in range(1, nblock):
        line = line + sq_recv[d]
    rg_send[...] = line

    def share_region(peer, mine):
        return to_region(rg_send, rg_recv.at[mine], rg_ss.at[peer], rg_rs.at[mine], peer)

    each_region(lambda peer: share_region(peer, region).start())
    rg_recv[region] = line

    @pl.when(has_next)
    def _():
        seam_where_in = to_region(seam_tgt, seam_tgt_in, seam_ss.at[1], seam_rs.at[1], up)
        seam_where_in.wait_recv()
        mask = jnp.where(
            seam_tgt_in[...] == lax.broadcasted_iota(i32, (rows, rows), 0), 1.0, 0.0
        ).astype(bf16)
        seam_bwd.wait_recv()
        got = jnp.dot(mask, seam_ret_in[...].reshape(rows, width), preferred_element_type=f32)
        out_ref[...] = out_ref[...] - got.reshape(nbd, chans, width)

    def add(pair):
        blocks_back = ret_recv[pl.ds(pair * group, group)].reshape(group * part, width)
        got = jnp.dot(spread[pair], blocks_back, preferred_element_type=f32)
        out_ref[...] = out_ref[...] - got.reshape(nbd, chans, width)

    each_peer(lambda peer: give(me, peer).wait_recv(), nearest=True)
    for pair in range(nblock // group):
        add(pair)

    each_region(lambda peer: share_region(region, peer).wait_recv())
    total = rg_recv[0]
    for r in range(1, nregion):
        total = total + rg_recv[r]
    total_live = jnp.sum(jnp.where(live_lane, total, 0.0), axis=1, keepdims=True)
    blocks = nbd * nblock * nregion
    gtau_ref[...] = (
        0.5 * total[:, :chans] - 0.5 * width * total_live / tau_ref[...]
    ) / (blocks * width)

    def sent(peer):
        request(peer, me).wait_send()
        serve(peer, me).wait_send()
        give(peer, me).wait_send()
        share(peer, me).wait_send()

    each_peer(sent)
    each_region(lambda peer: share_region(peer, region).wait_send())

    @pl.when(has_next)
    def _():
        seam_fwd.wait_send()

    @pl.when(has_prev)
    def _():
        seam_where.wait_send()
        seam_bwd.wait_send()


def line_kernel(
    nblock,
    nregion,
    cap,
    dev_hbm,
    slot_hbm,
    counts_hbm,
    tau_hbm,
    obs_hbm,
    predict_hbm,
    factor_hbm,
    out_ref,
    gtau_ref,
    dev_ref,
    slot_ref,
    counts_ref,
    tau_ref,
    obs,
    predict,
    factor,
    req_send,
    req_recv,
    near_send,
    near_recv,
    raw_sib,
    raw_far,
    raw_relay,
    ret_send,
    ret_recv,
    seam_obs,
    seam_tgt,
    seam_tgt_in,
    seam_ret,
    seam_ret_in,
    held,
    held_ref,
    spread,
    partial,
    adj_slot,
    seam_slot,
    sq_send,
    sq_recv,
    local_sem,
    req_ss,
    req_rs,
    near_ss,
    near_rs,
    ret_ss,
    ret_rs,
    sq_ss,
    sq_rs,
    seam_ss,
    seam_rs,
    raw_ss,
    raw_rs,
):
    nbd, chans, width = obs.shape
    rows = nbd * chans
    part = cap * chans
    me = lax.axis_index("block")
    region = lax.axis_index("region")
    bf16, f32, i32 = jnp.bfloat16, jnp.float32, jnp.int32
    nt = (((1,), (1,)), ((), ()))

    def flip(d, bit):
        return d + bit - 2 * bit * lax.rem(d // bit, 2)

    sib = flip(me, 1)
    chip = me // 2
    own = [me, sib]
    beside = [flip(d, 2) for d in own]
    skip = [flip(d, 4) for d in own]
    mirror = [flip(d, 4) for d in beside]
    at_end = chip * (nblock // 2 - 1 - chip) == 0
    inner = jnp.logical_not(at_end)
    others = mirror + skip + beside + [sib]

    def to_block(src, dst, ss, rs, peer):
        return pltpu.make_async_remote_copy(
            src_ref=src,
            dst_ref=dst,
            send_sem=ss,
            recv_sem=rs,
            device_id={"block": peer},
            device_id_type=MESH,
        )

    def to_region(src, dst, ss, rs, peer):
        return pltpu.make_async_remote_copy(
            src_ref=src,
            dst_ref=dst,
            send_sem=ss,
            recv_sem=rs,
            device_id={"region": peer},
            device_id_type=MESH,
        )

    regions = [lax.rem(region + step, nregion) for step in range(1, nregion)]

    small = [
        pltpu.make_async_copy(src, dst, local_sem.at[3 + i])
        for i, (src, dst) in enumerate(
            [(dev_hbm, dev_ref), (slot_hbm, slot_ref), (counts_hbm, counts_ref), (tau_hbm, tau_ref)]
        )
    ]
    for copy in small:
        copy.start()

    barrier = pltpu.get_barrier_semaphore()
    for peer in others:
        pl.semaphore_signal(barrier, inc=1, device_id={"block": peer}, device_id_type=MESH)
    for peer in regions:
        pl.semaphore_signal(barrier, inc=1, device_id={"region": peer}, device_id_type=MESH)
    load_obs = pltpu.make_async_copy(obs_hbm, obs, local_sem.at[0])
    load_predict = pltpu.make_async_copy(predict_hbm, predict, local_sem.at[1])
    load_factor = pltpu.make_async_copy(factor_hbm, factor, local_sem.at[2])
    load_obs.start()
    load_predict.start()
    load_factor.start()

    for copy in small:
        copy.wait()

    dest = [dev_ref[0, h] for h in range(nbd)]
    flat = []
    for h in range(nbd):
        rank = jnp.int32(0)
        for g in range(h):
            rank = rank + (dest[g] == dest[h]).astype(i32)
        flat.append(dest[h] * cap + rank)

    lane = lax.broadcasted_iota(i32, (nblock, part), 1)
    spot = lax.broadcasted_iota(i32, (nblock, part), 0) * cap + lane // chans
    wanted = jnp.full((nblock, part), -1, i32)
    for h in range(nbd):
        wanted = jnp.where(spot == flat[h], slot_ref[0, h] * chans + lane % chans, wanted)
    for d in range(nblock):
        req_send[d] = wanted[d : d + 1]

    block_lane = lax.broadcasted_iota(i32, (1, rows), 1)
    owner_of = block_lane // chans
    seam_row = jnp.zeros((1, rows), i32)
    for h in range(nbd):
        seam_row = jnp.where(owner_of == h, slot_ref[1, h], seam_row)
    seam_tgt[...] = seam_row * chans + block_lane % chans

    place_lane = lax.broadcasted_iota(i32, (1, LANES), 1)
    holder = jnp.full((1, LANES), nbd, i32)
    for h in range(nbd):
        holder = jnp.where(place_lane == flat[h], h, holder)
    held[...] = holder
    load_held = pltpu.make_async_copy(held, held_ref, local_sem.at[7])
    load_held.start()

    pl.semaphore_wait(barrier, nblock - 1 + nregion - 1)

    def request(peer, mine):
        return to_block(req_send.at[peer], req_recv.at[mine], req_ss.at[peer], req_rs.at[mine], peer)

    for peer in others:
        request(peer, me).start()
    req_recv[me] = req_send[me]

    to_sib = to_block(obs_hbm, raw_sib, raw_ss.at[0], raw_rs.at[0], sib)
    to_far = to_block(obs_hbm, raw_far, raw_ss.at[1], raw_rs.at[1], mirror[0])
    relay = to_block(raw_far, raw_relay, raw_ss.at[2], raw_rs.at[2], sib)

    down = lax.rem(region + 1, nregion)
    up = lax.rem(region + nregion - 1, nregion)
    seam_fwd = to_region(obs_hbm, seam_obs, seam_ss.at[0], seam_rs.at[0], down)
    seam_where = to_region(seam_tgt, seam_tgt_in, seam_ss.at[1], seam_rs.at[1], up)
    seam_bwd = to_region(seam_ret, seam_ret_in, seam_ss.at[2], seam_rs.at[2], up)
    has_prev = region > 0
    has_next = region < nregion - 1

    @pl.when(at_end)
    def _():
        to_far.start()

    @pl.when(has_next)
    def _():
        seam_fwd.start()

    @pl.when(has_prev)
    def _():
        seam_where.start()

    to_sib.start()

    @pl.when(inner)
    def _():
        raw_far[...] = jnp.zeros_like(raw_far)
        raw_relay[...] = jnp.zeros_like(raw_relay)

    load_obs.wait()
    pick_lane = lax.broadcasted_iota(i32, (part, rows), 1)

    def picked(peer):
        row = jnp.broadcast_to(req_recv[peer], (LANES, part))
        column = jnp.concatenate([jnp.transpose(row)] * (rows // LANES), axis=1)
        mask = jnp.where(column == pick_lane, 1.0, 0.0).astype(bf16)
        got = jnp.dot(mask, obs[...].reshape(rows, width), preferred_element_type=f32)
        return got.astype(bf16).reshape(cap, chans, width)

    def span(d):
        return pl.ds(d * cap, cap)

    def serve(peer, mine):
        return to_block(
            near_send.at[span(peer)],
            near_recv.at[span(mine)],
            near_ss.at[peer],
            near_rs.at[mine],
            peer,
        )

    def put(peer):
        near_send[span(peer)] = picked(peer)
        serve(peer, me).start()

    for peer in mirror:
        request(me, peer).wait_recv()

    @pl.when(inner)
    def _():
        for peer in mirror:
            put(peer)

    @pl.when(at_end)
    def _():
        for peer in mirror:
            near_recv[span(peer)] = jnp.zeros((cap, chans, width), bf16)

    for peer in skip + beside:
        request(me, peer).wait_recv()
        put(peer)
    request(me, sib).wait_recv()

    def build(pair):
        wanted_row = jnp.concatenate([req_recv[pair * 2 + i] for i in range(2)], axis=1)
        spread[pair] = jnp.where(
            wanted_row == lax.broadcasted_iota(i32, (rows, 2 * part), 0), 1.0, 0.0
        ).astype(bf16)

    for pair in range(nblock // 2):
        build(pair)
    load_held.wait()

    eye = lax.broadcasted_iota(i32, (chans, LANES), 0) == lax.broadcasted_iota(
        i32, (chans, LANES), 1
    )
    tau_row = jnp.concatenate([tau_ref[...], jnp.zeros((1, LANES - chans), f32)], axis=1)
    tau_col = jnp.sum(jnp.where(eye, tau_row, 0.0), axis=1, keepdims=True)
    count = counts_ref[0]

    @pl.when(has_prev)
    def _():
        seam_fwd.wait_recv()

    @pl.when(jnp.logical_not(has_prev))
    def _():
        seam_obs[...] = jnp.zeros_like(seam_obs)

    @pl.when(at_end)
    def _():
        to_far.wait_recv()
        relay.start()

    load_predict.wait()
    for g in range(nbd):
        partial[g] = obs[g].astype(f32) - jnp.dot(
            seam_obs[slot_ref[1, g]], predict[g, 1], preferred_element_type=f32
        )
    load_factor.wait()

    def give(peer, mine):
        return to_block(ret_send.at[peer], ret_recv.at[mine], ret_ss.at[peer], ret_rs.at[mine], peer)

    squares = [jnp.zeros((chans, width), f32)]

    def process(peers, near_of, between=None):
        at = [peer * cap + k for peer in peers for k in range(cap)]
        every = range(len(at))
        who = [held_ref[0, i] for i in at]
        block = [jnp.minimum(w, nbd - 1) for w in who]
        live = [(w < count).astype(f32) for w in who]
        near = [near_of(i // cap, at[i], block[i]) for i in every]
        err = [
            (
                partial[block[i]]
                - jnp.dot(near[i], predict[block[i], 0], preferred_element_type=f32)
            ).astype(bf16)
            for i in every
        ]
        white = [jnp.dot(err[i], factor[block[i]], preferred_element_type=f32) for i in every]
        for i in every:
            squares[0] = squares[0] + live[i] * white[i] * white[i]
        if between is not None:
            between()
        weighted = [(live[i] * tau_col * white[i]).astype(bf16) for i in every]
        adj = [
            lax.dot_general(weighted[i], factor[block[i]], nt, preferred_element_type=f32)
            for i in every
        ]
        for i in every:
            adj_slot[at[i]] = adj[i]
        both = [
            lax.dot_general(
                adj[i].astype(bf16),
                predict[block[i]].reshape(2 * width, width),
                nt,
                preferred_element_type=f32,
            ).astype(bf16)
            for i in every
        ]
        for i in every:
            seam_slot[at[i]] = both[i][:, width:]
        return [both[i][:, :width] for i in every]

    def give_back(peers, back):
        for j, peer in enumerate(peers):
            for k in range(cap):
                ret_send[peer, k * chans : (k + 1) * chans] = back[j * cap + k]
            give(peer, me).start()

    @pl.when(at_end)
    def _():
        relay.wait_recv()

    @pl.when(inner)
    def _():
        for peer in mirror:
            serve(me, peer).wait_recv()

    raws = [raw_far, raw_relay]
    give_back(
        mirror,
        process(
            mirror,
            lambda j, i, h: jnp.where(at_end, raws[j][slot_ref[0, h]], near_recv[i]),
        ),
    )

    for peer in beside:
        serve(me, peer).wait_recv()
    give_back(beside, process(beside, lambda j, i, h: near_recv[i]))

    to_sib.wait_recv()
    homes = [obs, raw_sib]
    back = process(own, lambda j, i, h: homes[j][slot_ref[0, h]])
    for k in range(cap):
        ret_recv[me, k * chans : (k + 1) * chans] = back[k]
    give_back([sib], back[cap:])

    live_lane = lax.broadcasted_iota(i32, (1, LANES), 1) == chans

    everyone = [(r, b) for r in regions for b in others + [me]] + [(region, b) for b in others]
    mine = region * nblock + me

    def share(r, b):
        return pltpu.make_async_remote_copy(
            src_ref=sq_send,
            dst_ref=sq_recv.at[mine],
            send_sem=sq_ss.at[0],
            recv_sem=sq_rs.at[0],
            device_id={"region": r, "block": b},
            device_id_type=MESH,
        )

    def shared(sem):
        rest = sq_recv.at[pl.ds(0, len(everyone))]
        return pltpu.make_async_copy(rest, rest, sem.at[0])

    def share_all():
        sums = jnp.sum(
            jnp.where(eye, jnp.sum(squares[0], axis=1, keepdims=True), 0.0), axis=0, keepdims=True
        )
        sums = sums + jnp.where(live_lane, jnp.minimum(count, nbd).astype(f32), 0.0)
        sq_send[...] = sums
        for r, b in everyone:
            share(r, b).start()
        sq_recv[mine] = sums

    for peer in skip:
        serve(me, peer).wait_recv()
    give_back(skip, process(skip, lambda j, i, h: near_recv[i], share_all))

    @pl.when(has_prev)
    def _():
        for g in range(nbd):
            seam_ret[g] = seam_slot[flat[g]]
        seam_bwd.start()

    for g in range(nbd):
        out_ref[g] = adj_slot[flat[g]]

    def add(pair):
        blocks_back = ret_recv[pl.ds(pair * 2, 2)].reshape(2 * part, width)
        got = jnp.dot(spread[pair], blocks_back, preferred_element_type=f32)
        out_ref[...] = out_ref[...] - got.reshape(nbd, chans, width)

    def take(peers):
        for peer in peers:
            give(me, peer).wait_recv()

    take([sib])
    add(chip)
    take(beside)
    add(beside[0] // 2)

    take(mirror)
    add(mirror[0] // 2)

    @pl.when(has_next)
    def _():
        seam_where.wait_recv()
        mask = jnp.where(
            seam_tgt_in[...] == lax.broadcasted_iota(i32, (rows, rows), 0), 1.0, 0.0
        ).astype(bf16)
        seam_bwd.wait_recv()
        got = jnp.dot(mask, seam_ret_in[...].reshape(rows, width), preferred_element_type=f32)
        out_ref[...] = out_ref[...] - got.reshape(nbd, chans, width)

    take(skip)
    add(skip[0] // 2)

    shared(sq_rs).wait()
    total = sq_recv[0]
    for d in range(1, nregion * nblock):
        total = total + sq_recv[d]
    total_live = jnp.sum(jnp.where(live_lane, total, 0.0), axis=1, keepdims=True)
    blocks = nbd * nblock * nregion
    gtau_ref[...] = (
        0.5 * total[:, :chans] - 0.5 * width * total_live / tau_ref[...]
    ) / (blocks * width)

    for peer in others:
        request(peer, me).wait_send()
        give(peer, me).wait_send()
    for peer in skip + beside:
        serve(peer, me).wait_send()

    @pl.when(inner)
    def _():
        for peer in mirror:
            serve(peer, me).wait_send()

    to_sib.wait_send()

    @pl.when(at_end)
    def _():
        to_far.wait_send()
        relay.wait_send()

    shared(sq_ss).wait()

    @pl.when(has_next)
    def _():
        seam_fwd.wait_send()

    @pl.when(has_prev)
    def _():
        seam_where.wait_send()
        seam_bwd.wait_send()


def shards(obs, predict, factor, tau, nbr_dev, nbr_slot, counts):
    nbd, chans, width = obs.shape
    nblock = lax.axis_size("block")
    nregion = lax.axis_size("region")
    cap = max(2, 2 * nbd // nblock)
    rows = nbd * chans
    part = cap * chans
    lanes = -(-part // LANES) * LANES
    group = 2 if nblock % 2 == 0 and part % LANES == 0 else 1
    line = nblock == 8 and part == LANES
    bf16, f32, i32 = jnp.bfloat16, jnp.float32, jnp.int32
    vmem = pl.BlockSpec(memory_space=pltpu.VMEM)
    hbm = pl.BlockSpec(memory_space=pltpu.HBM)
    dma = pltpu.SemaphoreType.DMA
    blocks = pltpu.VMEM((nbd, chans, width), bf16)
    slots = pltpu.VMEM((nblock * cap, chans, width), bf16)
    inputs = [
        pltpu.SMEM((1, nbd), i32),
        pltpu.SMEM((2, nbd), i32),
        pltpu.SMEM((1,), i32),
        pltpu.VMEM((1, chans), f32),
        blocks,
        pltpu.VMEM((nbd, 2, width, width), bf16),
        pltpu.VMEM((nbd, width, width), bf16),
        pltpu.VMEM((nblock, 1, lanes), i32),
        pltpu.VMEM((nblock, 1, lanes), i32),
        slots,
        slots,
    ]
    middle = [
        pltpu.VMEM((nblock, part, width), bf16),
        pltpu.VMEM((nblock, part, width), bf16),
        blocks,
        pltpu.VMEM((1, rows), i32),
        pltpu.VMEM((1, rows), i32),
        blocks,
        blocks,
        pltpu.VMEM((1, LANES), i32),
        pltpu.SMEM((1, LANES), i32),
        pltpu.VMEM((nblock // group, rows, group * part), bf16),
        pltpu.VMEM((nbd, chans, width), f32),
    ]
    sums = [
        pltpu.VMEM((1, LANES), f32),
        pltpu.VMEM((nblock, 1, LANES), f32),
        pltpu.VMEM((1, LANES), f32),
        pltpu.VMEM((nregion, 1, LANES), f32),
        dma((8,)),
    ]
    sems = [dma((nblock,))] * 8 + [dma((nregion,))] * 2 + [dma((3,))] * 2
    if line:
        body = line_kernel
        scratch = inputs + [blocks] * 3 + middle
        scratch += [pltpu.VMEM((nblock * cap, chans, width), f32), slots, sums[0]]
        scratch += [pltpu.VMEM((nregion * nblock, 1, LANES), f32), sums[-1]]
        scratch += sems[:6] + [dma((1,))] * 2 + [dma((3,))] * 4
    else:
        body = kernel
        scratch = inputs + middle
        scratch += [pltpu.VMEM((nbd + 1, chans, width), bf16), blocks] + sums + sems
    grad_obs, grad_tau = pl.pallas_call(
        functools.partial(body, nblock, nregion, cap),
        out_shape=(
            jax.ShapeDtypeStruct((nbd, chans, width), f32),
            jax.ShapeDtypeStruct((1, chans), f32),
        ),
        in_specs=[hbm] * 7,
        out_specs=(vmem, vmem),
        scratch_shapes=scratch,
        compiler_params=pltpu.CompilerParams(
            collective_id=0, has_side_effects=True, vmem_limit_bytes=48 << 20
        ),
        name="vecchia",
    )(
        *(
            value if value is counts else pltpu.with_memory_space_constraint(value, pltpu.HBM)
            for value in (nbr_dev.T, nbr_slot.T, counts, tau.reshape(1, chans), obs, predict, factor)
        )
    )
    return grad_obs, grad_tau.reshape(chans)


def solution(mesh):
    in_specs = (
        P(("region", "block"), None, None),
        P(("region", "block"), None, None, None),
        P(("region", "block"), None, None),
        P(),
        P(("region", "block"), None),
        P(("region", "block"), None),
        P(("region", "block")),
    )
    out_specs = (P(("region", "block"), None, None), P())
    return jax.shard_map(shards, mesh=mesh, in_specs=in_specs, out_specs=out_specs, check_vma=False)
```

```python
import functools

import jax
import jax.numpy as jnp
from jax import lax
from jax.experimental import pallas as pl
from jax.experimental.pallas import tpu as pltpu
from jax.sharding import PartitionSpec as P

MESH = pl.DeviceIdType.MESH
LANES = 128


def kernel(
    nblock,
    nregion,
    cap,
    dev_hbm,
    slot_hbm,
    counts_hbm,
    tau_hbm,
    obs_hbm,
    predict_hbm,
    factor_hbm,
    out_ref,
    gtau_ref,
    dev_ref,
    slot_ref,
    counts_ref,
    tau_ref,
    obs,
    predict,
    factor,
    req_send,
    req_recv,
    near_send,
    near_recv,
    ret_send,
    ret_recv,
    seam_obs,
    seam_tgt,
    seam_tgt_in,
    seam_ret,
    seam_ret_in,
    held,
    held_ref,
    spread,
    partial,
    back,
    adjoint,
    sq_send,
    sq_recv,
    rg_send,
    rg_recv,
    local_sem,
    req_ss,
    req_rs,
    near_ss,
    near_rs,
    ret_ss,
    ret_rs,
    sq_ss,
    sq_rs,
    rg_ss,
    rg_rs,
    seam_ss,
    seam_rs,
):
    nbd, chans, width = obs.shape
    rows = nbd * chans
    part = cap * chans
    lanes = req_send.shape[2]
    group = 2 if nblock % 2 == 0 and part % LANES == 0 else 1
    me = lax.axis_index("block")
    region = lax.axis_index("region")
    bf16, f32, i32 = jnp.bfloat16, jnp.float32, jnp.int32

    half = me // (nblock // 2)

    def farthest(turn):
        below = nblock - 1 - turn - (me + turn + 1) // nblock
        above = turn + (turn - me + nblock) // nblock
        return below + half * (above - below)

    def each_peer(body, nearest=False):
        def visit(turn):
            body(farthest(nblock - 2 - turn if nearest else turn))

        if nblock <= 8:
            for turn in range(nblock - 1):
                visit(turn)
        else:

            def run(turn, carry):
                visit(turn)
                return carry

            lax.fori_loop(0, nblock - 1, run, 0)

    def each_region(body):
        for step in range(1, nregion):
            body(lax.rem(region + step, nregion))

    def to_block(src, dst, ss, rs, peer):
        return pltpu.make_async_remote_copy(
            src_ref=src,
            dst_ref=dst,
            send_sem=ss,
            recv_sem=rs,
            device_id={"block": peer},
            device_id_type=MESH,
        )

    def to_region(src, dst, ss, rs, peer):
        return pltpu.make_async_remote_copy(
            src_ref=src,
            dst_ref=dst,
            send_sem=ss,
            recv_sem=rs,
            device_id={"region": peer},
            device_id_type=MESH,
        )

    small = [
        pltpu.make_async_copy(src, dst, local_sem.at[3 + i])
        for i, (src, dst) in enumerate(
            [(dev_hbm, dev_ref), (slot_hbm, slot_ref), (counts_hbm, counts_ref), (tau_hbm, tau_ref)]
        )
    ]
    for copy in small:
        copy.start()

    barrier = pltpu.get_barrier_semaphore()
    each_peer(
        lambda peer: pl.semaphore_signal(
            barrier, inc=1, device_id={"block": peer}, device_id_type=MESH
        )
    )
    each_region(
        lambda peer: pl.semaphore_signal(
            barrier, inc=1, device_id={"region": peer}, device_id_type=MESH
        )
    )
    load_obs = pltpu.make_async_copy(obs_hbm, obs, local_sem.at[0])
    load_predict = pltpu.make_async_copy(predict_hbm, predict, local_sem.at[1])
    load_factor = pltpu.make_async_copy(factor_hbm, factor, local_sem.at[2])
    load_obs.start()
    load_predict.start()
    load_factor.start()

    for copy in small:
        copy.wait()

    dest = [dev_ref[0, h] for h in range(nbd)]
    flat = []
    for h in range(nbd):
        rank = jnp.int32(0)
        for g in range(h):
            rank = rank + (dest[g] == dest[h]).astype(i32)
        flat.append(dest[h] * cap + rank)

    lane = lax.broadcasted_iota(i32, (nblock, lanes), 1)
    spot = lax.broadcasted_iota(i32, (nblock, lanes), 0) * cap + lane // chans
    spot = jnp.where(lane < part, spot, -1)
    wanted = jnp.full((nblock, lanes), -1, i32)
    for h in range(nbd):
        wanted = jnp.where(spot == flat[h], slot_ref[0, h] * chans + lane % chans, wanted)
    for d in range(nblock):
        req_send[d] = wanted[d : d + 1]

    block_lane = lax.broadcasted_iota(i32, (1, rows), 1)
    owner_of = block_lane // chans
    seam_row = jnp.zeros((1, rows), i32)
    for h in range(nbd):
        seam_row = jnp.where(owner_of == h, slot_ref[1, h], seam_row)
    seam_tgt[...] = seam_row * chans + block_lane % chans

    place_lane = lax.broadcasted_iota(i32, (1, LANES), 1)
    holder = jnp.full((1, LANES), nbd, i32)
    for h in range(nbd):
        holder = jnp.where(place_lane == flat[h], h, holder)
    held[...] = holder
    load_held = pltpu.make_async_copy(held, held_ref, local_sem.at[7])
    load_held.start()
    back[nbd] = jnp.zeros((chans, width), bf16)

    pl.semaphore_wait(barrier, nblock - 1 + nregion - 1)

    def request(peer, mine):
        return to_block(req_send.at[peer], req_recv.at[mine], req_ss.at[peer], req_rs.at[mine], peer)

    each_peer(lambda peer: request(peer, me).start())
    req_recv[me] = req_send[me]

    down = lax.rem(region + 1, nregion)
    up = lax.rem(region + nregion - 1, nregion)
    seam_fwd = to_region(obs_hbm, seam_obs, seam_ss.at[0], seam_rs.at[0], down)
    seam_where = to_region(seam_tgt, seam_tgt_in, seam_ss.at[1], seam_rs.at[1], up)
    seam_bwd = to_region(seam_ret, seam_ret_in, seam_ss.at[2], seam_rs.at[2], up)
    has_prev = region > 0
    has_next = region < nregion - 1

    @pl.when(has_next)
    def _():
        seam_fwd.start()

    @pl.when(has_prev)
    def _():
        seam_where.start()

    load_obs.wait()
    pick_lane = lax.broadcasted_iota(i32, (part, rows), 1)

    def picked(peer):
        row = jnp.broadcast_to(req_recv[peer], (LANES, lanes))
        column = jnp.transpose(row)[:part]
        column = jnp.concatenate([column] * (rows // LANES), axis=1)
        mask = jnp.where(column == pick_lane, 1.0, 0.0).astype(bf16)
        got = jnp.dot(mask, obs[...].reshape(rows, width), preferred_element_type=f32)
        return got.astype(bf16).reshape(cap, chans, width)

    def span(d):
        return pl.ds(d * cap, cap)

    def serve(peer, mine):
        return to_block(
            near_send.at[span(peer)],
            near_recv.at[span(mine)],
            near_ss.at[peer],
            near_rs.at[mine],
            peer,
        )

    def put(peer):
        near_send[span(peer)] = picked(peer)
        serve(peer, me).start()

    def answer(peer):
        request(me, peer).wait_recv()
        put(peer)

    each_peer(answer, nearest=True)
    near_recv[span(me)] = picked(me)

    def build(pair):
        wanted_row = jnp.concatenate(
            [req_recv[pair * group + i][:, :part] for i in range(group)], axis=1
        )
        spread[pair] = jnp.where(
            wanted_row == lax.broadcasted_iota(i32, (rows, group * part), 0), 1.0, 0.0
        ).astype(bf16)

    for pair in range(nblock // group):
        build(pair)
    load_held.wait()

    @pl.when(has_prev)
    def _():
        seam_fwd.wait_recv()

    @pl.when(jnp.logical_not(has_prev))
    def _():
        seam_obs[...] = jnp.zeros_like(seam_obs)

    load_predict.wait()
    for g in range(nbd):
        partial[g] = obs[g].astype(f32) - jnp.dot(
            seam_obs[slot_ref[1, g]], predict[g, 1], preferred_element_type=f32
        )
    load_factor.wait()

    eye = lax.broadcasted_iota(i32, (chans, LANES), 0) == lax.broadcasted_iota(
        i32, (chans, LANES), 1
    )
    tau_row = jnp.concatenate([tau_ref[...], jnp.zeros((1, LANES - chans), f32)], axis=1)
    tau_col = jnp.sum(jnp.where(eye, tau_row, 0.0), axis=1, keepdims=True)
    count = counts_ref[0]

    each_peer(lambda peer: serve(me, peer).wait_recv(), nearest=True)

    nt = (((1,), (1,)), ((), ()))
    every = range(nbd)
    err = [
        (
            partial[g]
            - jnp.dot(near_recv[flat[g]], predict[g, 0], preferred_element_type=f32)
        ).astype(bf16)
        for g in every
    ]
    white = [jnp.dot(err[g], factor[g], preferred_element_type=f32) for g in every]
    live = [(g < count).astype(f32) for g in every]
    weighted = [(live[g] * tau_col * white[g]).astype(bf16) for g in every]
    squares = live[0] * white[0] * white[0]
    for g in range(1, nbd):
        squares = squares + live[g] * white[g] * white[g]
    live_lane = lax.broadcasted_iota(i32, (1, LANES), 1) == chans
    sums = jnp.sum(
        jnp.where(eye, jnp.sum(squares, axis=1, keepdims=True), 0.0), axis=0, keepdims=True
    )
    sums = sums + jnp.where(live_lane, jnp.minimum(count, nbd).astype(f32), 0.0)
    sq_send[...] = sums

    def share(peer, mine):
        return to_block(sq_send, sq_recv.at[mine], sq_ss.at[peer], sq_rs.at[mine], peer)

    each_peer(lambda peer: share(peer, me).start())
    sq_recv[me] = sums

    adj = [lax.dot_general(weighted[g], factor[g], nt, preferred_element_type=f32) for g in every]
    for g in every:
        out_ref[g] = adj[g]
        adjoint[g] = adj[g].astype(bf16)

    for g in every:
        back[g] = lax.dot_general(
            adjoint[g], predict[g, 0], nt, preferred_element_type=f32
        ).astype(bf16)

    def pack(dst, peer):
        for k in range(cap):
            dst[k * chans : (k + 1) * chans] = back[held_ref[0, peer * cap + k]]

    def give(peer, mine):
        return to_block(ret_send.at[peer], ret_recv.at[mine], ret_ss.at[peer], ret_rs.at[mine], peer)

    def give_back(peer):
        pack(ret_send.at[peer], peer)
        give(peer, me).start()

    each_peer(give_back)
    pack(ret_recv.at[me], me)

    @pl.when(has_prev)
    def _():
        for g in range(nbd):
            seam_ret[g] = lax.dot_general(
                adjoint[g], predict[g, 1], nt, preferred_element_type=f32
            ).astype(bf16)
        seam_bwd.start()

    each_peer(lambda peer: share(me, peer).wait_recv(), nearest=True)
    line = sq_recv[0]
    for d in range(1, nblock):
        line = line + sq_recv[d]
    rg_send[...] = line

    def share_region(peer, mine):
        return to_region(rg_send, rg_recv.at[mine], rg_ss.at[peer], rg_rs.at[mine], peer)

    each_region(lambda peer: share_region(peer, region).start())
    rg_recv[region] = line

    @pl.when(has_next)
    def _():
        seam_where_in = to_region(seam_tgt, seam_tgt_in, seam_ss.at[1], seam_rs.at[1], up)
        seam_where_in.wait_recv()
        mask = jnp.where(
            seam_tgt_in[...] == lax.broadcasted_iota(i32, (rows, rows), 0), 1.0, 0.0
        ).astype(bf16)
        seam_bwd.wait_recv()
        got = jnp.dot(mask, seam_ret_in[...].reshape(rows, width), preferred_element_type=f32)
        out_ref[...] = out_ref[...] - got.reshape(nbd, chans, width)

    def add(pair):
        blocks_back = ret_recv[pl.ds(pair * group, group)].reshape(group * part, width)
        got = jnp.dot(spread[pair], blocks_back, preferred_element_type=f32)
        out_ref[...] = out_ref[...] - got.reshape(nbd, chans, width)

    each_peer(lambda peer: give(me, peer).wait_recv(), nearest=True)
    for pair in range(nblock // group):
        add(pair)

    each_region(lambda peer: share_region(region, peer).wait_recv())
    total = rg_recv[0]
    for r in range(1, nregion):
        total = total + rg_recv[r]
    total_live = jnp.sum(jnp.where(live_lane, total, 0.0), axis=1, keepdims=True)
    blocks = nbd * nblock * nregion
    gtau_ref[...] = (
        0.5 * total[:, :chans] - 0.5 * width * total_live / tau_ref[...]
    ) / (blocks * width)

    def sent(peer):
        request(peer, me).wait_send()
        serve(peer, me).wait_send()
        give(peer, me).wait_send()
        share(peer, me).wait_send()

    each_peer(sent)
    each_region(lambda peer: share_region(peer, region).wait_send())

    @pl.when(has_next)
    def _():
        seam_fwd.wait_send()

    @pl.when(has_prev)
    def _():
        seam_where.wait_send()
        seam_bwd.wait_send()


def line_kernel(
    nblock,
    nregion,
    cap,
    dev_hbm,
    slot_hbm,
    counts_hbm,
    tau_hbm,
    obs_hbm,
    predict_hbm,
    factor_hbm,
    out_ref,
    gtau_ref,
    dev_ref,
    slot_ref,
    counts_ref,
    tau_ref,
    obs,
    predict,
    factor,
    req_send,
    req_recv,
    pass_recv,
    near_send,
    near_recv,
    raw_sib,
    raw_far,
    raw_relay,
    ret_send,
    ret_recv,
    seam_obs,
    seam_tgt,
    seam_tgt_in,
    seam_ret,
    seam_ret_in,
    held,
    held_ref,
    spread,
    partial,
    adj_slot,
    seam_slot,
    sq_send,
    sq_recv,
    local_sem,
    req_ss,
    req_rs,
    near_ss,
    near_rs,
    ret_ss,
    ret_rs,
    sq_ss,
    sq_rs,
    seam_ss,
    seam_rs,
    raw_ss,
    raw_rs,
    pass_ss,
    pass_rs,
):
    nbd, chans, width = obs.shape
    rows = nbd * chans
    part = cap * chans
    me = lax.axis_index("block")
    region = lax.axis_index("region")
    bf16, f32, i32 = jnp.bfloat16, jnp.float32, jnp.int32
    nt = (((1,), (1,)), ((), ()))

    def flip(d, bit):
        return d + bit - 2 * bit * lax.rem(d // bit, 2)

    sib = flip(me, 1)
    chip = me // 2
    own = [me, sib]
    beside = [flip(d, 2) for d in own]
    skip = [flip(d, 4) for d in own]
    mirror = [flip(d, 4) for d in beside]
    at_end = chip * (nblock // 2 - 1 - chip) == 0
    inner = jnp.logical_not(at_end)
    others = mirror + skip + beside + [sib]

    def to_block(src, dst, ss, rs, peer):
        return pltpu.make_async_remote_copy(
            src_ref=src,
            dst_ref=dst,
            send_sem=ss,
            recv_sem=rs,
            device_id={"block": peer},
            device_id_type=MESH,
        )

    def to_region(src, dst, ss, rs, peer):
        return pltpu.make_async_remote_copy(
            src_ref=src,
            dst_ref=dst,
            send_sem=ss,
            recv_sem=rs,
            device_id={"region": peer},
            device_id_type=MESH,
        )

    regions = [lax.rem(region + step, nregion) for step in range(1, nregion)]

    small = [
        pltpu.make_async_copy(src, dst, local_sem.at[3 + i])
        for i, (src, dst) in enumerate(
            [(dev_hbm, dev_ref), (slot_hbm, slot_ref), (counts_hbm, counts_ref), (tau_hbm, tau_ref)]
        )
    ]
    for copy in small:
        copy.start()

    barrier = pltpu.get_barrier_semaphore()
    for peer in others:
        pl.semaphore_signal(barrier, inc=1, device_id={"block": peer}, device_id_type=MESH)
    for peer in regions:
        pl.semaphore_signal(barrier, inc=1, device_id={"region": peer}, device_id_type=MESH)
    load_obs = pltpu.make_async_copy(obs_hbm, obs, local_sem.at[0])
    load_predict = pltpu.make_async_copy(predict_hbm, predict, local_sem.at[1])
    load_factor = pltpu.make_async_copy(factor_hbm, factor, local_sem.at[2])
    load_obs.start()
    load_predict.start()
    load_factor.start()

    for copy in small:
        copy.wait()

    dest = [dev_ref[0, h] for h in range(nbd)]
    flat = []
    for h in range(nbd):
        rank = jnp.int32(0)
        for g in range(h):
            rank = rank + (dest[g] == dest[h]).astype(i32)
        flat.append(dest[h] * cap + rank)

    lane = lax.broadcasted_iota(i32, (nblock, part), 1)
    spot = lax.broadcasted_iota(i32, (nblock, part), 0) * cap + lane // chans
    wanted = jnp.full((nblock, part), -1, i32)
    for h in range(nbd):
        wanted = jnp.where(spot == flat[h], slot_ref[0, h] * chans + lane % chans, wanted)
    for d in range(nblock):
        req_send[d] = wanted[d : d + 1]

    block_lane = lax.broadcasted_iota(i32, (1, rows), 1)
    owner_of = block_lane // chans
    seam_row = jnp.zeros((1, rows), i32)
    for h in range(nbd):
        seam_row = jnp.where(owner_of == h, slot_ref[1, h], seam_row)
    seam_tgt[...] = seam_row * chans + block_lane % chans

    place_lane = lax.broadcasted_iota(i32, (1, LANES), 1)
    holder = jnp.full((1, LANES), nbd, i32)
    for h in range(nbd):
        holder = jnp.where(place_lane == flat[h], h, holder)
    held[...] = holder
    load_held = pltpu.make_async_copy(held, held_ref, local_sem.at[7])
    load_held.start()

    pl.semaphore_wait(barrier, nblock - 1 + nregion - 1)

    def request(peer, mine):
        return to_block(req_send.at[peer], req_recv.at[mine], req_ss.at[peer], req_rs.at[mine], peer)

    def request_pass(owner, peer, mine):
        return to_block(
            req_send.at[owner], pass_recv.at[mine], pass_ss.at[peer], pass_rs.at[mine], peer
        )

    for peer in others:
        request(peer, me).start()
    req_recv[me] = req_send[me]

    @pl.when(inner)
    def _():
        for owner, peer in zip(skip, beside):
            request_pass(owner, peer, me).start()


    to_sib = to_block(obs_hbm, raw_sib, raw_ss.at[0], raw_rs.at[0], sib)
    to_far = to_block(obs_hbm, raw_far, raw_ss.at[1], raw_rs.at[1], mirror[0])
    relay = to_block(raw_far, raw_relay, raw_ss.at[2], raw_rs.at[2], sib)

    down = lax.rem(region + 1, nregion)
    up = lax.rem(region + nregion - 1, nregion)
    seam_fwd = to_region(obs_hbm, seam_obs, seam_ss.at[0], seam_rs.at[0], down)
    seam_where = to_region(seam_tgt, seam_tgt_in, seam_ss.at[1], seam_rs.at[1], up)
    seam_bwd = to_region(seam_ret, seam_ret_in, seam_ss.at[2], seam_rs.at[2], up)
    has_prev = region > 0
    has_next = region < nregion - 1

    @pl.when(at_end)
    def _():
        to_far.start()

    @pl.when(has_next)
    def _():
        seam_fwd.start()

    @pl.when(has_prev)
    def _():
        seam_where.start()

    to_sib.start()

    @pl.when(inner)
    def _():
        raw_far[...] = jnp.zeros_like(raw_far)
        raw_relay[...] = jnp.zeros_like(raw_relay)

    load_obs.wait()
    pick_lane = lax.broadcasted_iota(i32, (part, rows), 1)

    def picked(row, source):
        row = jnp.broadcast_to(row, (LANES, part))
        column = jnp.concatenate([jnp.transpose(row)] * (rows // LANES), axis=1)
        mask = jnp.where(column == pick_lane, 1.0, 0.0).astype(bf16)
        got = jnp.dot(mask, source[...].reshape(rows, width), preferred_element_type=f32)
        return got.astype(bf16).reshape(cap, chans, width)

    def span(d):
        return pl.ds(d * cap, cap)

    def serve(peer, mine):
        return to_block(
            near_send.at[span(peer)],
            near_recv.at[span(mine)],
            near_ss.at[peer],
            near_rs.at[mine],
            peer,
        )

    def put(peer):
        near_send[span(peer)] = picked(req_recv[peer], obs)
        serve(peer, me).start()

    def pass_on(j):
        return to_block(
            near_send.at[span(skip[j])],
            near_recv.at[span(mirror[0])],
            near_ss.at[skip[j]],
            near_rs.at[mirror[0]],
            beside[j],
        )

    for peer in mirror + skip:
        request(me, peer).wait_recv()

    @pl.when(inner)
    def _():
        for peer in mirror + skip:
            put(peer)

    @pl.when(at_end)
    def _():
        for peer in mirror:
            near_recv[span(peer)] = jnp.zeros((cap, chans, width), bf16)

    for peer in beside:
        request(me, peer).wait_recv()
        put(peer)
    request(me, sib).wait_recv()

    def build(pair):
        wanted_row = jnp.concatenate([req_recv[pair * 2 + i] for i in range(2)], axis=1)
        spread[pair] = jnp.where(
            wanted_row == lax.broadcasted_iota(i32, (rows, 2 * part), 0), 1.0, 0.0
        ).astype(bf16)

    for pair in range(nblock // 2):
        build(pair)
    load_held.wait()

    eye = lax.broadcasted_iota(i32, (chans, LANES), 0) == lax.broadcasted_iota(
        i32, (chans, LANES), 1
    )
    tau_row = jnp.concatenate([tau_ref[...], jnp.zeros((1, LANES - chans), f32)], axis=1)
    tau_col = jnp.sum(jnp.where(eye, tau_row, 0.0), axis=1, keepdims=True)
    count = counts_ref[0]

    @pl.when(has_prev)
    def _():
        seam_fwd.wait_recv()

    @pl.when(jnp.logical_not(has_prev))
    def _():
        seam_obs[...] = jnp.zeros_like(seam_obs)

    @pl.when(at_end)
    def _():
        to_far.wait_recv()
        relay.start()
        for j, peer in enumerate(beside):
            request_pass(mirror[0], me, peer).wait_recv()
            near_send[span(skip[j])] = picked(pass_recv[peer], raw_far)
            pass_on(j).start()

    load_predict.wait()
    for g in range(nbd):
        partial[g] = obs[g].astype(f32) - jnp.dot(
            seam_obs[slot_ref[1, g]], predict[g, 1], preferred_element_type=f32
        )
    load_factor.wait()

    def give(peer, mine):
        return to_block(ret_send.at[peer], ret_recv.at[mine], ret_ss.at[peer], ret_rs.at[mine], peer)

    squares = [jnp.zeros((chans, width), f32)]

    def process(peers, near_of, between=None):
        at = [peer * cap + k for peer in peers for k in range(cap)]
        every = range(len(at))
        who = [held_ref[0, i] for i in at]
        block = [jnp.minimum(w, nbd - 1) for w in who]
        live = [(w < count).astype(f32) for w in who]
        near = [near_of(i // cap, at[i], block[i]) for i in every]
        err = [
            (
                partial[block[i]]
                - jnp.dot(near[i], predict[block[i], 0], preferred_element_type=f32)
            ).astype(bf16)
            for i in every
        ]
        white = [jnp.dot(err[i], factor[block[i]], preferred_element_type=f32) for i in every]
        for i in every:
            squares[0] = squares[0] + live[i] * white[i] * white[i]
        if between is not None:
            between()
        weighted = [(live[i] * tau_col * white[i]).astype(bf16) for i in every]
        adj = [
            lax.dot_general(weighted[i], factor[block[i]], nt, preferred_element_type=f32)
            for i in every
        ]
        for i in every:
            adj_slot[at[i]] = adj[i]
        both = [
            lax.dot_general(
                adj[i].astype(bf16),
                predict[block[i]].reshape(2 * width, width),
                nt,
                preferred_element_type=f32,
            ).astype(bf16)
            for i in every
        ]
        for i in every:
            seam_slot[at[i]] = both[i][:, width:]
        return [both[i][:, :width] for i in every]

    def give_back(peers, back):
        for j, peer in enumerate(peers):
            for k in range(cap):
                ret_send[peer, k * chans : (k + 1) * chans] = back[j * cap + k]
            give(peer, me).start()

    @pl.when(at_end)
    def _():
        relay.wait_recv()

    @pl.when(inner)
    def _():
        for peer in mirror:
            serve(me, peer).wait_recv()

    raws = [raw_far, raw_relay]
    give_back(
        mirror,
        process(
            mirror,
            lambda j, i, h: jnp.where(at_end, raws[j][slot_ref[0, h]], near_recv[i]),
        ),
    )

    for peer in beside:
        serve(me, peer).wait_recv()
    give_back(beside, process(beside, lambda j, i, h: near_recv[i]))

    to_sib.wait_recv()
    homes = [obs, raw_sib]
    back = process(own, lambda j, i, h: homes[j][slot_ref[0, h]])
    for k in range(cap):
        ret_recv[me, k * chans : (k + 1) * chans] = back[k]
    give_back([sib], back[cap:])

    live_lane = lax.broadcasted_iota(i32, (1, LANES), 1) == chans

    everyone = [(r, b) for r in regions for b in others + [me]] + [(region, b) for b in others]
    mine = region * nblock + me

    def share(r, b):
        return pltpu.make_async_remote_copy(
            src_ref=sq_send,
            dst_ref=sq_recv.at[mine],
            send_sem=sq_ss.at[0],
            recv_sem=sq_rs.at[0],
            device_id={"region": r, "block": b},
            device_id_type=MESH,
        )

    def shared(sem):
        rest = sq_recv.at[pl.ds(0, len(everyone))]
        return pltpu.make_async_copy(rest, rest, sem.at[0])

    def share_all():
        sums = jnp.sum(
            jnp.where(eye, jnp.sum(squares[0], axis=1, keepdims=True), 0.0), axis=0, keepdims=True
        )
        sums = sums + jnp.where(live_lane, jnp.minimum(count, nbd).astype(f32), 0.0)
        sq_send[...] = sums
        for r, b in everyone:
            share(r, b).start()
        sq_recv[mine] = sums

    for peer in skip:
        serve(me, peer).wait_recv()
    give_back(skip, process(skip, lambda j, i, h: near_recv[i], share_all))

    @pl.when(has_prev)
    def _():
        for g in range(nbd):
            seam_ret[g] = seam_slot[flat[g]]
        seam_bwd.start()

    for g in range(nbd):
        out_ref[g] = adj_slot[flat[g]]

    def add(pair):
        blocks_back = ret_recv[pl.ds(pair * 2, 2)].reshape(2 * part, width)
        got = jnp.dot(spread[pair], blocks_back, preferred_element_type=f32)
        out_ref[...] = out_ref[...] - got.reshape(nbd, chans, width)

    def take(peers):
        for peer in peers:
            give(me, peer).wait_recv()

    for peer in others:
        request(peer, me).wait_send()
    for peer in beside:
        serve(peer, me).wait_send()

    @pl.when(inner)
    def _():
        for peer in mirror + skip:
            serve(peer, me).wait_send()
        for owner, peer in zip(skip, beside):
            request_pass(owner, peer, me).wait_send()

    to_sib.wait_send()

    @pl.when(at_end)
    def _():
        to_far.wait_send()
        relay.wait_send()
        for j in range(2):
            pass_on(j).wait_send()

    @pl.when(has_next)
    def _():
        seam_fwd.wait_send()

    @pl.when(has_prev)
    def _():
        seam_where.wait_send()

    take([sib])
    add(chip)
    take(beside)
    add(beside[0] // 2)

    take(mirror)
    add(mirror[0] // 2)

    @pl.when(has_next)
    def _():
        seam_where.wait_recv()
        mask = jnp.where(
            seam_tgt_in[...] == lax.broadcasted_iota(i32, (rows, rows), 0), 1.0, 0.0
        ).astype(bf16)
        seam_bwd.wait_recv()
        got = jnp.dot(mask, seam_ret_in[...].reshape(rows, width), preferred_element_type=f32)
        out_ref[...] = out_ref[...] - got.reshape(nbd, chans, width)

    take(skip)
    add(skip[0] // 2)

    shared(sq_rs).wait()
    total = sq_recv[0]
    for d in range(1, nregion * nblock):
        total = total + sq_recv[d]
    total_live = jnp.sum(jnp.where(live_lane, total, 0.0), axis=1, keepdims=True)
    blocks = nbd * nblock * nregion
    gtau_ref[...] = (
        0.5 * total[:, :chans] - 0.5 * width * total_live / tau_ref[...]
    ) / (blocks * width)

    for peer in others:
        give(peer, me).wait_send()
    shared(sq_ss).wait()

    @pl.when(has_prev)
    def _():
        seam_bwd.wait_send()


def write_out(obs_ref, tau_ref, obs_hbm, tau_hbm, sem):
    copies = [
        pltpu.make_async_copy(src, dst, sem.at[i])
        for i, (src, dst) in enumerate([(obs_ref, obs_hbm), (tau_ref, tau_hbm)])
    ]
    for copy in copies:
        copy.start()
    for copy in copies:
        copy.wait()


def shards(obs, predict, factor, tau, nbr_dev, nbr_slot, counts):
    nbd, chans, width = obs.shape
    nblock = lax.axis_size("block")
    nregion = lax.axis_size("region")
    cap = max(2, 2 * nbd // nblock)
    rows = nbd * chans
    part = cap * chans
    lanes = -(-part // LANES) * LANES
    group = 2 if nblock % 2 == 0 and part % LANES == 0 else 1
    line = nblock == 8 and part == LANES
    bf16, f32, i32 = jnp.bfloat16, jnp.float32, jnp.int32
    vmem = pl.BlockSpec(memory_space=pltpu.VMEM)
    hbm = pl.BlockSpec(memory_space=pltpu.HBM)
    dma = pltpu.SemaphoreType.DMA
    blocks = pltpu.VMEM((nbd, chans, width), bf16)
    slots = pltpu.VMEM((nblock * cap, chans, width), bf16)
    inputs = [
        pltpu.SMEM((1, nbd), i32),
        pltpu.SMEM((2, nbd), i32),
        pltpu.SMEM((1,), i32),
        pltpu.VMEM((1, chans), f32),
        blocks,
        pltpu.VMEM((nbd, 2, width, width), bf16),
        pltpu.VMEM((nbd, width, width), bf16),
        pltpu.VMEM((nblock, 1, lanes), i32),
        pltpu.VMEM((nblock, 1, lanes), i32),
        slots,
        slots,
    ]
    middle = [
        pltpu.VMEM((nblock, part, width), bf16),
        pltpu.VMEM((nblock, part, width), bf16),
        blocks,
        pltpu.VMEM((1, rows), i32),
        pltpu.VMEM((1, rows), i32),
        blocks,
        blocks,
        pltpu.VMEM((1, LANES), i32),
        pltpu.SMEM((1, LANES), i32),
        pltpu.VMEM((nblock // group, rows, group * part), bf16),
        pltpu.VMEM((nbd, chans, width), f32),
    ]
    sums = [
        pltpu.VMEM((1, LANES), f32),
        pltpu.VMEM((nblock, 1, LANES), f32),
        pltpu.VMEM((1, LANES), f32),
        pltpu.VMEM((nregion, 1, LANES), f32),
        dma((8,)),
    ]
    sems = [dma((nblock,))] * 8 + [dma((nregion,))] * 2 + [dma((3,))] * 2
    if line:
        body = line_kernel
        scratch = inputs[:9] + inputs[8:] + [blocks] * 3 + middle
        scratch += [pltpu.VMEM((nblock * cap, chans, width), f32), slots, sums[0]]
        scratch += [pltpu.VMEM((nregion * nblock, 1, LANES), f32), sums[-1]]
        scratch += sems[:6] + [dma((1,))] * 2 + [dma((3,))] * 4 + [dma((nblock,))] * 2
    else:
        body = kernel
        scratch = inputs + middle
        scratch += [pltpu.VMEM((nbd + 1, chans, width), bf16), blocks] + sums + sems
    grad_obs, grad_tau = pl.pallas_call(
        functools.partial(body, nblock, nregion, cap),
        out_shape=(
            jax.ShapeDtypeStruct((nbd, chans, width), f32),
            jax.ShapeDtypeStruct((1, chans), f32),
        ),
        in_specs=[hbm] * 7,
        out_specs=(vmem, vmem),
        scratch_shapes=scratch,
        compiler_params=pltpu.CompilerParams(
            collective_id=0, has_side_effects=True, vmem_limit_bytes=48 << 20
        ),
        name="vecchia",
    )(
        *(
            value if value is counts else pltpu.with_memory_space_constraint(value, pltpu.HBM)
            for value in (nbr_dev.T, nbr_slot.T, counts, tau.reshape(1, chans), obs, predict, factor)
        )
    )
    grad_obs, grad_tau = pl.pallas_call(
        write_out,
        out_shape=(
            jax.ShapeDtypeStruct((nbd, chans, width), f32),
            jax.ShapeDtypeStruct((1, chans), f32),
        ),
        in_specs=[vmem, vmem],
        out_specs=(hbm, hbm),
        scratch_shapes=[dma((2,))],
        name="write_out",
    )(*(pltpu.with_memory_space_constraint(x, pltpu.VMEM) for x in (grad_obs, grad_tau)))
    return grad_obs, grad_tau.reshape(chans)


def solution(mesh):
    in_specs = (
        P(("region", "block"), None, None),
        P(("region", "block"), None, None, None),
        P(("region", "block"), None, None),
        P(),
        P(("region", "block"), None),
        P(("region", "block"), None),
        P(("region", "block")),
    )
    out_specs = (P(("region", "block"), None, None), P())
    return jax.shard_map(shards, mesh=mesh, in_specs=in_specs, out_specs=out_specs, check_vma=False)
```

```python
import functools

import jax
import jax.numpy as jnp
from jax import lax
from jax.experimental import pallas as pl
from jax.experimental.pallas import tpu as pltpu
from jax.sharding import PartitionSpec as P

MESH = pl.DeviceIdType.MESH
LANES = 128


def kernel(
    nblock,
    nregion,
    cap,
    dev_hbm,
    slot_hbm,
    counts_hbm,
    tau_hbm,
    obs_hbm,
    predict_hbm,
    factor_hbm,
    out_ref,
    gtau_ref,
    dev_ref,
    slot_ref,
    counts_ref,
    tau_ref,
    obs,
    predict,
    factor,
    req_send,
    req_recv,
    near_send,
    near_recv,
    ret_send,
    ret_recv,
    seam_obs,
    seam_tgt,
    seam_tgt_in,
    seam_ret,
    seam_ret_in,
    held,
    held_ref,
    spread,
    partial,
    back,
    adjoint,
    sq_send,
    sq_recv,
    rg_send,
    rg_recv,
    local_sem,
    req_ss,
    req_rs,
    near_ss,
    near_rs,
    ret_ss,
    ret_rs,
    sq_ss,
    sq_rs,
    rg_ss,
    rg_rs,
    seam_ss,
    seam_rs,
):
    nbd, chans, width = obs.shape
    rows = nbd * chans
    part = cap * chans
    lanes = req_send.shape[2]
    group = 2 if nblock % 2 == 0 and part % LANES == 0 else 1
    me = lax.axis_index("block")
    region = lax.axis_index("region")
    bf16, f32, i32 = jnp.bfloat16, jnp.float32, jnp.int32

    half = me // (nblock // 2)

    def farthest(turn):
        below = nblock - 1 - turn - (me + turn + 1) // nblock
        above = turn + (turn - me + nblock) // nblock
        return below + half * (above - below)

    def each_peer(body, nearest=False):
        def visit(turn):
            body(farthest(nblock - 2 - turn if nearest else turn))

        if nblock <= 8:
            for turn in range(nblock - 1):
                visit(turn)
        else:

            def run(turn, carry):
                visit(turn)
                return carry

            lax.fori_loop(0, nblock - 1, run, 0)

    def each_region(body):
        for step in range(1, nregion):
            body(lax.rem(region + step, nregion))

    def to_block(src, dst, ss, rs, peer):
        return pltpu.make_async_remote_copy(
            src_ref=src,
            dst_ref=dst,
            send_sem=ss,
            recv_sem=rs,
            device_id={"block": peer},
            device_id_type=MESH,
        )

    def to_region(src, dst, ss, rs, peer):
        return pltpu.make_async_remote_copy(
            src_ref=src,
            dst_ref=dst,
            send_sem=ss,
            recv_sem=rs,
            device_id={"region": peer},
            device_id_type=MESH,
        )

    small = [
        pltpu.make_async_copy(src, dst, local_sem.at[3 + i])
        for i, (src, dst) in enumerate(
            [(dev_hbm, dev_ref), (slot_hbm, slot_ref), (counts_hbm, counts_ref), (tau_hbm, tau_ref)]
        )
    ]
    for copy in small:
        copy.start()

    barrier = pltpu.get_barrier_semaphore()
    each_peer(
        lambda peer: pl.semaphore_signal(
            barrier, inc=1, device_id={"block": peer}, device_id_type=MESH
        )
    )
    each_region(
        lambda peer: pl.semaphore_signal(
            barrier, inc=1, device_id={"region": peer}, device_id_type=MESH
        )
    )
    load_obs = pltpu.make_async_copy(obs_hbm, obs, local_sem.at[0])
    load_predict = pltpu.make_async_copy(predict_hbm, predict, local_sem.at[1])
    load_factor = pltpu.make_async_copy(factor_hbm, factor, local_sem.at[2])
    load_obs.start()
    load_predict.start()
    load_factor.start()

    for copy in small:
        copy.wait()

    dest = [dev_ref[0, h] for h in range(nbd)]
    flat = []
    for h in range(nbd):
        rank = jnp.int32(0)
        for g in range(h):
            rank = rank + (dest[g] == dest[h]).astype(i32)
        flat.append(dest[h] * cap + rank)

    lane = lax.broadcasted_iota(i32, (nblock, lanes), 1)
    spot = lax.broadcasted_iota(i32, (nblock, lanes), 0) * cap + lane // chans
    spot = jnp.where(lane < part, spot, -1)
    wanted = jnp.full((nblock, lanes), -1, i32)
    for h in range(nbd):
        wanted = jnp.where(spot == flat[h], slot_ref[0, h] * chans + lane % chans, wanted)
    for d in range(nblock):
        req_send[d] = wanted[d : d + 1]

    block_lane = lax.broadcasted_iota(i32, (1, rows), 1)
    owner_of = block_lane // chans
    seam_row = jnp.zeros((1, rows), i32)
    for h in range(nbd):
        seam_row = jnp.where(owner_of == h, slot_ref[1, h], seam_row)
    seam_tgt[...] = seam_row * chans + block_lane % chans

    place_lane = lax.broadcasted_iota(i32, (1, LANES), 1)
    holder = jnp.full((1, LANES), nbd, i32)
    for h in range(nbd):
        holder = jnp.where(place_lane == flat[h], h, holder)
    held[...] = holder
    load_held = pltpu.make_async_copy(held, held_ref, local_sem.at[7])
    load_held.start()
    back[nbd] = jnp.zeros((chans, width), bf16)

    pl.semaphore_wait(barrier, nblock - 1 + nregion - 1)

    def request(peer, mine):
        return to_block(req_send.at[peer], req_recv.at[mine], req_ss.at[peer], req_rs.at[mine], peer)

    each_peer(lambda peer: request(peer, me).start())
    req_recv[me] = req_send[me]

    down = lax.rem(region + 1, nregion)
    up = lax.rem(region + nregion - 1, nregion)
    seam_fwd = to_region(obs_hbm, seam_obs, seam_ss.at[0], seam_rs.at[0], down)
    seam_where = to_region(seam_tgt, seam_tgt_in, seam_ss.at[1], seam_rs.at[1], up)
    seam_bwd = to_region(seam_ret, seam_ret_in, seam_ss.at[2], seam_rs.at[2], up)
    has_prev = region > 0
    has_next = region < nregion - 1

    @pl.when(has_next)
    def _():
        seam_fwd.start()

    @pl.when(has_prev)
    def _():
        seam_where.start()

    load_obs.wait()
    pick_lane = lax.broadcasted_iota(i32, (part, rows), 1)

    def picked(peer):
        row = jnp.broadcast_to(req_recv[peer], (LANES, lanes))
        column = jnp.transpose(row)[:part]
        column = jnp.concatenate([column] * (rows // LANES), axis=1)
        mask = jnp.where(column == pick_lane, 1.0, 0.0).astype(bf16)
        got = jnp.dot(mask, obs[...].reshape(rows, width), preferred_element_type=f32)
        return got.astype(bf16).reshape(cap, chans, width)

    def span(d):
        return pl.ds(d * cap, cap)

    def serve(peer, mine):
        return to_block(
            near_send.at[span(peer)],
            near_recv.at[span(mine)],
            near_ss.at[peer],
            near_rs.at[mine],
            peer,
        )

    def put(peer):
        near_send[span(peer)] = picked(peer)
        serve(peer, me).start()

    def answer(peer):
        request(me, peer).wait_recv()
        put(peer)

    each_peer(answer, nearest=True)
    near_recv[span(me)] = picked(me)

    def build(pair):
        wanted_row = jnp.concatenate(
            [req_recv[pair * group + i][:, :part] for i in range(group)], axis=1
        )
        spread[pair] = jnp.where(
            wanted_row == lax.broadcasted_iota(i32, (rows, group * part), 0), 1.0, 0.0
        ).astype(bf16)

    for pair in range(nblock // group):
        build(pair)
    load_held.wait()

    @pl.when(has_prev)
    def _():
        seam_fwd.wait_recv()

    @pl.when(jnp.logical_not(has_prev))
    def _():
        seam_obs[...] = jnp.zeros_like(seam_obs)

    load_predict.wait()
    for g in range(nbd):
        partial[g] = obs[g].astype(f32) - jnp.dot(
            seam_obs[slot_ref[1, g]], predict[g, 1], preferred_element_type=f32
        )
    load_factor.wait()

    eye = lax.broadcasted_iota(i32, (chans, LANES), 0) == lax.broadcasted_iota(
        i32, (chans, LANES), 1
    )
    tau_row = jnp.concatenate([tau_ref[...], jnp.zeros((1, LANES - chans), f32)], axis=1)
    tau_col = jnp.sum(jnp.where(eye, tau_row, 0.0), axis=1, keepdims=True)
    count = counts_ref[0]

    each_peer(lambda peer: serve(me, peer).wait_recv(), nearest=True)

    nt = (((1,), (1,)), ((), ()))
    every = range(nbd)
    err = [
        (
            partial[g]
            - jnp.dot(near_recv[flat[g]], predict[g, 0], preferred_element_type=f32)
        ).astype(bf16)
        for g in every
    ]
    white = [jnp.dot(err[g], factor[g], preferred_element_type=f32) for g in every]
    live = [(g < count).astype(f32) for g in every]
    weighted = [(live[g] * tau_col * white[g]).astype(bf16) for g in every]
    squares = live[0] * white[0] * white[0]
    for g in range(1, nbd):
        squares = squares + live[g] * white[g] * white[g]
    live_lane = lax.broadcasted_iota(i32, (1, LANES), 1) == chans
    sums = jnp.sum(
        jnp.where(eye, jnp.sum(squares, axis=1, keepdims=True), 0.0), axis=0, keepdims=True
    )
    sums = sums + jnp.where(live_lane, jnp.minimum(count, nbd).astype(f32), 0.0)
    sq_send[...] = sums

    def share(peer, mine):
        return to_block(sq_send, sq_recv.at[mine], sq_ss.at[peer], sq_rs.at[mine], peer)

    each_peer(lambda peer: share(peer, me).start())
    sq_recv[me] = sums

    adj = [lax.dot_general(weighted[g], factor[g], nt, preferred_element_type=f32) for g in every]
    for g in every:
        out_ref[g] = adj[g]
        adjoint[g] = adj[g].astype(bf16)

    for g in every:
        back[g] = lax.dot_general(
            adjoint[g], predict[g, 0], nt, preferred_element_type=f32
        ).astype(bf16)

    def pack(dst, peer):
        for k in range(cap):
            dst[k * chans : (k + 1) * chans] = back[held_ref[0, peer * cap + k]]

    def give(peer, mine):
        return to_block(ret_send.at[peer], ret_recv.at[mine], ret_ss.at[peer], ret_rs.at[mine], peer)

    def give_back(peer):
        pack(ret_send.at[peer], peer)
        give(peer, me).start()

    each_peer(give_back)
    pack(ret_recv.at[me], me)

    @pl.when(has_prev)
    def _():
        for g in range(nbd):
            seam_ret[g] = lax.dot_general(
                adjoint[g], predict[g, 1], nt, preferred_element_type=f32
            ).astype(bf16)
        seam_bwd.start()

    each_peer(lambda peer: share(me, peer).wait_recv(), nearest=True)
    line = sq_recv[0]
    for d in range(1, nblock):
        line = line + sq_recv[d]
    rg_send[...] = line

    def share_region(peer, mine):
        return to_region(rg_send, rg_recv.at[mine], rg_ss.at[peer], rg_rs.at[mine], peer)

    each_region(lambda peer: share_region(peer, region).start())
    rg_recv[region] = line

    @pl.when(has_next)
    def _():
        seam_where_in = to_region(seam_tgt, seam_tgt_in, seam_ss.at[1], seam_rs.at[1], up)
        seam_where_in.wait_recv()
        mask = jnp.where(
            seam_tgt_in[...] == lax.broadcasted_iota(i32, (rows, rows), 0), 1.0, 0.0
        ).astype(bf16)
        seam_bwd.wait_recv()
        got = jnp.dot(mask, seam_ret_in[...].reshape(rows, width), preferred_element_type=f32)
        out_ref[...] = out_ref[...] - got.reshape(nbd, chans, width)

    def add(pair):
        blocks_back = ret_recv[pl.ds(pair * group, group)].reshape(group * part, width)
        got = jnp.dot(spread[pair], blocks_back, preferred_element_type=f32)
        out_ref[...] = out_ref[...] - got.reshape(nbd, chans, width)

    each_peer(lambda peer: give(me, peer).wait_recv(), nearest=True)
    for pair in range(nblock // group):
        add(pair)

    each_region(lambda peer: share_region(region, peer).wait_recv())
    total = rg_recv[0]
    for r in range(1, nregion):
        total = total + rg_recv[r]
    total_live = jnp.sum(jnp.where(live_lane, total, 0.0), axis=1, keepdims=True)
    blocks = nbd * nblock * nregion
    gtau_ref[...] = (
        0.5 * total[:, :chans] - 0.5 * width * total_live / tau_ref[...]
    ) / (blocks * width)

    def sent(peer):
        request(peer, me).wait_send()
        serve(peer, me).wait_send()
        give(peer, me).wait_send()
        share(peer, me).wait_send()

    each_peer(sent)
    each_region(lambda peer: share_region(peer, region).wait_send())

    @pl.when(has_next)
    def _():
        seam_fwd.wait_send()

    @pl.when(has_prev)
    def _():
        seam_where.wait_send()
        seam_bwd.wait_send()


def line_kernel(
    nblock,
    nregion,
    cap,
    dev_hbm,
    slot_hbm,
    counts_hbm,
    tau_hbm,
    obs_hbm,
    predict_hbm,
    factor_hbm,
    out_ref,
    gtau_ref,
    dev_ref,
    slot_ref,
    counts_ref,
    tau_ref,
    obs,
    predict,
    factor,
    req_send,
    req_recv,
    pass_recv,
    near_send,
    near_recv,
    raw_sib,
    raw_far,
    raw_relay,
    ret_send,
    ret_recv,
    seam_obs,
    seam_tgt,
    seam_tgt_in,
    seam_ret,
    seam_ret_in,
    held,
    held_ref,
    spread,
    partial,
    adj_slot,
    seam_slot,
    sq_send,
    sq_recv,
    local_sem,
    req_ss,
    req_rs,
    near_ss,
    near_rs,
    ret_ss,
    ret_rs,
    sq_ss,
    sq_rs,
    seam_ss,
    seam_rs,
    raw_ss,
    raw_rs,
    pass_ss,
    pass_rs,
):
    nbd, chans, width = obs.shape
    rows = nbd * chans
    part = cap * chans
    me = lax.axis_index("block")
    region = lax.axis_index("region")
    bf16, f32, i32 = jnp.bfloat16, jnp.float32, jnp.int32
    nt = (((1,), (1,)), ((), ()))

    def flip(d, bit):
        return d + bit - 2 * bit * lax.rem(d // bit, 2)

    sib = flip(me, 1)
    chip = me // 2
    own = [me, sib]
    beside = [flip(d, 2) for d in own]
    skip = [flip(d, 4) for d in own]
    mirror = [flip(d, 4) for d in beside]
    at_end = chip * (nblock // 2 - 1 - chip) == 0
    inner = jnp.logical_not(at_end)
    others = mirror + skip + beside + [sib]
    end = 1 - lax.rem((chip + 1) // 2, 2)
    kinds = [mirror, skip, beside, [sib]]
    third = [b + end * (s - b) for b, s in zip(beside, skip)]
    fourth = [s + end * (b - s) for b, s in zip(beside, skip)]

    def to_block(src, dst, ss, rs, peer):
        return pltpu.make_async_remote_copy(
            src_ref=src,
            dst_ref=dst,
            send_sem=ss,
            recv_sem=rs,
            device_id={"block": peer},
            device_id_type=MESH,
        )

    def to_region(src, dst, ss, rs, peer):
        return pltpu.make_async_remote_copy(
            src_ref=src,
            dst_ref=dst,
            send_sem=ss,
            recv_sem=rs,
            device_id={"region": peer},
            device_id_type=MESH,
        )

    def wait(ref, sem):
        pltpu.make_async_copy(ref, ref, sem).wait()

    regions = [lax.rem(region + step, nregion) for step in range(1, nregion)]

    small = [
        pltpu.make_async_copy(src, dst, local_sem.at[3 + i])
        for i, (src, dst) in enumerate(
            [(dev_hbm, dev_ref), (slot_hbm, slot_ref), (counts_hbm, counts_ref), (tau_hbm, tau_ref)]
        )
    ]
    for copy in small:
        copy.start()

    barrier = pltpu.get_barrier_semaphore()
    for peer in others:
        pl.semaphore_signal(barrier, inc=1, device_id={"block": peer}, device_id_type=MESH)
    for peer in regions:
        pl.semaphore_signal(barrier, inc=1, device_id={"region": peer}, device_id_type=MESH)
    load_obs = pltpu.make_async_copy(obs_hbm, obs, local_sem.at[0])
    load_predict = pltpu.make_async_copy(predict_hbm, predict, local_sem.at[1])
    load_factor = pltpu.make_async_copy(factor_hbm, factor, local_sem.at[2])
    load_obs.start()
    load_predict.start()
    load_factor.start()

    for copy in small:
        copy.wait()

    dest = [dev_ref[0, h] for h in range(nbd)]
    flat = []
    for h in range(nbd):
        rank = jnp.int32(0)
        for g in range(h):
            rank = rank + (dest[g] == dest[h]).astype(i32)
        flat.append(dest[h] * cap + rank)

    lane = lax.broadcasted_iota(i32, (nblock, part), 1)
    spot = lax.broadcasted_iota(i32, (nblock, part), 0) * cap + lane // chans
    wanted = jnp.full((nblock, part), -1, i32)
    for h in range(nbd):
        wanted = jnp.where(spot == flat[h], slot_ref[0, h] * chans + lane % chans, wanted)
    for d in range(nblock):
        req_send[d] = wanted[d : d + 1]

    block_lane = lax.broadcasted_iota(i32, (1, rows), 1)
    owner_of = block_lane // chans
    seam_row = jnp.zeros((1, rows), i32)
    for h in range(nbd):
        seam_row = jnp.where(owner_of == h, slot_ref[1, h], seam_row)
    seam_tgt[...] = seam_row * chans + block_lane % chans

    place_lane = lax.broadcasted_iota(i32, (1, LANES), 1)
    holder = jnp.full((1, LANES), nbd, i32)
    for h in range(nbd):
        holder = jnp.where(place_lane == flat[h], h, holder)
    held[...] = holder
    load_held = pltpu.make_async_copy(held, held_ref, local_sem.at[7])
    load_held.start()

    pl.semaphore_wait(barrier, nblock - 1 + nregion - 1)

    def request(peer, kind):
        return to_block(req_send.at[peer], req_recv.at[me], req_ss.at[0], req_rs.at[kind], peer)

    def asked(kind):
        wait(req_recv.at[pl.ds(0, len(kinds[kind]))], req_rs.at[kind])

    def request_pass(owner, peer):
        return to_block(req_send.at[owner], pass_recv.at[me], pass_ss.at[0], pass_rs.at[0], peer)

    for kind, peers in enumerate(kinds):
        for peer in peers:
            request(peer, kind).start()
    req_recv[me] = req_send[me]

    @pl.when(inner)
    def _():
        for owner, peer in zip(skip, beside):
            request_pass(owner, peer).start()


    to_sib = to_block(obs_hbm, raw_sib, raw_ss.at[0], raw_rs.at[0], sib)
    to_far = to_block(obs_hbm, raw_far, raw_ss.at[1], raw_rs.at[1], mirror[0])
    relay = to_block(raw_far, raw_relay, raw_ss.at[2], raw_rs.at[2], sib)

    down = lax.rem(region + 1, nregion)
    up = lax.rem(region + nregion - 1, nregion)
    seam_fwd = to_region(obs_hbm, seam_obs, seam_ss.at[0], seam_rs.at[0], down)
    seam_where = to_region(seam_tgt, seam_tgt_in, seam_ss.at[1], seam_rs.at[1], up)
    seam_bwd = to_region(seam_ret, seam_ret_in, seam_ss.at[2], seam_rs.at[2], up)
    has_prev = region > 0
    has_next = region < nregion - 1

    @pl.when(at_end)
    def _():
        to_far.start()

    @pl.when(has_next)
    def _():
        seam_fwd.start()

    @pl.when(has_prev)
    def _():
        seam_where.start()

    to_sib.start()

    @pl.when(inner)
    def _():
        raw_far[...] = jnp.zeros_like(raw_far)
        raw_relay[...] = jnp.zeros_like(raw_relay)

    load_obs.wait()
    pick_lane = lax.broadcasted_iota(i32, (part, rows), 1)

    def picked(row, source):
        row = jnp.broadcast_to(row, (LANES, part))
        column = jnp.concatenate([jnp.transpose(row)] * (rows // LANES), axis=1)
        mask = jnp.where(column == pick_lane, 1.0, 0.0).astype(bf16)
        got = jnp.dot(mask, source[...].reshape(rows, width), preferred_element_type=f32)
        return got.astype(bf16).reshape(cap, chans, width)

    def span(d):
        return pl.ds(d * cap, cap)

    def serve(peer, kind):
        return to_block(
            near_send.at[span(peer)],
            near_recv.at[span(me)],
            near_ss.at[0],
            near_rs.at[kind],
            peer,
        )

    def arrived(kind):
        wait(near_recv.at[pl.ds(0, 2 * cap)], near_rs.at[kind])

    def pass_on(j):
        return to_block(
            near_send.at[span(skip[j])],
            near_recv.at[span(mirror[0])],
            near_ss.at[0],
            near_rs.at[1],
            beside[j],
        )

    def answer(kind):
        asked(kind)
        for peer in kinds[kind]:
            near_send[span(peer)] = picked(req_recv[peer], obs)
            serve(peer, kind).start()

    @pl.when(inner)
    def _():
        for kind in range(3):
            answer(kind)

    @pl.when(at_end)
    def _():
        answer(2)
        for peer in mirror:
            near_recv[span(peer)] = jnp.zeros((cap, chans, width), bf16)
        asked(1)
        asked(0)

    asked(3)

    def build(pair):
        wanted_row = jnp.concatenate([req_recv[pair * 2 + i] for i in range(2)], axis=1)
        spread[pair] = jnp.where(
            wanted_row == lax.broadcasted_iota(i32, (rows, 2 * part), 0), 1.0, 0.0
        ).astype(bf16)

    for pair in range(nblock // 2):
        build(pair)
    load_held.wait()

    eye = lax.broadcasted_iota(i32, (chans, LANES), 0) == lax.broadcasted_iota(
        i32, (chans, LANES), 1
    )
    tau_row = jnp.concatenate([tau_ref[...], jnp.zeros((1, LANES - chans), f32)], axis=1)
    tau_col = jnp.sum(jnp.where(eye, tau_row, 0.0), axis=1, keepdims=True)
    count = counts_ref[0]

    @pl.when(has_prev)
    def _():
        seam_fwd.wait_recv()

    @pl.when(jnp.logical_not(has_prev))
    def _():
        seam_obs[...] = jnp.zeros_like(seam_obs)

    load_predict.wait()
    for g in range(nbd):
        partial[g] = obs[g].astype(f32) - jnp.dot(
            seam_obs[slot_ref[1, g]], predict[g, 1], preferred_element_type=f32
        )
    load_factor.wait()

    def give(peer, kind):
        return to_block(ret_send.at[peer], ret_recv.at[me], ret_ss.at[0], ret_rs.at[kind], peer)

    squares = [jnp.zeros((chans, width), f32)]

    def process(peers, near_of, between=None):
        at = [peer * cap + k for peer in peers for k in range(cap)]
        every = range(len(at))
        who = [held_ref[0, i] for i in at]
        block = [jnp.minimum(w, nbd - 1) for w in who]
        live = [(w < count).astype(f32) for w in who]
        near = [near_of(i // cap, at[i], block[i]) for i in every]
        err = [
            (
                partial[block[i]]
                - jnp.dot(near[i], predict[block[i], 0], preferred_element_type=f32)
            ).astype(bf16)
            for i in every
        ]
        white = [jnp.dot(err[i], factor[block[i]], preferred_element_type=f32) for i in every]
        for i in every:
            squares[0] = squares[0] + live[i] * white[i] * white[i]
        if between is not None:
            between()
        weighted = [(live[i] * tau_col * white[i]).astype(bf16) for i in every]
        adj = [
            lax.dot_general(weighted[i], factor[block[i]], nt, preferred_element_type=f32)
            for i in every
        ]
        for i in every:
            adj_slot[at[i]] = adj[i]
        both = [
            lax.dot_general(
                adj[i].astype(bf16),
                predict[block[i]].reshape(2 * width, width),
                nt,
                preferred_element_type=f32,
            ).astype(bf16)
            for i in every
        ]
        for i in every:
            seam_slot[at[i]] = both[i][:, width:]
        return [both[i][:, :width] for i in every]

    def give_back(kind, peers, back):
        for j, peer in enumerate(peers):
            for k in range(cap):
                ret_send[peer, k * chans : (k + 1) * chans] = back[j * cap + k]
            give(peer, kind).start()

    to_sib.wait_recv()
    homes = [obs, raw_sib]
    back = process(own, lambda j, i, h: homes[j][slot_ref[0, h]])
    for k in range(cap):
        ret_recv[me, k * chans : (k + 1) * chans] = back[k]
    give_back(3, [sib], back[cap:])

    @pl.when(at_end)
    def _():
        to_far.wait_recv()
        relay.start()
        wait(pass_recv.at[pl.ds(0, 2)], pass_rs.at[0])
        for j, peer in enumerate(beside):
            near_send[span(skip[j])] = picked(pass_recv[peer], raw_far)
            pass_on(j).start()

    @pl.when(at_end)
    def _():
        relay.wait_recv()

    @pl.when(inner)
    def _():
        arrived(0)

    raws = [raw_far, raw_relay]
    give_back(
        0,
        mirror,
        process(
            mirror,
            lambda j, i, h: jnp.where(at_end, raws[j][slot_ref[0, h]], near_recv[i]),
        ),
    )

    arrived(2 - end)
    give_back(2 - end, third, process(third, lambda j, i, h: near_recv[i]))

    live_lane = lax.broadcasted_iota(i32, (1, LANES), 1) == chans

    everyone = [(r, b) for r in regions for b in others + [me]] + [(region, b) for b in others]
    mine = region * nblock + me

    def share(r, b):
        return pltpu.make_async_remote_copy(
            src_ref=sq_send,
            dst_ref=sq_recv.at[mine],
            send_sem=sq_ss.at[0],
            recv_sem=sq_rs.at[0],
            device_id={"region": r, "block": b},
            device_id_type=MESH,
        )

    sums_in = sq_recv.at[pl.ds(0, len(everyone))]

    def share_all():
        sums = jnp.sum(
            jnp.where(eye, jnp.sum(squares[0], axis=1, keepdims=True), 0.0), axis=0, keepdims=True
        )
        sums = sums + jnp.where(live_lane, jnp.minimum(count, nbd).astype(f32), 0.0)
        sq_send[...] = sums
        for r, b in everyone:
            share(r, b).start()
        sq_recv[mine] = sums

    arrived(1 + end)
    give_back(1 + end, fourth, process(fourth, lambda j, i, h: near_recv[i], share_all))

    @pl.when(has_prev)
    def _():
        for g in range(nbd):
            seam_ret[g] = seam_slot[flat[g]]
        seam_bwd.start()

    for g in range(nbd):
        out_ref[g] = adj_slot[flat[g]]

    def add(pair):
        blocks_back = ret_recv[pl.ds(pair * 2, 2)].reshape(2 * part, width)
        got = jnp.dot(spread[pair], blocks_back, preferred_element_type=f32)
        out_ref[...] = out_ref[...] - got.reshape(nbd, chans, width)

    def take(kind):
        wait(ret_recv.at[pl.ds(0, len(kinds[kind]))], ret_rs.at[kind])

    wait(req_send.at[pl.ds(0, len(others))], req_ss.at[0])

    @pl.when(inner)
    def _():
        wait(near_send.at[pl.ds(0, 6 * cap)], near_ss.at[0])
        wait(pass_recv.at[pl.ds(0, 2)], pass_ss.at[0])

    to_sib.wait_send()

    @pl.when(at_end)
    def _():
        to_far.wait_send()
        relay.wait_send()
        wait(near_send.at[pl.ds(0, 4 * cap)], near_ss.at[0])

    @pl.when(has_next)
    def _():
        seam_fwd.wait_send()

    @pl.when(has_prev)
    def _():
        seam_where.wait_send()

    take(3)
    add(chip)
    take(2)
    add(beside[0] // 2)

    take(0)
    add(mirror[0] // 2)

    @pl.when(has_next)
    def _():
        seam_where.wait_recv()
        mask = jnp.where(
            seam_tgt_in[...] == lax.broadcasted_iota(i32, (rows, rows), 0), 1.0, 0.0
        ).astype(bf16)
        seam_bwd.wait_recv()
        got = jnp.dot(mask, seam_ret_in[...].reshape(rows, width), preferred_element_type=f32)
        out_ref[...] = out_ref[...] - got.reshape(nbd, chans, width)

    take(1)
    add(skip[0] // 2)

    wait(sums_in, sq_rs.at[0])
    total = sq_recv[0]
    for d in range(1, nregion * nblock):
        total = total + sq_recv[d]
    total_live = jnp.sum(jnp.where(live_lane, total, 0.0), axis=1, keepdims=True)
    blocks = nbd * nblock * nregion
    gtau_ref[...] = (
        0.5 * total[:, :chans] - 0.5 * width * total_live / tau_ref[...]
    ) / (blocks * width)

    wait(ret_send.at[pl.ds(0, len(others))], ret_ss.at[0])
    wait(sums_in, sq_ss.at[0])

    @pl.when(has_prev)
    def _():
        seam_bwd.wait_send()


def write_out(obs_ref, tau_ref, obs_hbm, tau_hbm, sem):
    copies = [
        pltpu.make_async_copy(src, dst, sem.at[i])
        for i, (src, dst) in enumerate([(obs_ref, obs_hbm), (tau_ref, tau_hbm)])
    ]
    for copy in copies:
        copy.start()
    for copy in copies:
        copy.wait()


def shards(obs, predict, factor, tau, nbr_dev, nbr_slot, counts):
    nbd, chans, width = obs.shape
    nblock = lax.axis_size("block")
    nregion = lax.axis_size("region")
    cap = max(2, 2 * nbd // nblock)
    rows = nbd * chans
    part = cap * chans
    lanes = -(-part // LANES) * LANES
    group = 2 if nblock % 2 == 0 and part % LANES == 0 else 1
    line = nblock == 8 and part == LANES
    bf16, f32, i32 = jnp.bfloat16, jnp.float32, jnp.int32
    vmem = pl.BlockSpec(memory_space=pltpu.VMEM)
    hbm = pl.BlockSpec(memory_space=pltpu.HBM)
    dma = pltpu.SemaphoreType.DMA
    blocks = pltpu.VMEM((nbd, chans, width), bf16)
    slots = pltpu.VMEM((nblock * cap, chans, width), bf16)
    inputs = [
        pltpu.SMEM((1, nbd), i32),
        pltpu.SMEM((2, nbd), i32),
        pltpu.SMEM((1,), i32),
        pltpu.VMEM((1, chans), f32),
        blocks,
        pltpu.VMEM((nbd, 2, width, width), bf16),
        pltpu.VMEM((nbd, width, width), bf16),
        pltpu.VMEM((nblock, 1, lanes), i32),
        pltpu.VMEM((nblock, 1, lanes), i32),
        slots,
        slots,
    ]
    middle = [
        pltpu.VMEM((nblock, part, width), bf16),
        pltpu.VMEM((nblock, part, width), bf16),
        blocks,
        pltpu.VMEM((1, rows), i32),
        pltpu.VMEM((1, rows), i32),
        blocks,
        blocks,
        pltpu.VMEM((1, LANES), i32),
        pltpu.SMEM((1, LANES), i32),
        pltpu.VMEM((nblock // group, rows, group * part), bf16),
        pltpu.VMEM((nbd, chans, width), f32),
    ]
    sums = [
        pltpu.VMEM((1, LANES), f32),
        pltpu.VMEM((nblock, 1, LANES), f32),
        pltpu.VMEM((1, LANES), f32),
        pltpu.VMEM((nregion, 1, LANES), f32),
        dma((8,)),
    ]
    sems = [dma((nblock,))] * 8 + [dma((nregion,))] * 2 + [dma((3,))] * 2
    if line:
        body = line_kernel
        scratch = inputs[:9] + inputs[8:] + [blocks] * 3 + middle
        scratch += [pltpu.VMEM((nblock * cap, chans, width), f32), slots, sums[0]]
        scratch += [pltpu.VMEM((nregion * nblock, 1, LANES), f32), sums[-1]]
        scratch += [dma((n,)) for n in (1, 4, 1, 3, 1, 4, 1, 1, 3, 3, 3, 3, 1, 1)]
    else:
        body = kernel
        scratch = inputs + middle
        scratch += [pltpu.VMEM((nbd + 1, chans, width), bf16), blocks] + sums + sems
    grad_obs, grad_tau = pl.pallas_call(
        functools.partial(body, nblock, nregion, cap),
        out_shape=(
            jax.ShapeDtypeStruct((nbd, chans, width), f32),
            jax.ShapeDtypeStruct((1, chans), f32),
        ),
        in_specs=[hbm] * 7,
        out_specs=(vmem, vmem),
        scratch_shapes=scratch,
        compiler_params=pltpu.CompilerParams(
            collective_id=0, has_side_effects=True, vmem_limit_bytes=48 << 20
        ),
        name="vecchia",
    )(
        *(
            value if value is counts else pltpu.with_memory_space_constraint(value, pltpu.HBM)
            for value in (nbr_dev.T, nbr_slot.T, counts, tau.reshape(1, chans), obs, predict, factor)
        )
    )
    grad_obs, grad_tau = pl.pallas_call(
        write_out,
        out_shape=(
            jax.ShapeDtypeStruct((nbd, chans, width), f32),
            jax.ShapeDtypeStruct((1, chans), f32),
        ),
        in_specs=[vmem, vmem],
        out_specs=(hbm, hbm),
        scratch_shapes=[dma((2,))],
        name="write_out",
    )(*(pltpu.with_memory_space_constraint(x, pltpu.VMEM) for x in (grad_obs, grad_tau)))
    return grad_obs, grad_tau.reshape(chans)


def solution(mesh):
    in_specs = (
        P(("region", "block"), None, None),
        P(("region", "block"), None, None, None),
        P(("region", "block"), None, None),
        P(),
        P(("region", "block"), None),
        P(("region", "block"), None),
        P(("region", "block")),
    )
    out_specs = (P(("region", "block"), None, None), P())
    return jax.shard_map(shards, mesh=mesh, in_specs=in_specs, out_specs=out_specs, check_vma=False)
```

```python
import functools

import jax
import jax.numpy as jnp
from jax import lax
from jax.experimental import pallas as pl
from jax.experimental.pallas import tpu as pltpu
from jax.sharding import PartitionSpec as P

MESH = pl.DeviceIdType.MESH
LANES = 128


def kernel(
    nblock,
    nregion,
    cap,
    dev_hbm,
    slot_hbm,
    counts_hbm,
    tau_hbm,
    obs_hbm,
    predict_hbm,
    factor_hbm,
    out_ref,
    gtau_ref,
    dev_ref,
    slot_ref,
    counts_ref,
    tau_ref,
    obs,
    predict,
    factor,
    req_send,
    req_recv,
    near_send,
    near_recv,
    ret_send,
    ret_recv,
    seam_obs,
    seam_tgt,
    seam_tgt_in,
    seam_ret,
    seam_ret_in,
    held,
    held_ref,
    spread,
    partial,
    back,
    adjoint,
    sq_send,
    sq_recv,
    rg_send,
    rg_recv,
    local_sem,
    req_ss,
    req_rs,
    near_ss,
    near_rs,
    ret_ss,
    ret_rs,
    sq_ss,
    sq_rs,
    rg_ss,
    rg_rs,
    seam_ss,
    seam_rs,
):
    nbd, chans, width = obs.shape
    rows = nbd * chans
    part = cap * chans
    lanes = req_send.shape[2]
    group = 2 if nblock % 2 == 0 and part % LANES == 0 else 1
    me = lax.axis_index("block")
    region = lax.axis_index("region")
    bf16, f32, i32 = jnp.bfloat16, jnp.float32, jnp.int32

    half = me // (nblock // 2)

    def farthest(turn):
        below = nblock - 1 - turn - (me + turn + 1) // nblock
        above = turn + (turn - me + nblock) // nblock
        return below + half * (above - below)

    def each_peer(body, nearest=False):
        def visit(turn):
            body(farthest(nblock - 2 - turn if nearest else turn))

        if nblock <= 8:
            for turn in range(nblock - 1):
                visit(turn)
        else:

            def run(turn, carry):
                visit(turn)
                return carry

            lax.fori_loop(0, nblock - 1, run, 0)

    def each_region(body):
        for step in range(1, nregion):
            body(lax.rem(region + step, nregion))

    def to_block(src, dst, ss, rs, peer):
        return pltpu.make_async_remote_copy(
            src_ref=src,
            dst_ref=dst,
            send_sem=ss,
            recv_sem=rs,
            device_id={"block": peer},
            device_id_type=MESH,
        )

    def to_region(src, dst, ss, rs, peer):
        return pltpu.make_async_remote_copy(
            src_ref=src,
            dst_ref=dst,
            send_sem=ss,
            recv_sem=rs,
            device_id={"region": peer},
            device_id_type=MESH,
        )

    small = [
        pltpu.make_async_copy(src, dst, local_sem.at[3 + i])
        for i, (src, dst) in enumerate(
            [(dev_hbm, dev_ref), (slot_hbm, slot_ref), (counts_hbm, counts_ref), (tau_hbm, tau_ref)]
        )
    ]
    for copy in small:
        copy.start()

    barrier = pltpu.get_barrier_semaphore()
    each_peer(
        lambda peer: pl.semaphore_signal(
            barrier, inc=1, device_id={"block": peer}, device_id_type=MESH
        )
    )
    each_region(
        lambda peer: pl.semaphore_signal(
            barrier, inc=1, device_id={"region": peer}, device_id_type=MESH
        )
    )
    load_obs = pltpu.make_async_copy(obs_hbm, obs, local_sem.at[0])
    load_predict = pltpu.make_async_copy(predict_hbm, predict, local_sem.at[1])
    load_factor = pltpu.make_async_copy(factor_hbm, factor, local_sem.at[2])
    load_obs.start()
    load_predict.start()
    load_factor.start()

    for copy in small:
        copy.wait()

    dest = [dev_ref[0, h] for h in range(nbd)]
    flat = []
    for h in range(nbd):
        rank = jnp.int32(0)
        for g in range(h):
            rank = rank + (dest[g] == dest[h]).astype(i32)
        flat.append(dest[h] * cap + rank)

    lane = lax.broadcasted_iota(i32, (nblock, lanes), 1)
    spot = lax.broadcasted_iota(i32, (nblock, lanes), 0) * cap + lane // chans
    spot = jnp.where(lane < part, spot, -1)
    wanted = jnp.full((nblock, lanes), -1, i32)
    for h in range(nbd):
        wanted = jnp.where(spot == flat[h], slot_ref[0, h] * chans + lane % chans, wanted)
    for d in range(nblock):
        req_send[d] = wanted[d : d + 1]

    block_lane = lax.broadcasted_iota(i32, (1, rows), 1)
    owner_of = block_lane // chans
    seam_row = jnp.zeros((1, rows), i32)
    for h in range(nbd):
        seam_row = jnp.where(owner_of == h, slot_ref[1, h], seam_row)
    seam_tgt[...] = seam_row * chans + block_lane % chans

    place_lane = lax.broadcasted_iota(i32, (1, LANES), 1)
    holder = jnp.full((1, LANES), nbd, i32)
    for h in range(nbd):
        holder = jnp.where(place_lane == flat[h], h, holder)
    held[...] = holder
    load_held = pltpu.make_async_copy(held, held_ref, local_sem.at[7])
    load_held.start()
    back[nbd] = jnp.zeros((chans, width), bf16)

    pl.semaphore_wait(barrier, nblock - 1 + nregion - 1)

    def request(peer, mine):
        return to_block(req_send.at[peer], req_recv.at[mine], req_ss.at[peer], req_rs.at[mine], peer)

    each_peer(lambda peer: request(peer, me).start())
    req_recv[me] = req_send[me]

    down = lax.rem(region + 1, nregion)
    up = lax.rem(region + nregion - 1, nregion)
    seam_fwd = to_region(obs_hbm, seam_obs, seam_ss.at[0], seam_rs.at[0], down)
    seam_where = to_region(seam_tgt, seam_tgt_in, seam_ss.at[1], seam_rs.at[1], up)
    seam_bwd = to_region(seam_ret, seam_ret_in, seam_ss.at[2], seam_rs.at[2], up)
    has_prev = region > 0
    has_next = region < nregion - 1

    @pl.when(has_next)
    def _():
        seam_fwd.start()

    @pl.when(has_prev)
    def _():
        seam_where.start()

    load_obs.wait()
    pick_lane = lax.broadcasted_iota(i32, (part, rows), 1)

    def picked(peer):
        row = jnp.broadcast_to(req_recv[peer], (LANES, lanes))
        column = jnp.transpose(row)[:part]
        column = jnp.concatenate([column] * (rows // LANES), axis=1)
        mask = jnp.where(column == pick_lane, 1.0, 0.0).astype(bf16)
        got = jnp.dot(mask, obs[...].reshape(rows, width), preferred_element_type=f32)
        return got.astype(bf16).reshape(cap, chans, width)

    def span(d):
        return pl.ds(d * cap, cap)

    def serve(peer, mine):
        return to_block(
            near_send.at[span(peer)],
            near_recv.at[span(mine)],
            near_ss.at[peer],
            near_rs.at[mine],
            peer,
        )

    def put(peer):
        near_send[span(peer)] = picked(peer)
        serve(peer, me).start()

    def answer(peer):
        request(me, peer).wait_recv()
        put(peer)

    each_peer(answer, nearest=True)
    near_recv[span(me)] = picked(me)

    def build(pair):
        wanted_row = jnp.concatenate(
            [req_recv[pair * group + i][:, :part] for i in range(group)], axis=1
        )
        spread[pair] = jnp.where(
            wanted_row == lax.broadcasted_iota(i32, (rows, group * part), 0), 1.0, 0.0
        ).astype(bf16)

    for pair in range(nblock // group):
        build(pair)
    load_held.wait()

    @pl.when(has_prev)
    def _():
        seam_fwd.wait_recv()

    @pl.when(jnp.logical_not(has_prev))
    def _():
        seam_obs[...] = jnp.zeros_like(seam_obs)

    load_predict.wait()
    for g in range(nbd):
        partial[g] = obs[g].astype(f32) - jnp.dot(
            seam_obs[slot_ref[1, g]], predict[g, 1], preferred_element_type=f32
        )
    load_factor.wait()

    eye = lax.broadcasted_iota(i32, (chans, LANES), 0) == lax.broadcasted_iota(
        i32, (chans, LANES), 1
    )
    tau_row = jnp.concatenate([tau_ref[...], jnp.zeros((1, LANES - chans), f32)], axis=1)
    tau_col = jnp.sum(jnp.where(eye, tau_row, 0.0), axis=1, keepdims=True)
    count = counts_ref[0]

    each_peer(lambda peer: serve(me, peer).wait_recv(), nearest=True)

    nt = (((1,), (1,)), ((), ()))
    every = range(nbd)
    err = [
        (
            partial[g]
            - jnp.dot(near_recv[flat[g]], predict[g, 0], preferred_element_type=f32)
        ).astype(bf16)
        for g in every
    ]
    white = [jnp.dot(err[g], factor[g], preferred_element_type=f32) for g in every]
    live = [(g < count).astype(f32) for g in every]
    weighted = [(live[g] * tau_col * white[g]).astype(bf16) for g in every]
    squares = live[0] * white[0] * white[0]
    for g in range(1, nbd):
        squares = squares + live[g] * white[g] * white[g]
    live_lane = lax.broadcasted_iota(i32, (1, LANES), 1) == chans
    sums = jnp.sum(
        jnp.where(eye, jnp.sum(squares, axis=1, keepdims=True), 0.0), axis=0, keepdims=True
    )
    sums = sums + jnp.where(live_lane, jnp.minimum(count, nbd).astype(f32), 0.0)
    sq_send[...] = sums

    def share(peer, mine):
        return to_block(sq_send, sq_recv.at[mine], sq_ss.at[peer], sq_rs.at[mine], peer)

    each_peer(lambda peer: share(peer, me).start())
    sq_recv[me] = sums

    adj = [lax.dot_general(weighted[g], factor[g], nt, preferred_element_type=f32) for g in every]
    for g in every:
        out_ref[g] = adj[g]
        adjoint[g] = adj[g].astype(bf16)

    for g in every:
        back[g] = lax.dot_general(
            adjoint[g], predict[g, 0], nt, preferred_element_type=f32
        ).astype(bf16)

    def pack(dst, peer):
        for k in range(cap):
            dst[k * chans : (k + 1) * chans] = back[held_ref[0, peer * cap + k]]

    def give(peer, mine):
        return to_block(ret_send.at[peer], ret_recv.at[mine], ret_ss.at[peer], ret_rs.at[mine], peer)

    def give_back(peer):
        pack(ret_send.at[peer], peer)
        give(peer, me).start()

    each_peer(give_back)
    pack(ret_recv.at[me], me)

    @pl.when(has_prev)
    def _():
        for g in range(nbd):
            seam_ret[g] = lax.dot_general(
                adjoint[g], predict[g, 1], nt, preferred_element_type=f32
            ).astype(bf16)
        seam_bwd.start()

    each_peer(lambda peer: share(me, peer).wait_recv(), nearest=True)
    line = sq_recv[0]
    for d in range(1, nblock):
        line = line + sq_recv[d]
    rg_send[...] = line

    def share_region(peer, mine):
        return to_region(rg_send, rg_recv.at[mine], rg_ss.at[peer], rg_rs.at[mine], peer)

    each_region(lambda peer: share_region(peer, region).start())
    rg_recv[region] = line

    @pl.when(has_next)
    def _():
        seam_where_in = to_region(seam_tgt, seam_tgt_in, seam_ss.at[1], seam_rs.at[1], up)
        seam_where_in.wait_recv()
        mask = jnp.where(
            seam_tgt_in[...] == lax.broadcasted_iota(i32, (rows, rows), 0), 1.0, 0.0
        ).astype(bf16)
        seam_bwd.wait_recv()
        got = jnp.dot(mask, seam_ret_in[...].reshape(rows, width), preferred_element_type=f32)
        out_ref[...] = out_ref[...] - got.reshape(nbd, chans, width)

    def add(pair):
        blocks_back = ret_recv[pl.ds(pair * group, group)].reshape(group * part, width)
        got = jnp.dot(spread[pair], blocks_back, preferred_element_type=f32)
        out_ref[...] = out_ref[...] - got.reshape(nbd, chans, width)

    each_peer(lambda peer: give(me, peer).wait_recv(), nearest=True)
    for pair in range(nblock // group):
        add(pair)

    each_region(lambda peer: share_region(region, peer).wait_recv())
    total = rg_recv[0]
    for r in range(1, nregion):
        total = total + rg_recv[r]
    total_live = jnp.sum(jnp.where(live_lane, total, 0.0), axis=1, keepdims=True)
    blocks = nbd * nblock * nregion
    gtau_ref[...] = (
        0.5 * total[:, :chans] - 0.5 * width * total_live / tau_ref[...]
    ) / (blocks * width)

    def sent(peer):
        request(peer, me).wait_send()
        serve(peer, me).wait_send()
        give(peer, me).wait_send()
        share(peer, me).wait_send()

    each_peer(sent)
    each_region(lambda peer: share_region(peer, region).wait_send())

    @pl.when(has_next)
    def _():
        seam_fwd.wait_send()

    @pl.when(has_prev)
    def _():
        seam_where.wait_send()
        seam_bwd.wait_send()


def line_kernel(
    nblock,
    nregion,
    cap,
    dev_hbm,
    slot_hbm,
    counts_hbm,
    tau_hbm,
    obs_hbm,
    predict_hbm,
    factor_hbm,
    out_ref,
    gtau_ref,
    dev_ref,
    slot_ref,
    counts_ref,
    tau_ref,
    obs,
    predict,
    factor,
    req_send,
    req_recv,
    pass_recv,
    near_send,
    near_recv,
    raw_sib,
    raw_far,
    ret_send,
    ret_recv,
    seam_obs,
    seam_tgt,
    seam_tgt_in,
    seam_ret,
    seam_ret_in,
    held,
    held_ref,
    spread,
    partial,
    adj_slot,
    seam_slot,
    sq_send,
    sq_recv,
    local_sem,
    req_ss,
    req_rs,
    near_ss,
    near_rs,
    ret_ss,
    ret_rs,
    sq_ss,
    sq_rs,
    seam_ss,
    seam_rs,
    raw_ss,
    raw_rs,
    pass_ss,
    pass_rs,
):
    nbd, chans, width = obs.shape
    rows = nbd * chans
    part = cap * chans
    me = lax.axis_index("block")
    region = lax.axis_index("region")
    bf16, f32, i32 = jnp.bfloat16, jnp.float32, jnp.int32
    nt = (((1,), (1,)), ((), ()))

    def flip(d, bit):
        return d + bit - 2 * bit * lax.rem(d // bit, 2)

    sib = flip(me, 1)
    chip = me // 2
    own = [me, sib]
    beside = [flip(d, 2) for d in own]
    skip = [flip(d, 4) for d in own]
    mirror = [flip(d, 4) for d in beside]
    at_end = chip * (nblock // 2 - 1 - chip) == 0
    inner = jnp.logical_not(at_end)
    others = mirror + skip + beside + [sib]
    end = 1 - lax.rem((chip + 1) // 2, 2)
    kinds = [mirror, skip, beside, [sib]]
    core = lax.rem(me, 2)
    lead = jnp.logical_and(at_end, core == 1)
    tail = jnp.logical_and(at_end, core == 0)
    m0, s0, b0 = [2 * (d[0] // 2) for d in (mirror, skip, beside)]
    m1, s1, b1 = m0 + 1, s0 + 1, b0 + 1

    def by_place(inside, outside):
        return [tuple(i + end * (o - i) for i, o in zip(*two)) for two in zip(inside, outside)]


    def to_block(src, dst, ss, rs, peer):
        return pltpu.make_async_remote_copy(
            src_ref=src,
            dst_ref=dst,
            send_sem=ss,
            recv_sem=rs,
            device_id={"block": peer},
            device_id_type=MESH,
        )

    def to_region(src, dst, ss, rs, peer):
        return pltpu.make_async_remote_copy(
            src_ref=src,
            dst_ref=dst,
            send_sem=ss,
            recv_sem=rs,
            device_id={"region": peer},
            device_id_type=MESH,
        )

    def wait(ref, sem):
        pltpu.make_async_copy(ref, ref, sem).wait()

    regions = [lax.rem(region + step, nregion) for step in range(1, nregion)]

    small = [
        pltpu.make_async_copy(src, dst, local_sem.at[3 + i])
        for i, (src, dst) in enumerate(
            [(dev_hbm, dev_ref), (slot_hbm, slot_ref), (counts_hbm, counts_ref), (tau_hbm, tau_ref)]
        )
    ]
    for copy in small:
        copy.start()

    barrier = pltpu.get_barrier_semaphore()
    for peer in others:
        pl.semaphore_signal(barrier, inc=1, device_id={"block": peer}, device_id_type=MESH)
    for peer in regions:
        pl.semaphore_signal(barrier, inc=1, device_id={"region": peer}, device_id_type=MESH)
    load_obs = pltpu.make_async_copy(obs_hbm, obs, local_sem.at[0])
    load_predict = pltpu.make_async_copy(predict_hbm, predict, local_sem.at[1])
    load_factor = pltpu.make_async_copy(factor_hbm, factor, local_sem.at[2])
    load_obs.start()
    load_predict.start()
    load_factor.start()

    for copy in small:
        copy.wait()

    dest = [dev_ref[0, h] for h in range(nbd)]
    flat = []
    for h in range(nbd):
        rank = jnp.int32(0)
        for g in range(h):
            rank = rank + (dest[g] == dest[h]).astype(i32)
        flat.append(dest[h] * cap + rank)

    lane = lax.broadcasted_iota(i32, (nblock, part), 1)
    spot = lax.broadcasted_iota(i32, (nblock, part), 0) * cap + lane // chans
    wanted = jnp.full((nblock, part), -1, i32)
    for h in range(nbd):
        wanted = jnp.where(spot == flat[h], slot_ref[0, h] * chans + lane % chans, wanted)
    for d in range(nblock):
        req_send[d] = wanted[d : d + 1]

    block_lane = lax.broadcasted_iota(i32, (1, rows), 1)
    owner_of = block_lane // chans
    seam_row = jnp.zeros((1, rows), i32)
    for h in range(nbd):
        seam_row = jnp.where(owner_of == h, slot_ref[1, h], seam_row)
    seam_tgt[...] = seam_row * chans + block_lane % chans

    place_lane = lax.broadcasted_iota(i32, (1, LANES), 1)
    holder = jnp.full((1, LANES), nbd, i32)
    for h in range(nbd):
        holder = jnp.where(place_lane == flat[h], h, holder)
    held[...] = holder
    load_held = pltpu.make_async_copy(held, held_ref, local_sem.at[7])
    load_held.start()

    pl.semaphore_wait(barrier, nblock - 1 + nregion - 1)

    def request(peer, kind):
        return to_block(req_send.at[peer], req_recv.at[me], req_ss.at[0], req_rs.at[kind], peer)

    def asked(kind):
        wait(req_recv.at[pl.ds(0, len(kinds[kind]))], req_rs.at[kind])

    def request_pass(owner, peer):
        return to_block(req_send.at[owner], pass_recv.at[me], pass_ss.at[0], pass_rs.at[0], peer)

    for kind, peers in enumerate(kinds):
        for peer in peers:
            request(peer, kind).start()
    req_recv[me] = req_send[me]

    @pl.when(inner)
    def _():
        request_pass(s1, b1).start()


    to_sib = to_block(obs_hbm, raw_sib, raw_ss.at[0], raw_rs.at[0], sib)
    to_far = to_block(obs_hbm, raw_far, raw_ss.at[1], raw_rs.at[1], mirror[0])
    relay = to_block(raw_far, raw_far, raw_ss.at[2], raw_rs.at[2], sib)

    down = lax.rem(region + 1, nregion)
    up = lax.rem(region + nregion - 1, nregion)
    seam_fwd = to_region(obs_hbm, seam_obs, seam_ss.at[0], seam_rs.at[0], down)
    seam_where = to_region(seam_tgt, seam_tgt_in, seam_ss.at[1], seam_rs.at[1], up)
    seam_bwd = to_region(seam_ret, seam_ret_in, seam_ss.at[2], seam_rs.at[2], up)
    has_prev = region > 0
    has_next = region < nregion - 1

    @pl.when(lead)
    def _():
        to_far.start()

    @pl.when(has_next)
    def _():
        seam_fwd.start()

    @pl.when(has_prev)
    def _():
        seam_where.start()

    to_sib.start()

    @pl.when(inner)
    def _():
        raw_far[...] = jnp.zeros_like(raw_far)

    load_obs.wait()
    pick_lane = lax.broadcasted_iota(i32, (part, rows), 1)

    def picked(row, source):
        row = jnp.broadcast_to(row, (LANES, part))
        column = jnp.concatenate([jnp.transpose(row)] * (rows // LANES), axis=1)
        mask = jnp.where(column == pick_lane, 1.0, 0.0).astype(bf16)
        got = jnp.dot(mask, source[...].reshape(rows, width), preferred_element_type=f32)
        return got.astype(bf16).reshape(cap, chans, width)

    def span(d):
        return pl.ds(d * cap, cap)

    def serve(peer):
        return to_block(
            near_send.at[span(peer)],
            near_recv.at[span(me)],
            near_ss.at[0],
            near_rs.at[me],
            peer,
        )

    def arrived(owner):
        wait(near_recv.at[span(owner)], near_rs.at[owner])

    def pass_on(j):
        return to_block(
            near_send.at[span(skip[j])],
            near_recv.at[span(mirror[0])],
            near_ss.at[0],
            near_rs.at[mirror[0]],
            beside[j],
        )

    def answer(kind):
        asked(kind)
        for peer in kinds[kind]:
            near_send[span(peer)] = picked(req_recv[peer], obs)
            serve(peer).start()

    @pl.when(inner)
    def _():
        for kind in (0, 2, 1):
            answer(kind)

    @pl.when(tail)
    def _():
        for kind in (1, 2, 0):
            answer(kind)

    @pl.when(lead)
    def _():
        answer(2)
        asked(1)
        asked(0)

    @pl.when(at_end)
    def _():
        near_recv[span(m1)] = jnp.zeros((cap, chans, width), bf16)

    asked(3)

    def build(pair):
        wanted_row = jnp.concatenate([req_recv[pair * 2 + i] for i in range(2)], axis=1)
        spread[pair] = jnp.where(
            wanted_row == lax.broadcasted_iota(i32, (rows, 2 * part), 0), 1.0, 0.0
        ).astype(bf16)

    for pair in range(nblock // 2):
        build(pair)
    load_held.wait()

    eye = lax.broadcasted_iota(i32, (chans, LANES), 0) == lax.broadcasted_iota(
        i32, (chans, LANES), 1
    )
    tau_row = jnp.concatenate([tau_ref[...], jnp.zeros((1, LANES - chans), f32)], axis=1)
    tau_col = jnp.sum(jnp.where(eye, tau_row, 0.0), axis=1, keepdims=True)
    count = counts_ref[0]

    @pl.when(has_prev)
    def _():
        seam_fwd.wait_recv()

    @pl.when(jnp.logical_not(has_prev))
    def _():
        seam_obs[...] = jnp.zeros_like(seam_obs)

    load_predict.wait()
    for g in range(nbd):
        partial[g] = obs[g].astype(f32) - jnp.dot(
            seam_obs[slot_ref[1, g]], predict[g, 1], preferred_element_type=f32
        )
    load_factor.wait()

    def give(peer, kind):
        return to_block(ret_send.at[peer], ret_recv.at[me], ret_ss.at[0], ret_rs.at[kind], peer)

    squares = [jnp.zeros((chans, width), f32)]

    def process(peers, near_of, between=None):
        at = [peer * cap + k for peer in peers for k in range(cap)]
        every = range(len(at))
        who = [held_ref[0, i] for i in at]
        block = [jnp.minimum(w, nbd - 1) for w in who]
        live = [(w < count).astype(f32) for w in who]
        near = [near_of(i // cap, at[i], block[i]) for i in every]
        err = [
            (
                partial[block[i]]
                - jnp.dot(near[i], predict[block[i], 0], preferred_element_type=f32)
            ).astype(bf16)
            for i in every
        ]
        white = [jnp.dot(err[i], factor[block[i]], preferred_element_type=f32) for i in every]
        for i in every:
            squares[0] = squares[0] + live[i] * white[i] * white[i]
        if between is not None:
            between()
        weighted = [(live[i] * tau_col * white[i]).astype(bf16) for i in every]
        adj = [
            lax.dot_general(weighted[i], factor[block[i]], nt, preferred_element_type=f32)
            for i in every
        ]
        for i in every:
            adj_slot[at[i]] = adj[i]
        both = [
            lax.dot_general(
                adj[i].astype(bf16),
                predict[block[i]].reshape(2 * width, width),
                nt,
                preferred_element_type=f32,
            ).astype(bf16)
            for i in every
        ]
        for i in every:
            seam_slot[at[i]] = both[i][:, width:]
        return [both[i][:, :width] for i in every]

    def hand_out(group, back):
        for j, (peer, kind) in enumerate(group):
            for k in range(cap):
                ret_send[peer, k * chans : (k + 1) * chans] = back[j * cap + k]
            give(peer, kind).start()

    to_sib.wait_recv()
    homes = [obs, raw_sib]
    back = process(own, lambda j, i, h: homes[j][slot_ref[0, h]])
    for k in range(cap):
        ret_recv[me, k * chans : (k + 1) * chans] = back[k]
    hand_out([(sib, 3)], back[cap:])

    @pl.when(lead)
    def _():
        to_far.wait_recv()
        relay.start()
        wait(pass_recv.at[pl.ds(0, 2)], pass_rs.at[0])
        for j, peer in enumerate(beside):
            near_send[span(skip[j])] = picked(pass_recv[peer], raw_far)
            pass_on(j).start()

    @pl.when(tail)
    def _():
        relay.wait_recv()

    @pl.when(inner)
    def _():
        arrived(m0)

    def turn(group, between=None):
        for owner, kind in group:
            arrived(owner)
        owners = [owner for owner, kind in group]
        hand_out(group, process(owners, lambda j, i, h: near_recv[i], between))

    early = by_place([(m0, 0)], [(m1, 0)])
    hand_out(
        early,
        process(
            [early[0][0]],
            lambda j, i, h: jnp.where(at_end, raw_far[slot_ref[0, h]], near_recv[i]),
        ),
    )
    turn(by_place([(m1, 0), (b0, 2)], [(b0, 2), (b1, 2)]))
    turn(by_place([(b1, 2), (s0, 1)], [(s0, 1), (s1, 1)]))
    live_lane = lax.broadcasted_iota(i32, (1, LANES), 1) == chans

    everyone = [(r, b) for r in regions for b in others + [me]] + [(region, b) for b in others]
    mine = region * nblock + me

    def share(r, b):
        return pltpu.make_async_remote_copy(
            src_ref=sq_send,
            dst_ref=sq_recv.at[mine],
            send_sem=sq_ss.at[0],
            recv_sem=sq_rs.at[0],
            device_id={"region": r, "block": b},
            device_id_type=MESH,
        )

    sums_in = sq_recv.at[pl.ds(0, len(everyone))]

    def share_all():
        sums = jnp.sum(
            jnp.where(eye, jnp.sum(squares[0], axis=1, keepdims=True), 0.0), axis=0, keepdims=True
        )
        sums = sums + jnp.where(live_lane, jnp.minimum(count, nbd).astype(f32), 0.0)
        sq_send[...] = sums
        for r, b in everyone:
            share(r, b).start()
        sq_recv[mine] = sums

    turn(by_place([(s1, 1)], [(m0, 0)]), share_all)

    @pl.when(has_prev)
    def _():
        for g in range(nbd):
            seam_ret[g] = seam_slot[flat[g]]
        seam_bwd.start()

    for g in range(nbd):
        out_ref[g] = adj_slot[flat[g]]

    def add(pair):
        blocks_back = ret_recv[pl.ds(pair * 2, 2)].reshape(2 * part, width)
        got = jnp.dot(spread[pair], blocks_back, preferred_element_type=f32)
        out_ref[...] = out_ref[...] - got.reshape(nbd, chans, width)

    def take(kind):
        wait(ret_recv.at[pl.ds(0, len(kinds[kind]))], ret_rs.at[kind])

    wait(req_send.at[pl.ds(0, len(others))], req_ss.at[0])

    @pl.when(inner)
    def _():
        wait(pass_recv.at[pl.ds(0, 1)], pass_ss.at[0])

    @pl.when(jnp.logical_not(lead))
    def _():
        wait(near_send.at[pl.ds(0, 6 * cap)], near_ss.at[0])

    to_sib.wait_send()

    @pl.when(lead)
    def _():
        to_far.wait_send()
        relay.wait_send()
        wait(near_send.at[pl.ds(0, 4 * cap)], near_ss.at[0])

    @pl.when(has_next)
    def _():
        seam_fwd.wait_send()

    @pl.when(has_prev)
    def _():
        seam_where.wait_send()

    take(3)
    add(chip)
    take(2)
    add(beside[0] // 2)

    take(0)
    add(mirror[0] // 2)

    @pl.when(has_next)
    def _():
        seam_where.wait_recv()
        mask = jnp.where(
            seam_tgt_in[...] == lax.broadcasted_iota(i32, (rows, rows), 0), 1.0, 0.0
        ).astype(bf16)
        seam_bwd.wait_recv()
        got = jnp.dot(mask, seam_ret_in[...].reshape(rows, width), preferred_element_type=f32)
        out_ref[...] = out_ref[...] - got.reshape(nbd, chans, width)

    take(1)
    add(skip[0] // 2)

    wait(sums_in, sq_rs.at[0])
    total = sq_recv[0]
    for d in range(1, nregion * nblock):
        total = total + sq_recv[d]
    total_live = jnp.sum(jnp.where(live_lane, total, 0.0), axis=1, keepdims=True)
    blocks = nbd * nblock * nregion
    gtau_ref[...] = (
        0.5 * total[:, :chans] - 0.5 * width * total_live / tau_ref[...]
    ) / (blocks * width)

    wait(ret_send.at[pl.ds(0, len(others))], ret_ss.at[0])
    wait(sums_in, sq_ss.at[0])

    @pl.when(has_prev)
    def _():
        seam_bwd.wait_send()


def write_out(obs_ref, tau_ref, obs_hbm, tau_hbm, sem):
    copies = [
        pltpu.make_async_copy(src, dst, sem.at[i])
        for i, (src, dst) in enumerate([(obs_ref, obs_hbm), (tau_ref, tau_hbm)])
    ]
    for copy in copies:
        copy.start()
    for copy in copies:
        copy.wait()


def shards(obs, predict, factor, tau, nbr_dev, nbr_slot, counts):
    nbd, chans, width = obs.shape
    nblock = lax.axis_size("block")
    nregion = lax.axis_size("region")
    cap = max(2, 2 * nbd // nblock)
    rows = nbd * chans
    part = cap * chans
    lanes = -(-part // LANES) * LANES
    group = 2 if nblock % 2 == 0 and part % LANES == 0 else 1
    line = nblock == 8 and part == LANES
    bf16, f32, i32 = jnp.bfloat16, jnp.float32, jnp.int32
    vmem = pl.BlockSpec(memory_space=pltpu.VMEM)
    hbm = pl.BlockSpec(memory_space=pltpu.HBM)
    dma = pltpu.SemaphoreType.DMA
    blocks = pltpu.VMEM((nbd, chans, width), bf16)
    slots = pltpu.VMEM((nblock * cap, chans, width), bf16)
    inputs = [
        pltpu.SMEM((1, nbd), i32),
        pltpu.SMEM((2, nbd), i32),
        pltpu.SMEM((1,), i32),
        pltpu.VMEM((1, chans), f32),
        blocks,
        pltpu.VMEM((nbd, 2, width, width), bf16),
        pltpu.VMEM((nbd, width, width), bf16),
        pltpu.VMEM((nblock, 1, lanes), i32),
        pltpu.VMEM((nblock, 1, lanes), i32),
        slots,
        slots,
    ]
    middle = [
        pltpu.VMEM((nblock, part, width), bf16),
        pltpu.VMEM((nblock, part, width), bf16),
        blocks,
        pltpu.VMEM((1, rows), i32),
        pltpu.VMEM((1, rows), i32),
        blocks,
        blocks,
        pltpu.VMEM((1, LANES), i32),
        pltpu.SMEM((1, LANES), i32),
        pltpu.VMEM((nblock // group, rows, group * part), bf16),
        pltpu.VMEM((nbd, chans, width), f32),
    ]
    sums = [
        pltpu.VMEM((1, LANES), f32),
        pltpu.VMEM((nblock, 1, LANES), f32),
        pltpu.VMEM((1, LANES), f32),
        pltpu.VMEM((nregion, 1, LANES), f32),
        dma((8,)),
    ]
    sems = [dma((nblock,))] * 8 + [dma((nregion,))] * 2 + [dma((3,))] * 2
    if line:
        body = line_kernel
        scratch = inputs[:9] + inputs[8:] + [blocks] * 2 + middle
        scratch += [pltpu.VMEM((nblock * cap, chans, width), f32), slots, sums[0]]
        scratch += [pltpu.VMEM((nregion * nblock, 1, LANES), f32), sums[-1]]
        scratch += [dma((n,)) for n in (1, 4, 1, nblock, 1, 4, 1, 1, 3, 3, 3, 3, 1, 1)]
    else:
        body = kernel
        scratch = inputs + middle
        scratch += [pltpu.VMEM((nbd + 1, chans, width), bf16), blocks] + sums + sems
    grad_obs, grad_tau = pl.pallas_call(
        functools.partial(body, nblock, nregion, cap),
        out_shape=(
            jax.ShapeDtypeStruct((nbd, chans, width), f32),
            jax.ShapeDtypeStruct((1, chans), f32),
        ),
        in_specs=[hbm] * 7,
        out_specs=(vmem, vmem),
        scratch_shapes=scratch,
        compiler_params=pltpu.CompilerParams(
            collective_id=0, has_side_effects=True, vmem_limit_bytes=48 << 20
        ),
        name="vecchia",
    )(
        *(
            value if value is counts else pltpu.with_memory_space_constraint(value, pltpu.HBM)
            for value in (nbr_dev.T, nbr_slot.T, counts, tau.reshape(1, chans), obs, predict, factor)
        )
    )
    grad_obs, grad_tau = pl.pallas_call(
        write_out,
        out_shape=(
            jax.ShapeDtypeStruct((nbd, chans, width), f32),
            jax.ShapeDtypeStruct((1, chans), f32),
        ),
        in_specs=[vmem, vmem],
        out_specs=(hbm, hbm),
        scratch_shapes=[dma((2,))],
        name="write_out",
    )(*(pltpu.with_memory_space_constraint(x, pltpu.VMEM) for x in (grad_obs, grad_tau)))
    return grad_obs, grad_tau.reshape(chans)


def solution(mesh):
    in_specs = (
        P(("region", "block"), None, None),
        P(("region", "block"), None, None, None),
        P(("region", "block"), None, None),
        P(),
        P(("region", "block"), None),
        P(("region", "block"), None),
        P(("region", "block")),
    )
    out_specs = (P(("region", "block"), None, None), P())
    return jax.shard_map(shards, mesh=mesh, in_specs=in_specs, out_specs=out_specs, check_vma=False)
```

```python
import functools

import jax
import jax.numpy as jnp
from jax import lax
from jax.experimental import pallas as pl
from jax.experimental.pallas import tpu as pltpu
from jax.sharding import PartitionSpec as P

MESH = pl.DeviceIdType.MESH
LANES = 128


def kernel(
    nblock,
    nregion,
    cap,
    dev_hbm,
    slot_hbm,
    counts_hbm,
    tau_hbm,
    obs_hbm,
    predict_hbm,
    factor_hbm,
    out_ref,
    gtau_ref,
    dev_ref,
    slot_ref,
    counts_ref,
    tau_ref,
    obs,
    predict,
    factor,
    req_send,
    req_recv,
    near_send,
    near_recv,
    ret_send,
    ret_recv,
    seam_obs,
    seam_tgt,
    seam_tgt_in,
    seam_ret,
    seam_ret_in,
    held,
    held_ref,
    spread,
    partial,
    back,
    adjoint,
    sq_send,
    sq_recv,
    rg_send,
    rg_recv,
    local_sem,
    req_ss,
    req_rs,
    near_ss,
    near_rs,
    ret_ss,
    ret_rs,
    sq_ss,
    sq_rs,
    rg_ss,
    rg_rs,
    seam_ss,
    seam_rs,
):
    nbd, chans, width = obs.shape
    rows = nbd * chans
    part = cap * chans
    lanes = req_send.shape[2]
    group = 2 if nblock % 2 == 0 and part % LANES == 0 else 1
    me = lax.axis_index("block")
    region = lax.axis_index("region")
    bf16, f32, i32 = jnp.bfloat16, jnp.float32, jnp.int32

    half = me // (nblock // 2)

    def farthest(turn):
        below = nblock - 1 - turn - (me + turn + 1) // nblock
        above = turn + (turn - me + nblock) // nblock
        return below + half * (above - below)

    def each_peer(body, nearest=False):
        def visit(turn):
            body(farthest(nblock - 2 - turn if nearest else turn))

        if nblock <= 8:
            for turn in range(nblock - 1):
                visit(turn)
        else:

            def run(turn, carry):
                visit(turn)
                return carry

            lax.fori_loop(0, nblock - 1, run, 0)

    def each_region(body):
        for step in range(1, nregion):
            body(lax.rem(region + step, nregion))

    def to_block(src, dst, ss, rs, peer):
        return pltpu.make_async_remote_copy(
            src_ref=src,
            dst_ref=dst,
            send_sem=ss,
            recv_sem=rs,
            device_id={"block": peer},
            device_id_type=MESH,
        )

    def to_region(src, dst, ss, rs, peer):
        return pltpu.make_async_remote_copy(
            src_ref=src,
            dst_ref=dst,
            send_sem=ss,
            recv_sem=rs,
            device_id={"region": peer},
            device_id_type=MESH,
        )

    small = [
        pltpu.make_async_copy(src, dst, local_sem.at[3 + i])
        for i, (src, dst) in enumerate(
            [(dev_hbm, dev_ref), (slot_hbm, slot_ref), (counts_hbm, counts_ref), (tau_hbm, tau_ref)]
        )
    ]
    for copy in small:
        copy.start()

    barrier = pltpu.get_barrier_semaphore()
    each_peer(
        lambda peer: pl.semaphore_signal(
            barrier, inc=1, device_id={"block": peer}, device_id_type=MESH
        )
    )
    each_region(
        lambda peer: pl.semaphore_signal(
            barrier, inc=1, device_id={"region": peer}, device_id_type=MESH
        )
    )
    load_obs = pltpu.make_async_copy(obs_hbm, obs, local_sem.at[0])
    load_predict = pltpu.make_async_copy(predict_hbm, predict, local_sem.at[1])
    load_factor = pltpu.make_async_copy(factor_hbm, factor, local_sem.at[2])
    load_obs.start()
    load_predict.start()
    load_factor.start()

    for copy in small:
        copy.wait()

    dest = [dev_ref[0, h] for h in range(nbd)]
    flat = []
    for h in range(nbd):
        rank = jnp.int32(0)
        for g in range(h):
            rank = rank + (dest[g] == dest[h]).astype(i32)
        flat.append(dest[h] * cap + rank)

    lane = lax.broadcasted_iota(i32, (nblock, lanes), 1)
    spot = lax.broadcasted_iota(i32, (nblock, lanes), 0) * cap + lane // chans
    spot = jnp.where(lane < part, spot, -1)
    wanted = jnp.full((nblock, lanes), -1, i32)
    for h in range(nbd):
        wanted = jnp.where(spot == flat[h], slot_ref[0, h] * chans + lane % chans, wanted)
    for d in range(nblock):
        req_send[d] = wanted[d : d + 1]

    block_lane = lax.broadcasted_iota(i32, (1, rows), 1)
    owner_of = block_lane // chans
    seam_row = jnp.zeros((1, rows), i32)
    for h in range(nbd):
        seam_row = jnp.where(owner_of == h, slot_ref[1, h], seam_row)
    seam_tgt[...] = seam_row * chans + block_lane % chans

    place_lane = lax.broadcasted_iota(i32, (1, LANES), 1)
    holder = jnp.full((1, LANES), nbd, i32)
    for h in range(nbd):
        holder = jnp.where(place_lane == flat[h], h, holder)
    held[...] = holder
    load_held = pltpu.make_async_copy(held, held_ref, local_sem.at[7])
    load_held.start()
    back[nbd] = jnp.zeros((chans, width), bf16)

    pl.semaphore_wait(barrier, nblock - 1 + nregion - 1)

    def request(peer, mine):
        return to_block(req_send.at[peer], req_recv.at[mine], req_ss.at[peer], req_rs.at[mine], peer)

    each_peer(lambda peer: request(peer, me).start())
    req_recv[me] = req_send[me]

    down = lax.rem(region + 1, nregion)
    up = lax.rem(region + nregion - 1, nregion)
    seam_fwd = to_region(obs_hbm, seam_obs, seam_ss.at[0], seam_rs.at[0], down)
    seam_where = to_region(seam_tgt, seam_tgt_in, seam_ss.at[1], seam_rs.at[1], up)
    seam_bwd = to_region(seam_ret, seam_ret_in, seam_ss.at[2], seam_rs.at[2], up)
    has_prev = region > 0
    has_next = region < nregion - 1

    @pl.when(has_next)
    def _():
        seam_fwd.start()

    @pl.when(has_prev)
    def _():
        seam_where.start()

    load_obs.wait()
    pick_lane = lax.broadcasted_iota(i32, (part, rows), 1)

    def picked(peer):
        row = jnp.broadcast_to(req_recv[peer], (LANES, lanes))
        column = jnp.transpose(row)[:part]
        column = jnp.concatenate([column] * (rows // LANES), axis=1)
        mask = jnp.where(column == pick_lane, 1.0, 0.0).astype(bf16)
        got = jnp.dot(mask, obs[...].reshape(rows, width), preferred_element_type=f32)
        return got.astype(bf16).reshape(cap, chans, width)

    def span(d):
        return pl.ds(d * cap, cap)

    def serve(peer, mine):
        return to_block(
            near_send.at[span(peer)],
            near_recv.at[span(mine)],
            near_ss.at[peer],
            near_rs.at[mine],
            peer,
        )

    def put(peer):
        near_send[span(peer)] = picked(peer)
        serve(peer, me).start()

    def answer(peer):
        request(me, peer).wait_recv()
        put(peer)

    each_peer(answer, nearest=True)
    near_recv[span(me)] = picked(me)

    def build(pair):
        wanted_row = jnp.concatenate(
            [req_recv[pair * group + i][:, :part] for i in range(group)], axis=1
        )
        spread[pair] = jnp.where(
            wanted_row == lax.broadcasted_iota(i32, (rows, group * part), 0), 1.0, 0.0
        ).astype(bf16)

    for pair in range(nblock // group):
        build(pair)
    load_held.wait()

    @pl.when(has_prev)
    def _():
        seam_fwd.wait_recv()

    @pl.when(jnp.logical_not(has_prev))
    def _():
        seam_obs[...] = jnp.zeros_like(seam_obs)

    load_predict.wait()
    for g in range(nbd):
        partial[g] = obs[g].astype(f32) - jnp.dot(
            seam_obs[slot_ref[1, g]], predict[g, 1], preferred_element_type=f32
        )
    load_factor.wait()

    eye = lax.broadcasted_iota(i32, (chans, LANES), 0) == lax.broadcasted_iota(
        i32, (chans, LANES), 1
    )
    tau_row = jnp.concatenate([tau_ref[...], jnp.zeros((1, LANES - chans), f32)], axis=1)
    tau_col = jnp.sum(jnp.where(eye, tau_row, 0.0), axis=1, keepdims=True)
    count = counts_ref[0]

    each_peer(lambda peer: serve(me, peer).wait_recv(), nearest=True)

    nt = (((1,), (1,)), ((), ()))
    every = range(nbd)
    err = [
        (
            partial[g]
            - jnp.dot(near_recv[flat[g]], predict[g, 0], preferred_element_type=f32)
        ).astype(bf16)
        for g in every
    ]
    white = [jnp.dot(err[g], factor[g], preferred_element_type=f32) for g in every]
    live = [(g < count).astype(f32) for g in every]
    weighted = [(live[g] * tau_col * white[g]).astype(bf16) for g in every]
    squares = live[0] * white[0] * white[0]
    for g in range(1, nbd):
        squares = squares + live[g] * white[g] * white[g]
    live_lane = lax.broadcasted_iota(i32, (1, LANES), 1) == chans
    sums = jnp.sum(
        jnp.where(eye, jnp.sum(squares, axis=1, keepdims=True), 0.0), axis=0, keepdims=True
    )
    sums = sums + jnp.where(live_lane, jnp.minimum(count, nbd).astype(f32), 0.0)
    sq_send[...] = sums

    def share(peer, mine):
        return to_block(sq_send, sq_recv.at[mine], sq_ss.at[peer], sq_rs.at[mine], peer)

    each_peer(lambda peer: share(peer, me).start())
    sq_recv[me] = sums

    adj = [lax.dot_general(weighted[g], factor[g], nt, preferred_element_type=f32) for g in every]
    for g in every:
        out_ref[g] = adj[g]
        adjoint[g] = adj[g].astype(bf16)

    for g in every:
        back[g] = lax.dot_general(
            adjoint[g], predict[g, 0], nt, preferred_element_type=f32
        ).astype(bf16)

    def pack(dst, peer):
        for k in range(cap):
            dst[k * chans : (k + 1) * chans] = back[held_ref[0, peer * cap + k]]

    def give(peer, mine):
        return to_block(ret_send.at[peer], ret_recv.at[mine], ret_ss.at[peer], ret_rs.at[mine], peer)

    def give_back(peer):
        pack(ret_send.at[peer], peer)
        give(peer, me).start()

    each_peer(give_back)
    pack(ret_recv.at[me], me)

    @pl.when(has_prev)
    def _():
        for g in range(nbd):
            seam_ret[g] = lax.dot_general(
                adjoint[g], predict[g, 1], nt, preferred_element_type=f32
            ).astype(bf16)
        seam_bwd.start()

    each_peer(lambda peer: share(me, peer).wait_recv(), nearest=True)
    line = sq_recv[0]
    for d in range(1, nblock):
        line = line + sq_recv[d]
    rg_send[...] = line

    def share_region(peer, mine):
        return to_region(rg_send, rg_recv.at[mine], rg_ss.at[peer], rg_rs.at[mine], peer)

    each_region(lambda peer: share_region(peer, region).start())
    rg_recv[region] = line

    @pl.when(has_next)
    def _():
        seam_where_in = to_region(seam_tgt, seam_tgt_in, seam_ss.at[1], seam_rs.at[1], up)
        seam_where_in.wait_recv()
        mask = jnp.where(
            seam_tgt_in[...] == lax.broadcasted_iota(i32, (rows, rows), 0), 1.0, 0.0
        ).astype(bf16)
        seam_bwd.wait_recv()
        got = jnp.dot(mask, seam_ret_in[...].reshape(rows, width), preferred_element_type=f32)
        out_ref[...] = out_ref[...] - got.reshape(nbd, chans, width)

    def add(pair):
        blocks_back = ret_recv[pl.ds(pair * group, group)].reshape(group * part, width)
        got = jnp.dot(spread[pair], blocks_back, preferred_element_type=f32)
        out_ref[...] = out_ref[...] - got.reshape(nbd, chans, width)

    each_peer(lambda peer: give(me, peer).wait_recv(), nearest=True)
    for pair in range(nblock // group):
        add(pair)

    each_region(lambda peer: share_region(region, peer).wait_recv())
    total = rg_recv[0]
    for r in range(1, nregion):
        total = total + rg_recv[r]
    total_live = jnp.sum(jnp.where(live_lane, total, 0.0), axis=1, keepdims=True)
    blocks = nbd * nblock * nregion
    gtau_ref[...] = (
        0.5 * total[:, :chans] - 0.5 * width * total_live / tau_ref[...]
    ) / (blocks * width)

    def sent(peer):
        request(peer, me).wait_send()
        serve(peer, me).wait_send()
        give(peer, me).wait_send()
        share(peer, me).wait_send()

    each_peer(sent)
    each_region(lambda peer: share_region(peer, region).wait_send())

    @pl.when(has_next)
    def _():
        seam_fwd.wait_send()

    @pl.when(has_prev)
    def _():
        seam_where.wait_send()
        seam_bwd.wait_send()


def line_kernel(
    nblock,
    nregion,
    cap,
    dev_hbm,
    slot_hbm,
    counts_hbm,
    tau_hbm,
    obs_hbm,
    predict_hbm,
    factor_hbm,
    out_ref,
    gtau_ref,
    dev_ref,
    slot_ref,
    counts_ref,
    tau_ref,
    obs,
    predict,
    factor,
    req_send,
    req_recv,
    pass_recv,
    near_send,
    near_recv,
    raw_sib,
    raw_far,
    ret_send,
    ret_recv,
    seam_obs,
    seam_tgt,
    seam_tgt_in,
    seam_ret,
    seam_ret_in,
    held,
    held_ref,
    spread,
    partial,
    adj_slot,
    seam_slot,
    sq_send,
    sq_recv,
    local_sem,
    req_ss,
    req_rs,
    near_ss,
    near_rs,
    ret_ss,
    ret_rs,
    sq_ss,
    sq_rs,
    seam_ss,
    seam_rs,
    raw_ss,
    raw_rs,
    pass_ss,
    pass_rs,
):
    nbd, chans, width = obs.shape
    rows = nbd * chans
    part = cap * chans
    me = lax.axis_index("block")
    region = lax.axis_index("region")
    bf16, f32, i32 = jnp.bfloat16, jnp.float32, jnp.int32
    nt = (((1,), (1,)), ((), ()))

    def flip(d, bit):
        return d + bit - 2 * bit * lax.rem(d // bit, 2)

    sib = flip(me, 1)
    chip = me // 2
    own = [me, sib]
    beside = [flip(d, 2) for d in own]
    skip = [flip(d, 4) for d in own]
    mirror = [flip(d, 4) for d in beside]
    at_end = chip * (nblock // 2 - 1 - chip) == 0
    inner = jnp.logical_not(at_end)
    others = mirror + skip + beside + [sib]
    end = 1 - lax.rem((chip + 1) // 2, 2)
    kinds = [mirror, skip, beside, [sib]]
    core = lax.rem(me, 2)
    lead = jnp.logical_and(at_end, core == 1)
    tail = jnp.logical_and(at_end, core == 0)
    m0, s0, b0 = [2 * (d[0] // 2) for d in (mirror, skip, beside)]
    m1, s1, b1 = m0 + 1, s0 + 1, b0 + 1

    def by_place(inside, outside):
        return [tuple(i + end * (o - i) for i, o in zip(*two)) for two in zip(inside, outside)]


    def to_block(src, dst, ss, rs, peer):
        return pltpu.make_async_remote_copy(
            src_ref=src,
            dst_ref=dst,
            send_sem=ss,
            recv_sem=rs,
            device_id={"block": peer},
            device_id_type=MESH,
        )

    def to_region(src, dst, ss, rs, peer):
        return pltpu.make_async_remote_copy(
            src_ref=src,
            dst_ref=dst,
            send_sem=ss,
            recv_sem=rs,
            device_id={"region": peer},
            device_id_type=MESH,
        )

    def wait(ref, sem):
        pltpu.make_async_copy(ref, ref, sem).wait()

    regions = [lax.rem(region + step, nregion) for step in range(1, nregion)]

    small = [
        pltpu.make_async_copy(src, dst, local_sem.at[3 + i])
        for i, (src, dst) in enumerate(
            [(dev_hbm, dev_ref), (slot_hbm, slot_ref), (counts_hbm, counts_ref), (tau_hbm, tau_ref)]
        )
    ]
    for copy in small:
        copy.start()

    barrier = pltpu.get_barrier_semaphore()
    for peer in others:
        pl.semaphore_signal(barrier, inc=1, device_id={"block": peer}, device_id_type=MESH)
    for peer in regions:
        pl.semaphore_signal(barrier, inc=1, device_id={"region": peer}, device_id_type=MESH)
    load_obs = pltpu.make_async_copy(obs_hbm, obs, local_sem.at[0])
    load_predict = pltpu.make_async_copy(predict_hbm, predict, local_sem.at[1])
    load_factor = pltpu.make_async_copy(factor_hbm, factor, local_sem.at[2])
    load_obs.start()
    load_predict.start()
    load_factor.start()

    for copy in small:
        copy.wait()

    dest = [dev_ref[0, h] for h in range(nbd)]
    flat = []
    for h in range(nbd):
        rank = jnp.int32(0)
        for g in range(h):
            rank = rank + (dest[g] == dest[h]).astype(i32)
        flat.append(dest[h] * cap + rank)

    lane = lax.broadcasted_iota(i32, (nblock, part), 1)
    spot = lax.broadcasted_iota(i32, (nblock, part), 0) * cap + lane // chans
    wanted = jnp.full((nblock, part), -1, i32)
    for h in range(nbd):
        wanted = jnp.where(spot == flat[h], slot_ref[0, h] * chans + lane % chans, wanted)
    for d in range(nblock):
        req_send[d] = wanted[d : d + 1]

    block_lane = lax.broadcasted_iota(i32, (1, rows), 1)
    owner_of = block_lane // chans
    seam_row = jnp.zeros((1, rows), i32)
    for h in range(nbd):
        seam_row = jnp.where(owner_of == h, slot_ref[1, h], seam_row)
    seam_tgt[...] = seam_row * chans + block_lane % chans

    place_lane = lax.broadcasted_iota(i32, (1, LANES), 1)
    holder = jnp.full((1, LANES), nbd, i32)
    for h in range(nbd):
        holder = jnp.where(place_lane == flat[h], h, holder)
    held[...] = holder
    load_held = pltpu.make_async_copy(held, held_ref, local_sem.at[7])
    load_held.start()

    pl.semaphore_wait(barrier, nblock - 1 + nregion - 1)

    def request(peer, kind):
        return to_block(req_send.at[peer], req_recv.at[me], req_ss.at[0], req_rs.at[kind], peer)

    def asked(kind):
        wait(req_recv.at[pl.ds(0, len(kinds[kind]))], req_rs.at[kind])

    def request_pass(owner, peer):
        return to_block(req_send.at[owner], pass_recv.at[me], pass_ss.at[0], pass_rs.at[0], peer)

    for kind, peers in enumerate(kinds):
        for peer in peers:
            request(peer, kind).start()
    req_recv[me] = req_send[me]

    @pl.when(inner)
    def _():
        request_pass(s1, b1).start()


    to_sib = to_block(obs_hbm, raw_sib, raw_ss.at[0], raw_rs.at[0], sib)
    to_far = to_block(obs_hbm, raw_far, raw_ss.at[0], raw_rs.at[1], mirror[0])
    relay = to_block(raw_far, raw_far, raw_ss.at[0], raw_rs.at[1], sib)

    down = lax.rem(region + 1, nregion)
    up = lax.rem(region + nregion - 1, nregion)
    seam_fwd = to_region(obs_hbm, seam_obs, seam_ss.at[0], seam_rs.at[0], down)
    seam_where = to_region(seam_tgt, seam_tgt_in, seam_ss.at[1], seam_rs.at[1], up)
    seam_bwd = to_region(seam_ret, seam_ret_in, seam_ss.at[2], seam_rs.at[2], up)
    has_prev = region > 0
    has_next = region < nregion - 1

    @pl.when(core == 1)
    def _():
        to_far.start()

    @pl.when(has_next)
    def _():
        seam_fwd.start()

    @pl.when(has_prev)
    def _():
        seam_where.start()

    to_sib.start()

    load_obs.wait()
    pick_lane = lax.broadcasted_iota(i32, (part, rows), 1)

    def picked(row, source):
        row = jnp.broadcast_to(row, (LANES, part))
        column = jnp.concatenate([jnp.transpose(row)] * (rows // LANES), axis=1)
        mask = jnp.where(column == pick_lane, 1.0, 0.0).astype(bf16)
        got = jnp.dot(mask, source[...].reshape(rows, width), preferred_element_type=f32)
        return got.astype(bf16).reshape(cap, chans, width)

    def span(d):
        return pl.ds(d * cap, cap)

    def serve(peer):
        return to_block(
            near_send.at[span(peer)],
            near_recv.at[span(me)],
            near_ss.at[0],
            near_rs.at[me],
            peer,
        )

    def arrived(owner):
        wait(near_recv.at[span(owner)], near_rs.at[owner])

    def pass_on(j):
        return to_block(
            near_send.at[span(skip[j])],
            near_recv.at[span(mirror[0])],
            near_ss.at[0],
            near_rs.at[mirror[0]],
            beside[j],
        )

    def answer(kind):
        asked(kind)
        for peer in kinds[kind]:
            near_send[span(peer)] = picked(req_recv[peer], obs)
            serve(peer).start()

    @pl.when(jnp.logical_and(inner, core == 0))
    def _():
        for kind in (0, 1, 2):
            answer(kind)

    @pl.when(jnp.logical_and(inner, core == 1))
    def _():
        for kind in (1, 2):
            answer(kind)
        asked(0)

    @pl.when(tail)
    def _():
        for kind in (1, 2, 0):
            answer(kind)

    @pl.when(lead)
    def _():
        answer(2)
        asked(1)
        asked(0)

    asked(3)

    def build(pair):
        wanted_row = jnp.concatenate([req_recv[pair * 2 + i] for i in range(2)], axis=1)
        spread[pair] = jnp.where(
            wanted_row == lax.broadcasted_iota(i32, (rows, 2 * part), 0), 1.0, 0.0
        ).astype(bf16)

    for pair in range(nblock // 2):
        build(pair)
    load_held.wait()

    eye = lax.broadcasted_iota(i32, (chans, LANES), 0) == lax.broadcasted_iota(
        i32, (chans, LANES), 1
    )
    tau_row = jnp.concatenate([tau_ref[...], jnp.zeros((1, LANES - chans), f32)], axis=1)
    tau_col = jnp.sum(jnp.where(eye, tau_row, 0.0), axis=1, keepdims=True)
    count = counts_ref[0]

    @pl.when(has_prev)
    def _():
        seam_fwd.wait_recv()

    @pl.when(jnp.logical_not(has_prev))
    def _():
        seam_obs[...] = jnp.zeros_like(seam_obs)

    load_predict.wait()
    for g in range(nbd):
        partial[g] = obs[g].astype(f32) - jnp.dot(
            seam_obs[slot_ref[1, g]], predict[g, 1], preferred_element_type=f32
        )
    load_factor.wait()

    def give(peer, kind):
        return to_block(ret_send.at[peer], ret_recv.at[me], ret_ss.at[0], ret_rs.at[kind], peer)

    squares = [jnp.zeros((chans, width), f32)]

    def process(peers, near_of, between=None):
        at = [peer * cap + k for peer in peers for k in range(cap)]
        every = range(len(at))
        who = [held_ref[0, i] for i in at]
        block = [jnp.minimum(w, nbd - 1) for w in who]
        live = [(w < count).astype(f32) for w in who]
        near = [near_of(i // cap, at[i], block[i]) for i in every]
        err = [
            (
                partial[block[i]]
                - jnp.dot(near[i], predict[block[i], 0], preferred_element_type=f32)
            ).astype(bf16)
            for i in every
        ]
        white = [jnp.dot(err[i], factor[block[i]], preferred_element_type=f32) for i in every]
        for i in every:
            squares[0] = squares[0] + live[i] * white[i] * white[i]
        if between is not None:
            between()
        weighted = [(live[i] * tau_col * white[i]).astype(bf16) for i in every]
        adj = [
            lax.dot_general(weighted[i], factor[block[i]], nt, preferred_element_type=f32)
            for i in every
        ]
        for i in every:
            adj_slot[at[i]] = adj[i]
        both = [
            lax.dot_general(
                adj[i].astype(bf16),
                predict[block[i]].reshape(2 * width, width),
                nt,
                preferred_element_type=f32,
            ).astype(bf16)
            for i in every
        ]
        for i in every:
            seam_slot[at[i]] = both[i][:, width:]
        return [both[i][:, :width] for i in every]

    def hand_out(group, back):
        for j, (peer, kind) in enumerate(group):
            for k in range(cap):
                ret_send[peer, k * chans : (k + 1) * chans] = back[j * cap + k]
            give(peer, kind).start()

    to_sib.wait_recv()
    homes = [obs, raw_sib]
    back = process(own, lambda j, i, h: homes[j][slot_ref[0, h]])
    for k in range(cap):
        ret_recv[me, k * chans : (k + 1) * chans] = back[k]
    hand_out([(sib, 3)], back[cap:])

    @pl.when(core == 1)
    def _():
        to_far.wait_recv()
        relay.start()

    @pl.when(lead)
    def _():
        wait(pass_recv.at[pl.ds(0, 2)], pass_rs.at[0])
        for j, peer in enumerate(beside):
            near_send[span(skip[j])] = picked(pass_recv[peer], raw_far)
            pass_on(j).start()

    @pl.when(core == 0)
    def _():
        relay.wait_recv()

    def send_seam():
        @pl.when(has_prev)
        def _():
            for g in range(nbd):
                seam_ret[g] = seam_slot[flat[g]]
            seam_bwd.start()

    def turn(group, between=None):
        for owner, kind in group:
            arrived(owner)
        owners = [owner for owner, kind in group]
        back = process(owners, lambda j, i, h: near_recv[i], between)
        if between is not None:
            send_seam()
        hand_out(group, back)

    hand_out([(m1, 0)], process([m1], lambda j, i, h: raw_far[slot_ref[0, h]]))
    turn(by_place([(b0, 2), (b1, 2)], [(b0, 2), (b1, 2)]))
    turn(by_place([(m0, 0), (s0, 1)], [(s0, 1), (s1, 1)]))
    live_lane = lax.broadcasted_iota(i32, (1, LANES), 1) == chans

    everyone = [(r, b) for r in regions for b in others + [me]] + [(region, b) for b in others]
    mine = region * nblock + me

    def share(r, b):
        return pltpu.make_async_remote_copy(
            src_ref=sq_send,
            dst_ref=sq_recv.at[mine],
            send_sem=sq_ss.at[0],
            recv_sem=sq_rs.at[0],
            device_id={"region": r, "block": b},
            device_id_type=MESH,
        )

    sums_in = sq_recv.at[pl.ds(0, len(everyone))]

    def share_all():
        sums = jnp.sum(
            jnp.where(eye, jnp.sum(squares[0], axis=1, keepdims=True), 0.0), axis=0, keepdims=True
        )
        sums = sums + jnp.where(live_lane, jnp.minimum(count, nbd).astype(f32), 0.0)
        sq_send[...] = sums
        for r, b in everyone:
            share(r, b).start()
        sq_recv[mine] = sums

    turn(by_place([(s1, 1)], [(m0, 0)]), share_all)

    for g in range(nbd):
        out_ref[g] = adj_slot[flat[g]]

    def add(pair):
        blocks_back = ret_recv[pl.ds(pair * 2, 2)].reshape(2 * part, width)
        got = jnp.dot(spread[pair], blocks_back, preferred_element_type=f32)
        out_ref[...] = out_ref[...] - got.reshape(nbd, chans, width)

    def take(kind):
        wait(ret_recv.at[pl.ds(0, len(kinds[kind]))], ret_rs.at[kind])

    wait(req_send.at[pl.ds(0, len(others))], req_ss.at[0])

    @pl.when(inner)
    def _():
        wait(pass_recv.at[pl.ds(0, 1)], pass_ss.at[0])

    @pl.when(core == 0)
    def _():
        wait(near_send.at[pl.ds(0, 6 * cap)], near_ss.at[0])

    @pl.when(core == 0)
    def _():
        to_sib.wait_send()

    @pl.when(core == 1)
    def _():
        wait(near_send.at[pl.ds(0, 4 * cap)], near_ss.at[0])
        wait(predict.at[pl.ds(0, 3 * nbd * chans // (2 * width))], raw_ss.at[0])

    @pl.when(has_next)
    def _():
        seam_fwd.wait_send()

    @pl.when(has_prev)
    def _():
        seam_where.wait_send()

    take(3)
    add(chip)
    take(2)
    add(beside[0] // 2)

    take(0)
    add(mirror[0] // 2)

    @pl.when(has_next)
    def _():
        seam_where.wait_recv()
        mask = jnp.where(
            seam_tgt_in[...] == lax.broadcasted_iota(i32, (rows, rows), 0), 1.0, 0.0
        ).astype(bf16)
        seam_bwd.wait_recv()
        got = jnp.dot(mask, seam_ret_in[...].reshape(rows, width), preferred_element_type=f32)
        out_ref[...] = out_ref[...] - got.reshape(nbd, chans, width)

    take(1)
    add(skip[0] // 2)

    wait(sums_in, sq_rs.at[0])
    total = sq_recv[0]
    for d in range(1, nregion * nblock):
        total = total + sq_recv[d]
    total_live = jnp.sum(jnp.where(live_lane, total, 0.0), axis=1, keepdims=True)
    blocks = nbd * nblock * nregion
    gtau_ref[...] = (
        0.5 * total[:, :chans] - 0.5 * width * total_live / tau_ref[...]
    ) / (blocks * width)

    wait(ret_send.at[pl.ds(0, len(others))], ret_ss.at[0])
    wait(sums_in, sq_ss.at[0])

    @pl.when(has_prev)
    def _():
        seam_bwd.wait_send()


def write_out(obs_ref, tau_ref, obs_hbm, tau_hbm, sem):
    copies = [
        pltpu.make_async_copy(src, dst, sem.at[i])
        for i, (src, dst) in enumerate([(obs_ref, obs_hbm), (tau_ref, tau_hbm)])
    ]
    for copy in copies:
        copy.start()
    for copy in copies:
        copy.wait()


def shards(obs, predict, factor, tau, nbr_dev, nbr_slot, counts):
    nbd, chans, width = obs.shape
    nblock = lax.axis_size("block")
    nregion = lax.axis_size("region")
    cap = max(2, 2 * nbd // nblock)
    rows = nbd * chans
    part = cap * chans
    lanes = -(-part // LANES) * LANES
    group = 2 if nblock % 2 == 0 and part % LANES == 0 else 1
    line = nblock == 8 and part == LANES
    bf16, f32, i32 = jnp.bfloat16, jnp.float32, jnp.int32
    vmem = pl.BlockSpec(memory_space=pltpu.VMEM)
    hbm = pl.BlockSpec(memory_space=pltpu.HBM)
    dma = pltpu.SemaphoreType.DMA
    blocks = pltpu.VMEM((nbd, chans, width), bf16)
    slots = pltpu.VMEM((nblock * cap, chans, width), bf16)
    inputs = [
        pltpu.SMEM((1, nbd), i32),
        pltpu.SMEM((2, nbd), i32),
        pltpu.SMEM((1,), i32),
        pltpu.VMEM((1, chans), f32),
        blocks,
        pltpu.VMEM((nbd, 2, width, width), bf16),
        pltpu.VMEM((nbd, width, width), bf16),
        pltpu.VMEM((nblock, 1, lanes), i32),
        pltpu.VMEM((nblock, 1, lanes), i32),
        slots,
        slots,
    ]
    middle = [
        pltpu.VMEM((nblock, part, width), bf16),
        pltpu.VMEM((nblock, part, width), bf16),
        blocks,
        pltpu.VMEM((1, rows), i32),
        pltpu.VMEM((1, rows), i32),
        blocks,
        blocks,
        pltpu.VMEM((1, LANES), i32),
        pltpu.SMEM((1, LANES), i32),
        pltpu.VMEM((nblock // group, rows, group * part), bf16),
        pltpu.VMEM((nbd, chans, width), f32),
    ]
    sums = [
        pltpu.VMEM((1, LANES), f32),
        pltpu.VMEM((nblock, 1, LANES), f32),
        pltpu.VMEM((1, LANES), f32),
        pltpu.VMEM((nregion, 1, LANES), f32),
        dma((8,)),
    ]
    sems = [dma((nblock,))] * 8 + [dma((nregion,))] * 2 + [dma((3,))] * 2
    if line:
        body = line_kernel
        scratch = inputs[:9] + inputs[8:] + [blocks] * 2 + middle
        scratch += [pltpu.VMEM((nblock * cap, chans, width), f32), slots, sums[0]]
        scratch += [pltpu.VMEM((nregion * nblock, 1, LANES), f32), sums[-1]]
        scratch += [dma((n,)) for n in (1, 4, 1, nblock, 1, 4, 1, 1, 3, 3, 1, 2, 1, 1)]
    else:
        body = kernel
        scratch = inputs + middle
        scratch += [pltpu.VMEM((nbd + 1, chans, width), bf16), blocks] + sums + sems
    grad_obs, grad_tau = pl.pallas_call(
        functools.partial(body, nblock, nregion, cap),
        out_shape=(
            jax.ShapeDtypeStruct((nbd, chans, width), f32),
            jax.ShapeDtypeStruct((1, chans), f32),
        ),
        in_specs=[hbm] * 7,
        out_specs=(vmem, vmem),
        scratch_shapes=scratch,
        compiler_params=pltpu.CompilerParams(
            collective_id=0, has_side_effects=True, vmem_limit_bytes=48 << 20
        ),
        name="vecchia",
    )(
        *(
            value if value is counts else pltpu.with_memory_space_constraint(value, pltpu.HBM)
            for value in (nbr_dev.T, nbr_slot.T, counts, tau.reshape(1, chans), obs, predict, factor)
        )
    )
    grad_obs, grad_tau = pl.pallas_call(
        write_out,
        out_shape=(
            jax.ShapeDtypeStruct((nbd, chans, width), f32),
            jax.ShapeDtypeStruct((1, chans), f32),
        ),
        in_specs=[vmem, vmem],
        out_specs=(hbm, hbm),
        scratch_shapes=[dma((2,))],
        name="write_out",
    )(*(pltpu.with_memory_space_constraint(x, pltpu.VMEM) for x in (grad_obs, grad_tau)))
    return grad_obs, grad_tau.reshape(chans)


def solution(mesh):
    in_specs = (
        P(("region", "block"), None, None),
        P(("region", "block"), None, None, None),
        P(("region", "block"), None, None),
        P(),
        P(("region", "block"), None),
        P(("region", "block"), None),
        P(("region", "block")),
    )
    out_specs = (P(("region", "block"), None, None), P())
    return jax.shard_map(shards, mesh=mesh, in_specs=in_specs, out_specs=out_specs, check_vma=False)
```

```python
import functools

import jax
import jax.numpy as jnp
from jax import lax
from jax.experimental import pallas as pl
from jax.experimental.pallas import tpu as pltpu
from jax.sharding import PartitionSpec as P

MESH = pl.DeviceIdType.MESH
LANES = 128


def kernel(
    nblock,
    nregion,
    cap,
    dev_hbm,
    slot_hbm,
    counts_hbm,
    tau_hbm,
    obs_hbm,
    predict_hbm,
    factor_hbm,
    out_ref,
    gtau_ref,
    dev_ref,
    slot_ref,
    counts_ref,
    tau_ref,
    obs,
    predict,
    factor,
    req_send,
    req_recv,
    near_send,
    near_recv,
    ret_send,
    ret_recv,
    seam_obs,
    seam_tgt,
    seam_tgt_in,
    seam_ret,
    seam_ret_in,
    held,
    held_ref,
    spread,
    partial,
    back,
    adjoint,
    sq_send,
    sq_recv,
    rg_send,
    rg_recv,
    local_sem,
    req_ss,
    req_rs,
    near_ss,
    near_rs,
    ret_ss,
    ret_rs,
    sq_ss,
    sq_rs,
    rg_ss,
    rg_rs,
    seam_ss,
    seam_rs,
):
    nbd, chans, width = obs.shape
    rows = nbd * chans
    part = cap * chans
    lanes = req_send.shape[2]
    group = 2 if nblock % 2 == 0 and part % LANES == 0 else 1
    me = lax.axis_index("block")
    region = lax.axis_index("region")
    bf16, f32, i32 = jnp.bfloat16, jnp.float32, jnp.int32

    half = me // (nblock // 2)

    def farthest(turn):
        below = nblock - 1 - turn - (me + turn + 1) // nblock
        above = turn + (turn - me + nblock) // nblock
        return below + half * (above - below)

    def each_peer(body, nearest=False):
        def visit(turn):
            body(farthest(nblock - 2 - turn if nearest else turn))

        if nblock <= 8:
            for turn in range(nblock - 1):
                visit(turn)
        else:

            def run(turn, carry):
                visit(turn)
                return carry

            lax.fori_loop(0, nblock - 1, run, 0)

    def each_region(body):
        for step in range(1, nregion):
            body(lax.rem(region + step, nregion))

    def to_block(src, dst, ss, rs, peer):
        return pltpu.make_async_remote_copy(
            src_ref=src,
            dst_ref=dst,
            send_sem=ss,
            recv_sem=rs,
            device_id={"block": peer},
            device_id_type=MESH,
        )

    def to_region(src, dst, ss, rs, peer):
        return pltpu.make_async_remote_copy(
            src_ref=src,
            dst_ref=dst,
            send_sem=ss,
            recv_sem=rs,
            device_id={"region": peer},
            device_id_type=MESH,
        )

    small = [
        pltpu.make_async_copy(src, dst, local_sem.at[3 + i])
        for i, (src, dst) in enumerate(
            [(dev_hbm, dev_ref), (slot_hbm, slot_ref), (counts_hbm, counts_ref), (tau_hbm, tau_ref)]
        )
    ]
    for copy in small:
        copy.start()

    barrier = pltpu.get_barrier_semaphore()
    each_peer(
        lambda peer: pl.semaphore_signal(
            barrier, inc=1, device_id={"block": peer}, device_id_type=MESH
        )
    )
    each_region(
        lambda peer: pl.semaphore_signal(
            barrier, inc=1, device_id={"region": peer}, device_id_type=MESH
        )
    )
    load_obs = pltpu.make_async_copy(obs_hbm, obs, local_sem.at[0])
    load_predict = pltpu.make_async_copy(predict_hbm, predict, local_sem.at[1])
    load_factor = pltpu.make_async_copy(factor_hbm, factor, local_sem.at[2])
    load_obs.start()
    load_predict.start()
    load_factor.start()

    for copy in small:
        copy.wait()

    dest = [dev_ref[0, h] for h in range(nbd)]
    flat = []
    for h in range(nbd):
        rank = jnp.int32(0)
        for g in range(h):
            rank = rank + (dest[g] == dest[h]).astype(i32)
        flat.append(dest[h] * cap + rank)

    lane = lax.broadcasted_iota(i32, (nblock, lanes), 1)
    spot = lax.broadcasted_iota(i32, (nblock, lanes), 0) * cap + lane // chans
    spot = jnp.where(lane < part, spot, -1)
    wanted = jnp.full((nblock, lanes), -1, i32)
    for h in range(nbd):
        wanted = jnp.where(spot == flat[h], slot_ref[0, h] * chans + lane % chans, wanted)
    for d in range(nblock):
        req_send[d] = wanted[d : d + 1]

    block_lane = lax.broadcasted_iota(i32, (1, rows), 1)
    owner_of = block_lane // chans
    seam_row = jnp.zeros((1, rows), i32)
    for h in range(nbd):
        seam_row = jnp.where(owner_of == h, slot_ref[1, h], seam_row)
    seam_tgt[...] = seam_row * chans + block_lane % chans

    place_lane = lax.broadcasted_iota(i32, (1, LANES), 1)
    holder = jnp.full((1, LANES), nbd, i32)
    for h in range(nbd):
        holder = jnp.where(place_lane == flat[h], h, holder)
    held[...] = holder
    load_held = pltpu.make_async_copy(held, held_ref, local_sem.at[7])
    load_held.start()
    back[nbd] = jnp.zeros((chans, width), bf16)

    pl.semaphore_wait(barrier, nblock - 1 + nregion - 1)

    def request(peer, mine):
        return to_block(req_send.at[peer], req_recv.at[mine], req_ss.at[peer], req_rs.at[mine], peer)

    each_peer(lambda peer: request(peer, me).start())
    req_recv[me] = req_send[me]

    down = lax.rem(region + 1, nregion)
    up = lax.rem(region + nregion - 1, nregion)
    seam_fwd = to_region(obs_hbm, seam_obs, seam_ss.at[0], seam_rs.at[0], down)
    seam_where = to_region(seam_tgt, seam_tgt_in, seam_ss.at[1], seam_rs.at[1], up)
    seam_bwd = to_region(seam_ret, seam_ret_in, seam_ss.at[2], seam_rs.at[2], up)
    has_prev = region > 0
    has_next = region < nregion - 1

    @pl.when(has_next)
    def _():
        seam_fwd.start()

    @pl.when(has_prev)
    def _():
        seam_where.start()

    load_obs.wait()
    pick_lane = lax.broadcasted_iota(i32, (part, rows), 1)

    def picked(peer):
        row = jnp.broadcast_to(req_recv[peer], (LANES, lanes))
        column = jnp.transpose(row)[:part]
        column = jnp.concatenate([column] * (rows // LANES), axis=1)
        mask = jnp.where(column == pick_lane, 1.0, 0.0).astype(bf16)
        got = jnp.dot(mask, obs[...].reshape(rows, width), preferred_element_type=f32)
        return got.astype(bf16).reshape(cap, chans, width)

    def span(d):
        return pl.ds(d * cap, cap)

    def serve(peer, mine):
        return to_block(
            near_send.at[span(peer)],
            near_recv.at[span(mine)],
            near_ss.at[peer],
            near_rs.at[mine],
            peer,
        )

    def put(peer):
        near_send[span(peer)] = picked(peer)
        serve(peer, me).start()

    def answer(peer):
        request(me, peer).wait_recv()
        put(peer)

    each_peer(answer, nearest=True)
    near_recv[span(me)] = picked(me)

    def build(pair):
        wanted_row = jnp.concatenate(
            [req_recv[pair * group + i][:, :part] for i in range(group)], axis=1
        )
        spread[pair] = jnp.where(
            wanted_row == lax.broadcasted_iota(i32, (rows, group * part), 0), 1.0, 0.0
        ).astype(bf16)

    for pair in range(nblock // group):
        build(pair)
    load_held.wait()

    @pl.when(has_prev)
    def _():
        seam_fwd.wait_recv()

    @pl.when(jnp.logical_not(has_prev))
    def _():
        seam_obs[...] = jnp.zeros_like(seam_obs)

    load_predict.wait()
    for g in range(nbd):
        partial[g] = obs[g].astype(f32) - jnp.dot(
            seam_obs[slot_ref[1, g]], predict[g, 1], preferred_element_type=f32
        )
    load_factor.wait()

    eye = lax.broadcasted_iota(i32, (chans, LANES), 0) == lax.broadcasted_iota(
        i32, (chans, LANES), 1
    )
    tau_row = jnp.concatenate([tau_ref[...], jnp.zeros((1, LANES - chans), f32)], axis=1)
    tau_col = jnp.sum(jnp.where(eye, tau_row, 0.0), axis=1, keepdims=True)
    count = counts_ref[0]

    each_peer(lambda peer: serve(me, peer).wait_recv(), nearest=True)

    nt = (((1,), (1,)), ((), ()))
    every = range(nbd)
    err = [
        (
            partial[g]
            - jnp.dot(near_recv[flat[g]], predict[g, 0], preferred_element_type=f32)
        ).astype(bf16)
        for g in every
    ]
    white = [jnp.dot(err[g], factor[g], preferred_element_type=f32) for g in every]
    live = [(g < count).astype(f32) for g in every]
    weighted = [(live[g] * tau_col * white[g]).astype(bf16) for g in every]
    squares = live[0] * white[0] * white[0]
    for g in range(1, nbd):
        squares = squares + live[g] * white[g] * white[g]
    live_lane = lax.broadcasted_iota(i32, (1, LANES), 1) == chans
    sums = jnp.sum(
        jnp.where(eye, jnp.sum(squares, axis=1, keepdims=True), 0.0), axis=0, keepdims=True
    )
    sums = sums + jnp.where(live_lane, jnp.minimum(count, nbd).astype(f32), 0.0)
    sq_send[...] = sums

    def share(peer, mine):
        return to_block(sq_send, sq_recv.at[mine], sq_ss.at[peer], sq_rs.at[mine], peer)

    each_peer(lambda peer: share(peer, me).start())
    sq_recv[me] = sums

    adj = [lax.dot_general(weighted[g], factor[g], nt, preferred_element_type=f32) for g in every]
    for g in every:
        out_ref[g] = adj[g]
        adjoint[g] = adj[g].astype(bf16)

    for g in every:
        back[g] = lax.dot_general(
            adjoint[g], predict[g, 0], nt, preferred_element_type=f32
        ).astype(bf16)

    def pack(dst, peer):
        for k in range(cap):
            dst[k * chans : (k + 1) * chans] = back[held_ref[0, peer * cap + k]]

    def give(peer, mine):
        return to_block(ret_send.at[peer], ret_recv.at[mine], ret_ss.at[peer], ret_rs.at[mine], peer)

    def give_back(peer):
        pack(ret_send.at[peer], peer)
        give(peer, me).start()

    each_peer(give_back)
    pack(ret_recv.at[me], me)

    @pl.when(has_prev)
    def _():
        for g in range(nbd):
            seam_ret[g] = lax.dot_general(
                adjoint[g], predict[g, 1], nt, preferred_element_type=f32
            ).astype(bf16)
        seam_bwd.start()

    each_peer(lambda peer: share(me, peer).wait_recv(), nearest=True)
    line = sq_recv[0]
    for d in range(1, nblock):
        line = line + sq_recv[d]
    rg_send[...] = line

    def share_region(peer, mine):
        return to_region(rg_send, rg_recv.at[mine], rg_ss.at[peer], rg_rs.at[mine], peer)

    each_region(lambda peer: share_region(peer, region).start())
    rg_recv[region] = line

    @pl.when(has_next)
    def _():
        seam_where_in = to_region(seam_tgt, seam_tgt_in, seam_ss.at[1], seam_rs.at[1], up)
        seam_where_in.wait_recv()
        mask = jnp.where(
            seam_tgt_in[...] == lax.broadcasted_iota(i32, (rows, rows), 0), 1.0, 0.0
        ).astype(bf16)
        seam_bwd.wait_recv()
        got = jnp.dot(mask, seam_ret_in[...].reshape(rows, width), preferred_element_type=f32)
        out_ref[...] = out_ref[...] - got.reshape(nbd, chans, width)

    def add(pair):
        blocks_back = ret_recv[pl.ds(pair * group, group)].reshape(group * part, width)
        got = jnp.dot(spread[pair], blocks_back, preferred_element_type=f32)
        out_ref[...] = out_ref[...] - got.reshape(nbd, chans, width)

    each_peer(lambda peer: give(me, peer).wait_recv(), nearest=True)
    for pair in range(nblock // group):
        add(pair)

    each_region(lambda peer: share_region(region, peer).wait_recv())
    total = rg_recv[0]
    for r in range(1, nregion):
        total = total + rg_recv[r]
    total_live = jnp.sum(jnp.where(live_lane, total, 0.0), axis=1, keepdims=True)
    blocks = nbd * nblock * nregion
    gtau_ref[...] = (
        0.5 * total[:, :chans] - 0.5 * width * total_live / tau_ref[...]
    ) / (blocks * width)

    def sent(peer):
        request(peer, me).wait_send()
        serve(peer, me).wait_send()
        give(peer, me).wait_send()
        share(peer, me).wait_send()

    each_peer(sent)
    each_region(lambda peer: share_region(peer, region).wait_send())

    @pl.when(has_next)
    def _():
        seam_fwd.wait_send()

    @pl.when(has_prev)
    def _():
        seam_where.wait_send()
        seam_bwd.wait_send()


def line_kernel(
    nblock,
    nregion,
    cap,
    dev_hbm,
    slot_hbm,
    counts_hbm,
    tau_hbm,
    obs_hbm,
    predict_hbm,
    factor_hbm,
    out_ref,
    gtau_ref,
    dev_ref,
    slot_ref,
    counts_ref,
    tau_ref,
    obs,
    predict,
    factor,
    req_send,
    req_recv,
    pass_recv,
    near_send,
    near_recv,
    raw_sib,
    raw_far,
    ret_send,
    ret_recv,
    seam_obs,
    seam_tgt,
    seam_tgt_in,
    seam_ret,
    seam_ret_in,
    held,
    held_ref,
    spread,
    partial,
    adj_slot,
    seam_slot,
    sq_send,
    sq_recv,
    local_sem,
    req_ss,
    req_rs,
    near_ss,
    near_rs,
    ret_ss,
    ret_rs,
    sq_ss,
    sq_rs,
    seam_ss,
    seam_rs,
    raw_ss,
    raw_rs,
    pass_ss,
    pass_rs,
):
    nbd, chans, width = obs.shape
    rows = nbd * chans
    part = cap * chans
    me = lax.axis_index("block")
    region = lax.axis_index("region")
    bf16, f32, i32 = jnp.bfloat16, jnp.float32, jnp.int32
    nt = (((1,), (1,)), ((), ()))

    def flip(d, bit):
        return d + bit - 2 * bit * lax.rem(d // bit, 2)

    sib = flip(me, 1)
    chip = me // 2
    own = [me, sib]
    beside = [flip(d, 2) for d in own]
    skip = [flip(d, 4) for d in own]
    mirror = [flip(d, 4) for d in beside]
    at_end = chip * (nblock // 2 - 1 - chip) == 0
    inner = jnp.logical_not(at_end)
    others = mirror + skip + beside + [sib]
    end = 1 - lax.rem((chip + 1) // 2, 2)
    kinds = [mirror, skip, beside, [sib]]
    core = lax.rem(me, 2)
    lead = jnp.logical_and(at_end, core == 1)
    tail = jnp.logical_and(at_end, core == 0)
    m0, s0, b0 = [2 * (d[0] // 2) for d in (mirror, skip, beside)]
    m1, s1, b1 = m0 + 1, s0 + 1, b0 + 1

    def by_place(inside, outside):
        return [tuple(i + end * (o - i) for i, o in zip(*two)) for two in zip(inside, outside)]


    def to_block(src, dst, ss, rs, peer):
        return pltpu.make_async_remote_copy(
            src_ref=src,
            dst_ref=dst,
            send_sem=ss,
            recv_sem=rs,
            device_id={"block": peer},
            device_id_type=MESH,
        )

    def to_region(src, dst, ss, rs, peer):
        return pltpu.make_async_remote_copy(
            src_ref=src,
            dst_ref=dst,
            send_sem=ss,
            recv_sem=rs,
            device_id={"region": peer},
            device_id_type=MESH,
        )

    def wait(ref, sem):
        pltpu.make_async_copy(ref, ref, sem).wait()

    regions = [lax.rem(region + step, nregion) for step in range(1, nregion)]

    small = [
        pltpu.make_async_copy(src, dst, local_sem.at[3 + i])
        for i, (src, dst) in enumerate(
            [(dev_hbm, dev_ref), (slot_hbm, slot_ref), (counts_hbm, counts_ref), (tau_hbm, tau_ref)]
        )
    ]
    for copy in small:
        copy.start()

    barrier = pltpu.get_barrier_semaphore()
    for peer in others:
        pl.semaphore_signal(barrier, inc=1, device_id={"block": peer}, device_id_type=MESH)
    for peer in regions:
        pl.semaphore_signal(barrier, inc=1, device_id={"region": peer}, device_id_type=MESH)
    load_obs = pltpu.make_async_copy(obs_hbm, obs, local_sem.at[0])
    load_predict = pltpu.make_async_copy(predict_hbm, predict, local_sem.at[1])
    load_factor = pltpu.make_async_copy(factor_hbm, factor, local_sem.at[2])
    load_obs.start()
    load_predict.start()
    load_factor.start()

    for copy in small:
        copy.wait()

    dest = [dev_ref[0, h] for h in range(nbd)]
    flat = []
    for h in range(nbd):
        rank = jnp.int32(0)
        for g in range(h):
            rank = rank + (dest[g] == dest[h]).astype(i32)
        flat.append(dest[h] * cap + rank)

    lane = lax.broadcasted_iota(i32, (nblock, part), 1)
    spot = lax.broadcasted_iota(i32, (nblock, part), 0) * cap + lane // chans
    wanted = jnp.full((nblock, part), -1, i32)
    for h in range(nbd):
        wanted = jnp.where(spot == flat[h], slot_ref[0, h] * chans + lane % chans, wanted)
    for d in range(nblock):
        req_send[d] = wanted[d : d + 1]

    block_lane = lax.broadcasted_iota(i32, (1, rows), 1)
    owner_of = block_lane // chans
    seam_row = jnp.zeros((1, rows), i32)
    for h in range(nbd):
        seam_row = jnp.where(owner_of == h, slot_ref[1, h], seam_row)
    seam_tgt[...] = seam_row * chans + block_lane % chans

    place_lane = lax.broadcasted_iota(i32, (1, LANES), 1)
    holder = jnp.full((1, LANES), nbd, i32)
    for h in range(nbd):
        holder = jnp.where(place_lane == flat[h], h, holder)
    held[...] = holder
    load_held = pltpu.make_async_copy(held, held_ref, local_sem.at[7])
    load_held.start()

    pl.semaphore_wait(barrier, nblock - 1 + nregion - 1)

    def request(peer, kind):
        return to_block(req_send.at[peer], req_recv.at[me], req_ss.at[0], req_rs.at[kind], peer)

    def asked(kind):
        wait(req_recv.at[pl.ds(0, len(kinds[kind]))], req_rs.at[kind])

    def request_pass(owner, peer):
        return to_block(req_send.at[owner], pass_recv.at[me], pass_ss.at[0], pass_rs.at[0], peer)

    for kind, peers in enumerate(kinds):
        for peer in peers:
            request(peer, kind).start()
    req_recv[me] = req_send[me]

    @pl.when(inner)
    def _():
        request_pass(s1, b1).start()


    to_sib = to_block(obs_hbm, raw_sib, raw_ss.at[0], raw_rs.at[0], sib)
    to_far = to_block(obs_hbm, raw_far, raw_ss.at[0], raw_rs.at[1], mirror[0])
    relay = to_block(raw_far, raw_far, raw_ss.at[0], raw_rs.at[1], sib)

    down = lax.rem(region + 1, nregion)
    up = lax.rem(region + nregion - 1, nregion)
    seam_fwd = to_region(obs_hbm, seam_obs, seam_ss.at[0], seam_rs.at[0], down)
    seam_where = to_region(seam_tgt, seam_tgt_in, seam_ss.at[1], seam_rs.at[1], up)
    seam_bwd = to_region(seam_ret, seam_ret_in, seam_ss.at[2], seam_rs.at[2], up)
    has_prev = region > 0
    has_next = region < nregion - 1

    @pl.when(core == 1)
    def _():
        to_far.start()

    @pl.when(has_next)
    def _():
        seam_fwd.start()

    @pl.when(has_prev)
    def _():
        seam_where.start()

    to_sib.start()

    load_obs.wait()
    pick_lane = lax.broadcasted_iota(i32, (part, rows), 1)

    def picked(row, source):
        row = jnp.broadcast_to(row, (LANES, part))
        column = jnp.concatenate([jnp.transpose(row)] * (rows // LANES), axis=1)
        mask = jnp.where(column == pick_lane, 1.0, 0.0).astype(bf16)
        got = jnp.dot(mask, source[...].reshape(rows, width), preferred_element_type=f32)
        return got.astype(bf16).reshape(cap, chans, width)

    def span(d):
        return pl.ds(d * cap, cap)

    def serve(peer):
        return to_block(
            near_send.at[span(peer)],
            near_recv.at[span(me)],
            near_ss.at[0],
            near_rs.at[me],
            peer,
        )

    def arrived(owner):
        wait(near_recv.at[span(owner)], near_rs.at[owner])

    def pass_on(j):
        return to_block(
            near_send.at[span(skip[j])],
            near_recv.at[span(mirror[0])],
            near_ss.at[0],
            near_rs.at[mirror[0]],
            beside[j],
        )

    def answer(kind):
        asked(kind)
        for peer in kinds[kind]:
            near_send[span(peer)] = picked(req_recv[peer], obs)
            serve(peer).start()

    @pl.when(jnp.logical_and(inner, core == 0))
    def _():
        for kind in (0, 1, 2):
            answer(kind)

    @pl.when(jnp.logical_and(inner, core == 1))
    def _():
        for kind in (1, 2):
            answer(kind)
        asked(0)

    @pl.when(tail)
    def _():
        for kind in (1, 2, 0):
            answer(kind)

    @pl.when(lead)
    def _():
        answer(2)
        asked(1)
        asked(0)

    asked(3)

    def build(pair):
        wanted_row = jnp.concatenate([req_recv[pair * 2 + i] for i in range(2)], axis=1)
        spread[pair] = jnp.where(
            wanted_row == lax.broadcasted_iota(i32, (rows, 2 * part), 0), 1.0, 0.0
        ).astype(bf16)

    for pair in range(nblock // 2):
        build(pair)
    load_held.wait()

    eye = lax.broadcasted_iota(i32, (chans, LANES), 0) == lax.broadcasted_iota(
        i32, (chans, LANES), 1
    )
    tau_row = jnp.concatenate([tau_ref[...], jnp.zeros((1, LANES - chans), f32)], axis=1)
    tau_col = jnp.sum(jnp.where(eye, tau_row, 0.0), axis=1, keepdims=True)
    count = counts_ref[0]

    @pl.when(has_prev)
    def _():
        seam_fwd.wait_recv()

    @pl.when(jnp.logical_not(has_prev))
    def _():
        seam_obs[...] = jnp.zeros_like(seam_obs)

    load_predict.wait()
    for g in range(nbd):
        partial[g] = obs[g].astype(f32) - jnp.dot(
            seam_obs[slot_ref[1, g]], predict[g, 1], preferred_element_type=f32
        )
    load_factor.wait()

    def give(peer, kind):
        return to_block(ret_send.at[peer], ret_recv.at[me], ret_ss.at[0], ret_rs.at[kind], peer)

    squares = [jnp.zeros((chans, width), f32)]

    def process(peers, near_of, between=None):
        at = [peer * cap + k for peer in peers for k in range(cap)]
        every = range(len(at))
        who = [held_ref[0, i] for i in at]
        block = [jnp.minimum(w, nbd - 1) for w in who]
        live = [(w < count).astype(f32) for w in who]
        near = [near_of(i // cap, at[i], block[i]) for i in every]
        err = [
            (
                partial[block[i]]
                - jnp.dot(near[i], predict[block[i], 0], preferred_element_type=f32)
            ).astype(bf16)
            for i in every
        ]
        white = [jnp.dot(err[i], factor[block[i]], preferred_element_type=f32) for i in every]
        for i in every:
            squares[0] = squares[0] + live[i] * white[i] * white[i]
        if between is not None:
            between()
        weighted = [(live[i] * tau_col * white[i]).astype(bf16) for i in every]
        adj = [
            lax.dot_general(weighted[i], factor[block[i]], nt, preferred_element_type=f32)
            for i in every
        ]
        for i in every:
            adj_slot[at[i]] = adj[i]
        both = [
            lax.dot_general(
                adj[i].astype(bf16),
                predict[block[i]].reshape(2 * width, width),
                nt,
                preferred_element_type=f32,
            ).astype(bf16)
            for i in every
        ]
        for i in every:
            seam_slot[at[i]] = both[i][:, width:]
        return [both[i][:, :width] for i in every]

    def hand_out(group, back):
        for j, (peer, kind) in enumerate(group):
            for k in range(cap):
                ret_send[peer, k * chans : (k + 1) * chans] = back[j * cap + k]
            give(peer, kind).start()

    @pl.when(core == 1)
    def _():
        to_far.wait_recv()
        relay.start()

    @pl.when(lead)
    def _():
        wait(pass_recv.at[pl.ds(0, 2)], pass_rs.at[0])
        for j, peer in enumerate(beside):
            near_send[span(skip[j])] = picked(pass_recv[peer], raw_far)
            pass_on(j).start()

    to_sib.wait_recv()
    homes = [obs, raw_sib]
    back = process(own, lambda j, i, h: homes[j][slot_ref[0, h]])
    for k in range(cap):
        ret_recv[me, k * chans : (k + 1) * chans] = back[k]
    hand_out([(sib, 3)], back[cap:])

    @pl.when(core == 0)
    def _():
        relay.wait_recv()

    def send_seam():
        @pl.when(has_prev)
        def _():
            for g in range(nbd):
                seam_ret[g] = seam_slot[flat[g]]
            seam_bwd.start()

    def turn(group, between=None):
        for owner, kind in group:
            arrived(owner)
        owners = [owner for owner, kind in group]
        back = process(owners, lambda j, i, h: near_recv[i], between)
        if between is not None:
            send_seam()
        hand_out(group, back)

    hand_out([(m1, 0)], process([m1], lambda j, i, h: raw_far[slot_ref[0, h]]))
    turn(by_place([(b0, 2), (b1, 2)], [(b0, 2), (b1, 2)]))
    turn(by_place([(m0, 0), (s0, 1)], [(s0, 1), (s1, 1)]))
    live_lane = lax.broadcasted_iota(i32, (1, LANES), 1) == chans

    everyone = [(r, b) for r in regions for b in others + [me]] + [(region, b) for b in others]
    mine = region * nblock + me

    def share(r, b):
        return pltpu.make_async_remote_copy(
            src_ref=sq_send,
            dst_ref=sq_recv.at[mine],
            send_sem=sq_ss.at[0],
            recv_sem=sq_rs.at[0],
            device_id={"region": r, "block": b},
            device_id_type=MESH,
        )

    sums_in = sq_recv.at[pl.ds(0, len(everyone))]

    def share_all():
        sums = jnp.sum(
            jnp.where(eye, jnp.sum(squares[0], axis=1, keepdims=True), 0.0), axis=0, keepdims=True
        )
        sums = sums + jnp.where(live_lane, jnp.minimum(count, nbd).astype(f32), 0.0)
        sq_send[...] = sums
        for r, b in everyone:
            share(r, b).start()
        sq_recv[mine] = sums

    turn(by_place([(s1, 1)], [(m0, 0)]), share_all)

    for g in range(nbd):
        out_ref[g] = adj_slot[flat[g]]

    def add(pair):
        blocks_back = ret_recv[pl.ds(pair * 2, 2)].reshape(2 * part, width)
        got = jnp.dot(spread[pair], blocks_back, preferred_element_type=f32)
        out_ref[...] = out_ref[...] - got.reshape(nbd, chans, width)

    def take(kind):
        wait(ret_recv.at[pl.ds(0, len(kinds[kind]))], ret_rs.at[kind])

    wait(req_send.at[pl.ds(0, len(others))], req_ss.at[0])

    @pl.when(inner)
    def _():
        wait(pass_recv.at[pl.ds(0, 1)], pass_ss.at[0])

    @pl.when(core == 0)
    def _():
        wait(near_send.at[pl.ds(0, 6 * cap)], near_ss.at[0])

    @pl.when(core == 0)
    def _():
        to_sib.wait_send()

    @pl.when(core == 1)
    def _():
        wait(near_send.at[pl.ds(0, 4 * cap)], near_ss.at[0])
        wait(predict.at[pl.ds(0, 3 * nbd * chans // (2 * width))], raw_ss.at[0])

    @pl.when(has_next)
    def _():
        seam_fwd.wait_send()

    @pl.when(has_prev)
    def _():
        seam_where.wait_send()

    take(3)
    add(chip)
    take(2)
    add(beside[0] // 2)

    take(0)
    add(mirror[0] // 2)

    @pl.when(has_next)
    def _():
        seam_where.wait_recv()
        mask = jnp.where(
            seam_tgt_in[...] == lax.broadcasted_iota(i32, (rows, rows), 0), 1.0, 0.0
        ).astype(bf16)
        seam_bwd.wait_recv()
        got = jnp.dot(mask, seam_ret_in[...].reshape(rows, width), preferred_element_type=f32)
        out_ref[...] = out_ref[...] - got.reshape(nbd, chans, width)

    take(1)
    add(skip[0] // 2)

    wait(sums_in, sq_rs.at[0])
    total = sq_recv[0]
    for d in range(1, nregion * nblock):
        total = total + sq_recv[d]
    total_live = jnp.sum(jnp.where(live_lane, total, 0.0), axis=1, keepdims=True)
    blocks = nbd * nblock * nregion
    gtau_ref[...] = (
        0.5 * total[:, :chans] - 0.5 * width * total_live / tau_ref[...]
    ) / (blocks * width)

    wait(ret_send.at[pl.ds(0, len(others))], ret_ss.at[0])
    wait(sums_in, sq_ss.at[0])

    @pl.when(has_prev)
    def _():
        seam_bwd.wait_send()


def write_out(obs_ref, tau_ref, obs_hbm, tau_hbm, sem):
    copies = [
        pltpu.make_async_copy(src, dst, sem.at[i])
        for i, (src, dst) in enumerate([(obs_ref, obs_hbm), (tau_ref, tau_hbm)])
    ]
    for copy in copies:
        copy.start()
    for copy in copies:
        copy.wait()


def shards(obs, predict, factor, tau, nbr_dev, nbr_slot, counts):
    nbd, chans, width = obs.shape
    nblock = lax.axis_size("block")
    nregion = lax.axis_size("region")
    cap = max(2, 2 * nbd // nblock)
    rows = nbd * chans
    part = cap * chans
    lanes = -(-part // LANES) * LANES
    group = 2 if nblock % 2 == 0 and part % LANES == 0 else 1
    line = nblock == 8 and part == LANES
    bf16, f32, i32 = jnp.bfloat16, jnp.float32, jnp.int32
    vmem = pl.BlockSpec(memory_space=pltpu.VMEM)
    hbm = pl.BlockSpec(memory_space=pltpu.HBM)
    dma = pltpu.SemaphoreType.DMA
    blocks = pltpu.VMEM((nbd, chans, width), bf16)
    slots = pltpu.VMEM((nblock * cap, chans, width), bf16)
    inputs = [
        pltpu.SMEM((1, nbd), i32),
        pltpu.SMEM((2, nbd), i32),
        pltpu.SMEM((1,), i32),
        pltpu.VMEM((1, chans), f32),
        blocks,
        pltpu.VMEM((nbd, 2, width, width), bf16),
        pltpu.VMEM((nbd, width, width), bf16),
        pltpu.VMEM((nblock, 1, lanes), i32),
        pltpu.VMEM((nblock, 1, lanes), i32),
        slots,
        slots,
    ]
    middle = [
        pltpu.VMEM((nblock, part, width), bf16),
        pltpu.VMEM((nblock, part, width), bf16),
        blocks,
        pltpu.VMEM((1, rows), i32),
        pltpu.VMEM((1, rows), i32),
        blocks,
        blocks,
        pltpu.VMEM((1, LANES), i32),
        pltpu.SMEM((1, LANES), i32),
        pltpu.VMEM((nblock // group, rows, group * part), bf16),
        pltpu.VMEM((nbd, chans, width), f32),
    ]
    sums = [
        pltpu.VMEM((1, LANES), f32),
        pltpu.VMEM((nblock, 1, LANES), f32),
        pltpu.VMEM((1, LANES), f32),
        pltpu.VMEM((nregion, 1, LANES), f32),
        dma((8,)),
    ]
    sems = [dma((nblock,))] * 8 + [dma((nregion,))] * 2 + [dma((3,))] * 2
    if line:
        body = line_kernel
        scratch = inputs[:9] + inputs[8:] + [blocks] * 2 + middle
        scratch += [pltpu.VMEM((nblock * cap, chans, width), f32), slots, sums[0]]
        scratch += [pltpu.VMEM((nregion * nblock, 1, LANES), f32), sums[-1]]
        scratch += [dma((n,)) for n in (1, 4, 1, nblock, 1, 4, 1, 1, 3, 3, 1, 2, 1, 1)]
    else:
        body = kernel
        scratch = inputs + middle
        scratch += [pltpu.VMEM((nbd + 1, chans, width), bf16), blocks] + sums + sems
    grad_obs, grad_tau = pl.pallas_call(
        functools.partial(body, nblock, nregion, cap),
        out_shape=(
            jax.ShapeDtypeStruct((nbd, chans, width), f32),
            jax.ShapeDtypeStruct((1, chans), f32),
        ),
        in_specs=[hbm] * 7,
        out_specs=(vmem, vmem),
        scratch_shapes=scratch,
        compiler_params=pltpu.CompilerParams(
            collective_id=0, has_side_effects=True, vmem_limit_bytes=48 << 20
        ),
        name="vecchia",
    )(
        *(
            value if value is counts else pltpu.with_memory_space_constraint(value, pltpu.HBM)
            for value in (nbr_dev.T, nbr_slot.T, counts, tau.reshape(1, chans), obs, predict, factor)
        )
    )
    grad_obs, grad_tau = pl.pallas_call(
        write_out,
        out_shape=(
            jax.ShapeDtypeStruct((nbd, chans, width), f32),
            jax.ShapeDtypeStruct((1, chans), f32),
        ),
        in_specs=[vmem, vmem],
        out_specs=(hbm, hbm),
        scratch_shapes=[dma((2,))],
        name="write_out",
    )(*(pltpu.with_memory_space_constraint(x, pltpu.VMEM) for x in (grad_obs, grad_tau)))
    return grad_obs, grad_tau.reshape(chans)


def solution(mesh):
    in_specs = (
        P(("region", "block"), None, None),
        P(("region", "block"), None, None, None),
        P(("region", "block"), None, None),
        P(),
        P(("region", "block"), None),
        P(("region", "block"), None),
        P(("region", "block")),
    )
    out_specs = (P(("region", "block"), None, None), P())
    return jax.shard_map(shards, mesh=mesh, in_specs=in_specs, out_specs=out_specs, check_vma=False)
```
